768 devices in a mesh: gx: 16 (over y, core), gy: 12 (over z), gz: 4 (over x).
Axes of the slice: x: 4, y: 8, z: 12, core: 2. Of those that a mesh axis runs over, the one named last changes fastest.
Arguments:
- chi: float32 [256, 192, 512], P('gx', 'gy', 'gz'), may hold values from 0.05 to 4
- inducing: float32 [3, 256, 192, 512], P(None, 'gx', 'gy', 'gz'), may hold values from -6 to 6
- record_dest: int32 [16, 12, 4, 1024, 1], P('gx', 'gy', 'gz'), may hold values from 0 to 3; in each aligned block of 1024 rows (0 to 1023, 1024 to 2047, ..., all dimensions but the last counted through in order) at most 640 rows name the same one
- record_cell: int32 [16, 12, 4, 1024], P('gx', 'gy', 'gz'), may hold values from 0 to 32767
- record_value: float32 [16, 12, 4, 1024], P('gx', 'gy', 'gz'), may hold values from -16 to 16
Outputs:
- potential: float32 [256, 192, 512], P('gx', 'gy', 'gz')
The draws below stay inside these ranges and needn't reach their ends.
Inputs may be any that keep to these rules, and one draw needn't show every extreme that they name: `record_dest`: among the records of one device, at most 640 go to any one depth brick; in some devices exactly 640 do.
All inputs are finite; a program needn't handle non-finite values.
Results may differ from the reference program's by a relative error of at most 0.0001.
Values sent between devices are 32-bit elements; how exact they have to be, the bound alone decides.
A program may use at most 64 MiB of HBM per device.

```python
import math
import jax
import jax.numpy as jnp
import numpy as np
from jax import lax

CX = 16
CY = 16
CZ = 128
RECS = 1024
SMOOTH = 2
LEVELS = 3
COARSE_SWEEPS = 8
CAP = 640
NX = 256
NY = 192
NZ = 512
N_GX = 16
N_GY = 12
N_GZ = 4


def touch_ends(entries, stream_key, least, high):
    dims = entries.shape
    place = [jax.random.randint(jax.random.fold_in(stream_key, axis), (), 0, dims[axis]) for axis in range(len(dims))]
    entries = entries.at[tuple(place)].set(least)
    longest = dims.index(max(dims))
    place[longest] = (place[longest] + 1) % dims[longest]
    return entries.at[tuple(place)].set(high)


def block_levels(own_key, shape, pieces, smallest, largest):
    def one(axis_at, shards_of):
        heights = jax.random.uniform(jax.random.fold_in(jax.random.fold_in(own_key, 6), axis_at), (shards_of,), jnp.float32, smallest / len(pieces), largest / len(pieces))
        return jnp.repeat(jnp.exp(heights), shape[axis_at] // shards_of).reshape((-1,) + (1,) * (len(shape) - axis_at - 1))

    level = one(*pieces[0])
    for cut in pieces[1:]:
        level = level * one(*cut)
    return level


def assign_block(stream_key, own, number, rows, amount, top, reach, slope):
    sequence = jax.random.permutation(stream_key, amount)
    heavy_load, usual = portions_of(amount, rows * top, reach, slope, True), portions_of(amount, rows * top, reach, slope, False)
    places = jnp.arange(amount)

    def named(lengths, turn):
        used = int((lengths > 0).sum())
        fixed = max(1, used // 4)
        shifted = fixed + (places - fixed + turn * (used - fixed)) % max(1, amount - fixed)
        return jnp.zeros((amount,), jnp.int32).at[sequence[jnp.where(places < fixed, places, shifted)]].set(jnp.asarray(lengths, jnp.int32))

    lengths = jnp.where(number % 4 == 0, named(heavy_load, number // 4), named(usual, number - number // 4 - 1))
    mixed = jax.random.permutation(jax.random.fold_in(own, 3), amount)
    source_of, taker = mixed[0:amount // 2 * 2:2], mixed[1:amount // 2 * 2:2]
    room = jnp.minimum(lengths[source_of] - 1, reach - lengths[taker]) // 2
    room = jnp.where((source_of == sequence[0]) | (taker == sequence[0]) | (lengths[taker] == 0), 0, jnp.maximum(room, 0))
    shifted = jax.random.randint(jax.random.fold_in(own, 4), (amount // 2,), 0, 1 << 20) % (room + 1)
    lengths = lengths.at[source_of].add(-shifted).at[taker].add(shifted)
    labels = jnp.searchsorted(jnp.cumsum(lengths), jnp.arange(rows * top), side="right").astype(jnp.int32)
    grid = labels.reshape(top, rows).T
    grid = grid[jax.random.permutation(jax.random.fold_in(own, 1), rows)]
    turn = jax.random.randint(jax.random.fold_in(own, 2), (rows, 1), 0, top)
    return jnp.take_along_axis(grid, (jnp.arange(top)[None, :] + turn) % top, axis=1)


def portions_of(amount, total, bound, lean, full):
    loads = [(1 << 20) // math.isqrt(standing ** lean) + 1 for standing in range(1, amount + 1)]
    largest = bound if full else min(bound, max(-(-total // amount), total * loads[0] // sum(loads)))
    least = 1 if total - largest >= amount - 1 else 0
    counts, surplus = [largest] + [least] * (amount - 1), total - largest - least * (amount - 1)
    while surplus > 0:
        candidates = [i for i in range(1, amount) if counts[i] < largest] or [i for i in range(1, amount) if counts[i] < bound]
        pool, left = sum([loads[i] for i in candidates]), surplus
        for i in candidates:
            extra = min(bound - counts[i], max(1, left * loads[i] // pool), surplus)
            counts[i] = counts[i] + extra
            surplus = surplus - extra
    return np.array(counts)


def scatter_about(stream_key, dims, scale, reach, split=(), held_as=jnp.bfloat16):
    loudness = block_levels(stream_key, dims, split, -0.22, 0.18) if split else 1.0
    array = jax.random.normal(stream_key, dims, jnp.float32) * scale * loudness
    return jnp.minimum(jnp.maximum(array, -reach), reach).astype(held_as)


def setup_inputs(seed: int = 0) -> dict:
    keys = jax.random.split(jax.random.key(seed), 6)
    chi = jnp.clip(jnp.exp(math.log(4.0) - 4.3820266 * jax.random.uniform(keys[0], (NX, NY, NZ), jnp.float32) ** block_levels(keys[0], (NX, NY, NZ), ((0, 16), (1, 12), (2, 4)), -0.2, 0.2)), 0.05, 4.0)
    inducing = scatter_about(keys[1], (3, NX, NY, NZ), 1.0, 6.0, ((1, 16), (2, 12), (3, 4)), jnp.float32)
    record_dest_keys = jax.random.split(jax.random.fold_in(keys[2], 1), N_GX * N_GY * N_GZ * RECS // RECS)
    record_dest_turns = jax.random.permutation(jax.random.fold_in(keys[2], 3), N_GX * N_GY * N_GZ * RECS // RECS)
    record_dest = jax.vmap(lambda own, number: assign_block(jax.random.fold_in(keys[2], 2), own, number, RECS, N_GZ, 1, CAP, 1))(record_dest_keys, record_dest_turns).reshape((N_GX, N_GY, N_GZ, RECS, 1))
    record_cell = touch_ends(jax.random.randint(keys[3], (N_GX, N_GY, N_GZ, RECS), 0, CX * CY * CZ), jax.random.fold_in(keys[3], 1), 0, (CX * CY * CZ) - 1).astype(jnp.int32)
    record_value = scatter_about(keys[4], (N_GX, N_GY, N_GZ, RECS), 4.0, 16.0, ((0, 16), (1, 12), (2, 4)), jnp.float32)
    return dict(chi=chi, inducing=inducing, record_dest=record_dest, record_cell=record_cell, record_value=record_value)


OMEGA = 0.8


def restrict(x):
    s = x.shape
    return x.reshape(s[0] // 2, 2, s[1] // 2, 2, s[2] // 2, 2).mean(axis=(1, 3, 5))


def prolong(e):
    return jnp.repeat(jnp.repeat(jnp.repeat(e, 2, 0), 2, 1), 2, 2)


def neighbours(padded):
    return [padded[2:, 1:-1, 1:-1], padded[:-2, 1:-1, 1:-1], padded[1:-1, 2:, 1:-1],
            padded[1:-1, :-2, 1:-1], padded[1:-1, 1:-1, 2:], padded[1:-1, 1:-1, :-2]]


def coefficients(kappa):
    center = kappa
    return [0.5 * (center + other) for other in neighbours(jnp.pad(kappa, 1))]


def apply_op(v, coefs, scale):
    total = jnp.zeros_like(v)
    for coef, other in zip(coefs, neighbours(jnp.pad(v, 1))):
        total = total + coef * (v - other)
    return scale * total


def cycle(level, rhs, kappas):
    scale = 0.25 ** level
    coefs = coefficients(kappas[level])
    diag = scale * (coefs[0] + coefs[1] + coefs[2] + coefs[3] + coefs[4] + coefs[5])
    sweeps = COARSE_SWEEPS if level == LEVELS else SMOOTH
    v = OMEGA * rhs / diag
    for sweep in range(sweeps - 1):
        v = v + OMEGA * (rhs - apply_op(v, coefs, scale)) / diag
    if level == LEVELS:
        return v
    resid = rhs - apply_op(v, coefs, scale)
    corr = cycle(level + 1, restrict(resid), kappas)
    v = v + prolong(corr)
    for sweep in range(SMOOTH):
        v = v + OMEGA * (rhs - apply_op(v, coefs, scale)) / diag
    return v


def reference(chi, inducing, record_dest, record_cell, record_value):
    moment = chi[None] * inducing
    px = jnp.pad(moment[0], 1)
    py = jnp.pad(moment[1], 1)
    pz = jnp.pad(moment[2], 1)
    source = -0.5 * ((px[2:, 1:-1, 1:-1] - px[:-2, 1:-1, 1:-1])
                     + (py[1:-1, 2:, 1:-1] - py[1:-1, :-2, 1:-1])
                     + (pz[1:-1, 1:-1, 2:] - pz[1:-1, 1:-1, :-2]))
    dest = record_dest[..., 0].astype(jnp.int32)
    cell = record_cell.astype(jnp.int32)
    shape = cell.shape
    row_a = lax.broadcasted_iota(jnp.int32, shape, 0)
    row_b = lax.broadcasted_iota(jnp.int32, shape, 1)
    xpos = row_a * CX + cell // (CY * CZ)
    ypos = row_b * CY + (cell // CZ) % CY
    zpos = dest * CZ + cell % CZ
    flat = ((xpos * NY + ypos) * NZ + zpos).reshape(-1)
    rhs = source.reshape(-1).at[flat].add(record_value.reshape(-1)).reshape(source.shape)
    kappas = [1.0 + chi]
    for level in range(LEVELS):
        kappas.append(restrict(kappas[-1]))
    return cycle(0, rhs, kappas)
```

```python
import functools
import itertools

import jax
import jax.numpy as jnp
from jax import lax
from jax.experimental import pallas as pl
from jax.experimental.pallas import tpu as pltpu
from jax.sharding import PartitionSpec as P

OMEGA = 0.8
F32 = jnp.float32
BF16 = jnp.bfloat16
MESH = pl.DeviceIdType.MESH
BOX = [d for d in itertools.product((-1, 0, 1), repeat=3) if d != (0, 0, 0)]
BOX2 = [d for d in itertools.product((-1, 0, 1), repeat=2) if d != (0, 0)]
REACH = 5


class Level:
    def __init__(self, index, own, size, split, total):
        self.index, self.own, self.size, self.split, self.total = index, own, size, split, total
        self.scale = 0.25**index


L0 = Level(0, (16, 16, 128), (22, 24, 256), (19, 20, 192), (256, 192, 512))
L1 = Level(1, (8, 8, 64), (16, 16, 128), (12, 12, 96), (128, 96, 256))
L2 = Level(2, (4, 4, 0), (12, 16, 128), (8, 8, 128), (64, 48, 128))
L3 = Level(3, (2, 2, 0), (22, 24, 128), (12, 24, 128), (32, 24, 64))
LEVELS = (L0, L1, L2, L3)


def tiles_0(d):
    if d[2] == 0:
        if d[1] == 0:
            return 6
        return 8 if d[0] == 0 else 2
    return 2 if d[1] == 0 else 1


def tiles_1(d):
    if d[2] == 0:
        return 4 if d[0] == 0 else 2
    return 2 if d[0] == 0 else 1


def slots(count_of):
    table, at = {}, 0
    for d in BOX:
        table[d] = (at, count_of(d))
        at += count_of(d)
    return table, at


SLOT_0, TILES_0 = slots(tiles_0)
SLOT_1, TILES_1 = slots(tiles_1)


def peers(shape):
    nx, ny, nz = shape
    out = [tuple(d) for d in BOX]
    out += [(0, 0, k) for k in range(2, nz - 1)]
    out += [(0, k, 0) for k in range(2, ny - 1)]
    out += [(k, 0, 0) for k in range(-REACH, REACH + 1) if abs(k) > 1]
    return out


def split3(x):
    hi = x.astype(BF16)
    rest = x - hi.astype(F32)
    mid = rest.astype(BF16)
    low = (rest - mid.astype(F32)).astype(BF16)
    return hi, mid, low


def right(x, mat):
    parts = [jnp.dot(p, mat, preferred_element_type=F32) for p in split3(x)]
    return parts[0] + parts[1] + parts[2]


def left(mat, x):
    parts = [jnp.dot(mat, p, preferred_element_type=F32) for p in split3(x)]
    return parts[0] + parts[1] + parts[2]


def wrap(at, size):
    return jnp.where(at < 0, at + size, jnp.where(at >= size, at - size, at))


def kernel(shape, chi_ref, ind_ref, dest_ref, cell_ref, val_ref, out_ref, *refs):
    it = iter(refs)
    take = lambda n: [next(it) for _ in range(n)]
    K, B, VA, VB, IW, DW = [], [], [], [], [], []
    C = []
    for _ in LEVELS:
        k, b, va, vb, iw, dw, c = take(7)
        K.append(k), B.append(b), VA.append(va), VB.append(vb), IW.append(iw), DW.append(dw), C.append(c)
    rec, mom_out, mom_in, hot, val_hot, rhs = take(6)
    pack_0, land_0, pack_1, land_1 = take(4)
    pack_2, land_2z, full_2, land_2 = take(4)
    pack_3, land_3y, col_3, land_3x = take(4)
    tall_0, tall_1, tall_2, tall_3, tall_4 = take(5)
    send_sem, recv_sem = take(2)

    me = [lax.axis_index(a) for a in ("gx", "gy", "gz")]

    def device(o):
        return tuple(lax.rem(me[i] + (o[i] + shape[i]), shape[i]) for i in range(3))

    barrier = pltpu.get_barrier_semaphore()
    all_peers = peers(shape)
    for o in all_peers:
        pl.semaphore_signal(barrier, inc=1, device_id=device(o), device_id_type=MESH)

    sub = lax.broadcasted_iota(jnp.int32, (8, 128), 0)
    lane = lax.broadcasted_iota(jnp.int32, (8, 128), 1)
    lane16 = lax.broadcasted_iota(jnp.int32, (16, 128), 1)

    def send(src, dst, o, n):
        pltpu.make_async_remote_copy(
            src_ref=src, dst_ref=dst, send_sem=send_sem.at[n], recv_sem=recv_sem.at[n],
            device_id=device(o), device_id_type=MESH,
        ).start()

    def arrive(ref, n):
        pltpu.make_async_copy(ref, ref, recv_sem.at[n]).wait()

    def sent(ref, n):
        pltpu.make_async_copy(ref, ref, send_sem.at[n]).wait()

    def start_0(src, i, n):
        pack, land = pack_0.at[i], land_0.at[i]
        for p in range(3):
            for t in range(2):
                pack[2 * p + t] = src[13 + p, 8 * t : 8 * t + 8, 0:128]
                pack[6 + 2 * p + t] = src[p, 8 * t : 8 * t + 8, 0:128]
        for k in range(8):
            pack[12 + k] = jnp.where(sub >= 4, src[2 * k, 8:16, 0:128], pltpu.roll(src[2 * k + 1, 8:16, 0:128], 4, 0))
            pack[20 + k] = jnp.where(sub < 4, src[2 * k, 0:8, 0:128], pltpu.roll(src[2 * k + 1, 0:8, 0:128], 4, 0))
        up = jnp.zeros((16, 128), F32)
        down = jnp.zeros((16, 128), F32)
        for x in range(16):
            p = src[x, 0:16, 0:128]
            here = (lane16 >= 4 * x) & (lane16 < 4 * x + 4)
            up = jnp.where(here, pltpu.roll(p, (4 * x + 4) % 128, 1), up)
            down = jnp.where(here, pltpu.roll(p, 4 * x, 1) if x else p, down)
        for t in range(2):
            pack[28 + t] = up[8 * t : 8 * t + 8]
            pack[30 + t] = down[8 * t : 8 * t + 8]
        for d in BOX:
            at, count = SLOT_0[d]
            if d[2] == 0:
                if d[1] == 0:
                    first = 0 if d[0] == 1 else 6
                else:
                    first = (12 if d[1] == 1 else 20) + (6 if d[0] == 1 else 0)
            else:
                first = (28 if d[2] == 1 else 30) + (1 if d[1] == 1 else 0)
            send(pack.at[pl.ds(first, count)], land.at[pl.ds(at, count)], d, n)

    def finish_0(dst, i, n):
        land = land_0.at[i]
        arrive(land, n)
        for xp in range(22):
            sx, px = (0, xp) if xp < 16 else (1, xp - 16) if xp < 19 else (-1, xp - 6)
            at = lambda y, z: SLOT_0[(-sx, -y, -z)][0]
            base = 6 if sx == -1 else 0
            if sx:
                row = px - 13 if sx == -1 else px
                dst[xp, 0:8, 0:128] = land[at(0, 0) + 2 * row]
                dst[xp, 8:16, 0:128] = land[at(0, 0) + 2 * row + 1]
            k = px // 2 - base
            above, below = land[at(1, 0) + k], land[at(-1, 0) + k]
            if px % 2:
                above, below = pltpu.roll(above, 4, 0), pltpu.roll(below, 4, 0)
            dst[xp, 16:24, 0:128] = jnp.where(sub < 4, above, below)
            for t in range(3):
                if t < 2:
                    a, b = land[at(0, 1) + t], land[at(0, -1) + t]
                else:
                    a = jnp.where(sub < 4, land[at(1, 1)], land[at(-1, 1)])
                    b = jnp.where(sub < 4, land[at(1, -1)], land[at(-1, -1)])
                a = pltpu.roll(a, (128 - 4 * px) % 128, 1) if px else a
                b = pltpu.roll(b, 124 - 4 * px, 1)
                dst[xp, 8 * t : 8 * t + 8, 128:256] = jnp.where(lane < 64, a, b)

    def start_1(src, i, n):
        pack, land = pack_1.at[i], land_1.at[i]
        for k in range(4):
            pack[k] = jnp.where(lane < 64, src[2 * k, 0:8, :], pltpu.roll(src[2 * k + 1, 0:8, :], 64, 1))
        for t in range(2):
            up = jnp.zeros((8, 128), F32)
            down = jnp.zeros((8, 128), F32)
            for j in range(4):
                p = src[4 * t + j, 0:8, :]
                here = (lane >= 32 * j) & (lane < 32 * j + 32)
                up = jnp.where(here, pltpu.roll(p, (32 * j + 96) % 128, 1) if j != 1 else p, up)
                down = jnp.where(here, pltpu.roll(p, 32 * j, 1) if j else p, down)
            pack[4 + t] = up
            pack[6 + t] = down
        for d in BOX:
            at, count = SLOT_1[d]
            if d[2] == 0:
                first = 2 if d[0] == 1 else 0
            else:
                first = (4 if d[2] == 1 else 6) + (1 if d[0] == 1 else 0)
            send(pack.at[pl.ds(first, count)], land.at[pl.ds(at, count)], d, n)

    def finish_1(dst, i, n):
        land = land_1.at[i]
        arrive(land, n)
        for xp in range(16):
            sx, px = (0, xp) if xp < 8 else (1, xp - 8) if xp < 12 else (-1, xp - 8)
            half = 1 if sx == -1 else 0

            def piece(y, z):
                at = SLOT_1[(-sx, -y, -z)][0]
                return land[at + px // 2 - 2 * half] if z == 0 else land[at + px // 4 - half]

            for t in range(2):
                if t == 0:
                    a, b = piece(0, 1), piece(0, -1)
                    if sx == 0:
                        m = dst[xp, 0:8, :]
                    else:
                        m = piece(0, 0)
                else:
                    m, a, b = (jnp.where(sub < 4, piece(1, z), piece(-1, z)) for z in (0, 1, -1))
                if px % 2 and not (t == 0 and sx == 0):
                    m = pltpu.roll(m, 64, 1)
                sa, sb = (64 - 32 * (px % 4)) % 128, 96 - 32 * (px % 4)
                a = pltpu.roll(a, sa, 1) if sa else a
                b = pltpu.roll(b, sb, 1) if sb else b
                dst[xp, 8 * t : 8 * t + 8, :] = jnp.where(lane < 64, m, jnp.where(lane < 96, a, b))

    def start_2z(i, n):
        for k in range(1, shape[2]):
            send(pack_2.at[i], land_2z.at[i, k - 1], (0, 0, -k), n)

    def finish_2z(i, n):
        arrive(land_2z.at[i], n)
        whole = pack_2[i]
        for k in range(1, shape[2]):
            whole = whole + land_2z[i, k - 1]
        return whole

    def start_2(whole, i, n):
        full_2[i] = whole
        for j, d in enumerate(BOX2):
            send(full_2.at[i], land_2.at[i, j], (d[0], d[1], 0), n)

    def place_2(dst, block, sx, sy):
        x0 = 0 if sx == 0 else 4 if sx == 1 else 8
        y0 = 0 if sy == 0 else 4 if sy == 1 else 12
        for p in range(4):
            dst[x0 + p, y0 : y0 + 4, :] = block[4 * p : 4 * p + 4, :]

    def finish_2(dst, i, n, own=True):
        arrive(land_2.at[i], n)
        for j, d in enumerate(BOX2):
            place_2(dst, land_2[i, j], -d[0], -d[1])
        if own:
            place_2(dst, full_2[i], 0, 0)

    def start_3y(i, n):
        for k in range(1, shape[1]):
            send(pack_3.at[i], land_3y.at[i, k - 1], (0, -k, 0), n)

    def finish_3y(i, n):
        arrive(land_3y.at[i], n)
        col_3[i, 0:2, :] = pack_3[i]
        for k in range(1, shape[1]):
            col_3[i, 2 * k : 2 * k + 2, :] = land_3y[i, k - 1]

    def x_steps():
        return [k for k in range(-REACH, REACH + 1) if k]

    def start_3x(i, n):
        for j, k in enumerate(x_steps()):
            send(col_3.at[i], land_3x.at[i, j], (-k, 0, 0), n)

    def finish_3x(dst, i, n):
        arrive(land_3x.at[i], n)
        for k in range(-REACH, REACH + 1):
            pair = col_3[i] if k == 0 else land_3x[i, x_steps().index(k)]
            dst[(2 * k) % 22] = pair
            dst[(2 * k + 1) % 22] = pltpu.roll(pair, 64, 1)

    def around(ref, x, size):
        nx = size[0]
        v = ref[x]
        nxt = ref[jnp.where(x == nx - 1, 0, x + 1)]
        prv = ref[jnp.where(x == 0, nx - 1, x - 1)]
        return v, (
            nxt, prv,
            pltpu.roll(v, size[1] - 1, 0), pltpu.roll(v, 1, 0),
            pltpu.roll(v, size[2] - 1, 1), pltpu.roll(v, 1, 1),
        )

    def coefficients(lv):
        i = lv.index
        X, Y, Z = lv.size
        rows = lax.broadcasted_iota(jnp.int32, (Y, Z), 0)
        lanes = lax.broadcasted_iota(jnp.int32, (Y, Z), 1)
        y = wrap(me[1] * lv.own[1] + jnp.where(rows < lv.split[1], rows, rows - Y), lv.total[1])
        z = wrap(me[2] * lv.own[2] + jnp.where(lanes < lv.split[2], lanes, lanes - Z), lv.total[2])
        sides = [
            jnp.where(y == lv.total[1] - 1, 0.0, 1.0), jnp.where(y == 0, 0.0, 1.0),
            jnp.where(z == lv.total[2] - 1, 0.0, 1.0), jnp.where(z == 0, 0.0, 1.0),
        ]

        def body(x, carry):
            at = wrap(me[0] * lv.own[0] + jnp.where(x < lv.split[0], x, x - X), lv.total[0])
            masks = [jnp.where(at == lv.total[0] - 1, 0.0, 1.0), jnp.where(at == 0, 0.0, 1.0)] + sides
            k, near = around(K[i], x, lv.size)
            c = [0.5 * (k + m * o) for m, o in zip(masks, near)]
            total = c[0] + c[1] + c[2] + c[3] + c[4] + c[5]
            total = jnp.where(total > 0.5, total, 1.0)
            inv = OMEGA / total
            for j in range(6):
                C[i][j, x] = c[j] * masks[j] * inv
            IW[i][x] = inv * (1.0 / lv.scale)
            DW[i][x] = total * (lv.scale / OMEGA)
            return carry

        lax.fori_loop(0, X, body, 0)

    def gathered(lv, src, x):
        i = lv.index
        v, near = around(src, x, lv.size)
        acc = B[i][x]
        for j in range(6):
            acc = acc + C[i][j, x] * near[j]
        return v, acc

    def sweep(lv, src, dst, unroll=True):
        def body(x, carry):
            v, acc = gathered(lv, src, x)
            dst[x] = (1.0 - OMEGA) * v + acc
            return carry

        lax.fori_loop(0, lv.size[0], body, 0, unroll=unroll)

    def residual(lv, src, x):
        v, acc = gathered(lv, src, x)
        return (acc - OMEGA * v) * DW[lv.index][x]

    def eye(shape2, fn):
        r = lax.broadcasted_iota(jnp.int32, shape2, 0)
        c = lax.broadcasted_iota(jnp.int32, shape2, 1)
        return fn(r, c)

    def as_mat(cond, value=1.0):
        return jnp.where(cond, value, 0.0).astype(BF16)

    half = lambda a: lax.shift_right_arithmetic(a, 1)
    down_rows_0 = eye((8, 16), lambda r, c: as_mat(half(c) == r))
    down_rows = eye((8, 8), lambda r, c: as_mat((half(c) == r) & (r < 4)))
    down_lanes_0 = eye((128, 128), lambda r, c: as_mat(half(r) == c, 0.125))
    down_lanes_1 = eye((128, 128), lambda r, c: as_mat((half(r) + me[2] * 32 == c) & (r < 64), 0.125))
    down_lanes_2 = [
        eye((128, 128), lambda r, c: as_mat(half(r) + 64 * p == c, 0.125)) for p in range(2)
    ]

    def restrict_0(plane):
        for p in range(8):
            tall_0[16 * p : 16 * p + 16, :] = plane(2 * p) + plane(2 * p + 1)
        tall_0[...] = right(tall_0[...], down_lanes_0)
        return [left(down_rows_0, tall_0[16 * p : 16 * p + 16, :]) for p in range(8)]

    def restrict_1(plane, i):
        for p in range(4):
            tall_1[8 * p : 8 * p + 8, :] = plane(2 * p) + plane(2 * p + 1)
        tall_1[...] = right(tall_1[...], down_lanes_1)
        for p in range(4):
            pack_2[i, 4 * p : 4 * p + 4, :] = left(down_rows, tall_1[8 * p : 8 * p + 8, :])[0:4]

    def restrict_2(plane, i):
        both = right(plane(0) + plane(1), down_lanes_2[0]) + right(plane(2) + plane(3), down_lanes_2[1])
        pack_3[i] = left(down_rows, both)[0:2]

    def prolong(fine, coarse, e_ref, v_ref, tall, lanes_mat, rows_of):
        XF, YF, ZF = fine.size
        XC, YC, ZC = coarse.size
        rows_mat = eye((YF, YC), lambda r, c: as_mat(rows_of(r) == c))
        todo = {}
        for x in range(XF):
            rel = x if x < fine.split[0] else x - XF
            todo.setdefault((rel // 2) % XC, []).append(x)
        planes = sorted(todo)
        for q, p in enumerate(planes):
            tall[YC * q : YC * q + YC, :] = e_ref[p]
        spread = right(tall[...], lanes_mat)
        for q, p in enumerate(planes):
            out = left(rows_mat, spread[YC * q : YC * q + YC])
            for x in todo[p]:
                v_ref[x] = v_ref[x] + out

    pl.semaphore_wait(barrier, len(all_peers))

    rec[0, 0:8, :] = dest_ref[...].astype(F32)
    rec[0, 8:16, :] = cell_ref[...].astype(F32)
    rec[0, 16:24, :] = val_ref[...]
    for k in range(1, shape[2]):
        send(rec.at[0], rec.at[k], (0, 0, -k), 0)

    up = jnp.zeros((16, 128), F32)
    down = jnp.zeros((16, 128), F32)
    for x in range(16):
        mz = chi_ref[x] * ind_ref[2, x]
        up = jnp.where(lane16 == x, pltpu.roll(mz, (x + 1) % 128, 1), up)
        down = jnp.where(lane16 == x, pltpu.roll(mz, x, 1) if x else mz, down)
        my = chi_ref[x] * ind_ref[1, x]
        mom_out[2, x : x + 1, :] = my[15:16]
        mom_out[3, x : x + 1, :] = my[0:1]
    mom_out[0] = chi_ref[15] * ind_ref[0, 15]
    mom_out[1] = chi_ref[0] * ind_ref[0, 0]
    mom_out[4] = up
    mom_out[5] = down
    FACES = [(1, 0, 0), (-1, 0, 0), (0, 1, 0), (0, -1, 0), (0, 0, 1), (0, 0, -1)]
    for j, d in enumerate(FACES):
        send(mom_out.at[j], mom_in.at[j], d, 1)

    for lv in LEVELS:
        i = lv.index
        if i:
            K[i][...] = jnp.zeros(lv.size, F32)
            B[i][...] = jnp.zeros(lv.size, F32)

    def fill(x, carry):
        K[0][x] = jnp.zeros((24, 256), F32)
        B[0][x] = jnp.zeros((24, 256), F32)
        return carry

    lax.fori_loop(0, 22, fill, 0)
    for x in range(16):
        K[0][x, 0:16, 0:128] = 1.0 + chi_ref[x]
    start_0(K[0], 0, 2)
    for p, block in enumerate(restrict_0(lambda x: K[0][x, 0:16, 0:128])):
        K[1][p, 0:8, :] = block
    start_1(K[1], 0, 3)
    restrict_1(lambda x: K[1][x, 0:8, :], 0)
    start_2z(0, 4)

    rows256 = lax.broadcasted_iota(jnp.int32, (256, 128), 0).astype(F32)
    rows128 = lax.broadcasted_iota(jnp.int32, (128, 128), 0).astype(F32)
    mine = me[2].astype(F32)

    def deposit(s):
        to, cell = rec[s, 0:8, :], rec[s, 8:16, :]
        row = jnp.floor(cell * (1.0 / 128.0))
        col = cell - 128.0 * row
        row = jnp.where(to == mine, row, -1.0)
        parts = [p.astype(F32) for p in split3(rec[s, 16:24, :])]
        for j in range(8):
            hot[:, 128 * j : 128 * j + 128] = jnp.where(rows256 == row[j : j + 1], 1.0, 0.0).astype(BF16)
            same = rows128 == col[j : j + 1]
            for q in range(3):
                val_hot[128 * q : 128 * q + 128, 128 * j : 128 * j + 128] = jnp.where(same, parts[q][j : j + 1], 0.0).astype(BF16)
        got = lax.dot_general(hot[...], val_hot[...], (((1,), (1,)), ((), ())), preferred_element_type=F32)
        return got[:, 0:128] + got[:, 128:256] + got[:, 256:384]

    rhs[...] = deposit(0)

    arrive(rec.at[pl.ds(1, 3)], 0)

    def more(s, carry):
        rhs[...] = rhs[...] + deposit(s)
        return carry

    lax.fori_loop(1, shape[2], more, 0)

    finish_0(K[0], 0, 2)
    coefficients(L0)

    arrive(mom_in, 1)
    inside = [
        jnp.where(me[i] == edge, 0.0, 1.0) for i in range(3) for edge in (shape[i] - 1, 0)
    ]
    row16 = lax.broadcasted_iota(jnp.int32, (16, 128), 0)
    for x in range(16):
        xp = chi_ref[x + 1] * ind_ref[0, x + 1] if x < 15 else mom_in[1] * inside[0]
        xm = chi_ref[x - 1] * ind_ref[0, x - 1] if x > 0 else mom_in[0] * inside[1]
        my = chi_ref[x] * ind_ref[1, x]
        yp = jnp.where(row16 == 15, mom_in[3, x : x + 1, :] * inside[2], pltpu.roll(my, 15, 0))
        ym = jnp.where(row16 == 0, mom_in[2, x : x + 1, :] * inside[3], pltpu.roll(my, 1, 0))
        mz = chi_ref[x] * ind_ref[2, x]
        far = pltpu.roll(mom_in[5] * inside[4], 127 - x, 1)
        near = mom_in[4] * inside[5]
        near = pltpu.roll(near, 128 - x, 1) if x else near
        zp = jnp.where(lane16 == 127, far, pltpu.roll(mz, 127, 1))
        zm = jnp.where(lane16 == 0, near, pltpu.roll(mz, 1, 1))
        total = -0.5 * (xp - xm + (yp - ym) + (zp - zm)) + rhs[16 * x : 16 * x + 16, :]
        B[0][x, 0:16, 0:128] = total * IW[0][x, 0:16, 0:128]
    start_0(B[0], 1, 5)

    finish_1(K[1], 0, 3)
    coefficients(L1)
    start_2(finish_2z(0, 4), 0, 6)
    for p in range(4):
        K[2][p, 0:4, :] = full_2[0, 4 * p : 4 * p + 4, :]
    restrict_2(lambda x: K[2][x, 0:8, :], 0)
    start_3y(0, 7)

    finish_0(B[0], 1, 5)
    sweep(L0, B[0], VA[0])

    blocks = restrict_0(lambda x: residual(L0, VA[0], x)[0:16, 0:128])
    for p, block in enumerate(blocks):
        B[1][p, 0:8, :] = block * IW[1][p, 0:8, :]
    start_1(B[1], 1, 8)
    finish_2(K[2], 0, 6)
    coefficients(L2)
    finish_3y(0, 7)
    start_3x(0, 9)

    finish_1(B[1], 1, 8)
    sweep(L1, B[1], VA[1])
    restrict_1(lambda x: residual(L1, VA[1], x)[0:8, :], 1)
    start_2z(1, 10)
    finish_3x(K[3], 0, 9)
    coefficients(L3)

    whole = finish_2z(1, 10)
    for p in range(4):
        B[2][p, 0:4, :] = whole[4 * p : 4 * p + 4, :] * IW[2][p, 0:4, :]
        full_2[1, 4 * p : 4 * p + 4, :] = B[2][p, 0:4, :]
    start_2(full_2[1], 1, 11)
    finish_2(B[2], 1, 11, own=False)
    sweep(L2, B[2], VA[2])
    restrict_2(lambda x: residual(L2, VA[2], x)[0:8, :], 1)
    own_rows = pack_3[1]
    low = IW[3][0, 0:2, :]
    high = pltpu.roll(IW[3][1], 64, 1)[0:2, :]
    pack_3[1] = own_rows * jnp.where(lax.broadcasted_iota(jnp.int32, (2, 128), 1) < 64, low, high)
    start_3y(1, 12)
    for p in range(4):
        full_2[2, 4 * p : 4 * p + 4, :] = VA[2][p, 0:4, :]
    start_2(full_2[2], 2, 13)

    finish_3y(1, 12)
    start_3x(1, 14)
    finish_2(VA[2], 2, 13, own=False)
    finish_3x(B[3], 1, 14)
    sweep(L3, B[3], VA[3])

    def two(_, carry):
        sweep(L3, VA[3], VB[3])
        sweep(L3, VB[3], VA[3])
        return carry

    lax.fori_loop(0, 3, two, 0)

    up_2 = eye((128, 128), lambda r, c: as_mat(r == half(c)))
    prolong(L2, L3, VA[3], VA[2], tall_2, up_2, lambda r: wrap(half(jnp.where(r < 8, r, r - 16)), 24))
    sweep(L2, VA[2], VB[2])
    sweep(L2, VB[2], VA[2])
    up_1 = eye((128, 128), lambda r, c: as_mat(r == wrap(half(jnp.where(c < 96, c, c - 128)) + 32 * me[2], 128)))
    prolong(L1, L2, VA[2], VA[1], tall_3, up_1, lambda r: wrap(half(jnp.where(r < 12, r, r - 16)), 16))
    sweep(L1, VA[1], VB[1])
    sweep(L1, VB[1], VA[1])
    up_0 = eye((128, 256), lambda r, c: as_mat(r == wrap(half(jnp.where(c < 192, c, c - 256)), 128)))
    prolong(L0, L1, VA[1], VA[0], tall_4, up_0, lambda r: wrap(half(jnp.where(r < 20, r, r - 24)), 16))
    sweep(L0, VA[0], VB[0])

    for x in range(16):
        v, acc = gathered(L0, VB[0], x)
        out_ref[x] = ((1.0 - OMEGA) * v + acc)[0:16, 0:128]

    sent(rec.at[pl.ds(1, 3)], 0)
    sent(mom_in, 1)
    for i, n in ((0, 2), (1, 5)):
        sent(land_0.at[i], n)
    for i, n in ((0, 3), (1, 8)):
        sent(land_1.at[i], n)
    for i, n in ((0, 4), (1, 10)):
        sent(land_2z.at[i], n)
    for i, n in ((0, 6), (1, 11), (2, 13)):
        sent(land_2.at[i], n)
    for i, n in ((0, 7), (1, 12)):
        sent(land_3y.at[i], n)
    for i, n in ((0, 9), (1, 14)):
        sent(land_3x.at[i], n)


def scratch(shape):
    out = []
    for lv in LEVELS:
        out += [pltpu.VMEM(lv.size, F32)] * 6 + [pltpu.VMEM((6,) + lv.size, F32)]
    ny, nz = shape[1], shape[2]
    out += [
        pltpu.VMEM((nz, 24, 128), F32), pltpu.VMEM((6, 16, 128), F32), pltpu.VMEM((6, 16, 128), F32),
        pltpu.VMEM((256, 1024), BF16), pltpu.VMEM((384, 1024), BF16), pltpu.VMEM((256, 128), F32),
        pltpu.VMEM((2, 32, 8, 128), F32), pltpu.VMEM((2, TILES_0, 8, 128), F32),
        pltpu.VMEM((2, 8, 8, 128), F32), pltpu.VMEM((2, TILES_1, 8, 128), F32),
        pltpu.VMEM((2, 16, 128), F32), pltpu.VMEM((2, nz - 1, 16, 128), F32),
        pltpu.VMEM((3, 16, 128), F32), pltpu.VMEM((3, 8, 16, 128), F32),
        pltpu.VMEM((2, 2, 128), F32), pltpu.VMEM((2, ny - 1, 2, 128), F32),
        pltpu.VMEM((2, 24, 128), F32), pltpu.VMEM((2, 2 * REACH, 24, 128), F32),
        pltpu.VMEM((128, 128), F32), pltpu.VMEM((32, 128), F32),
        pltpu.VMEM((144, 128), F32), pltpu.VMEM((128, 128), F32),
        pltpu.VMEM((192, 128), F32),
        pltpu.SemaphoreType.DMA((15,)), pltpu.SemaphoreType.DMA((15,)),
    ]
    return out


def per_device(shape, chi, inducing, record_dest, record_cell, record_value):
    vmem = pl.BlockSpec(memory_space=pltpu.VMEM)
    return pl.pallas_call(
        functools.partial(kernel, shape),
        out_shape=jax.ShapeDtypeStruct((16, 16, 128), F32),
        in_specs=[vmem] * 5,
        out_specs=vmem,
        scratch_shapes=scratch(shape),
        compiler_params=pltpu.CompilerParams(
            collective_id=0, has_side_effects=True, vmem_limit_bytes=40 * 1024 * 1024
        ),
        name="cycle",
    )(chi, inducing, record_dest.reshape(8, 128), record_cell.reshape(8, 128), record_value.reshape(8, 128))


def solution(mesh):
    shape = tuple(mesh.shape[a] for a in ("gx", "gy", "gz"))
    placed = (
        P("gx", "gy", "gz"),
        P(None, "gx", "gy", "gz"),
        P("gx", "gy", "gz", None, None),
        P("gx", "gy", "gz", None),
        P("gx", "gy", "gz", None),
    )
    return jax.shard_map(
        functools.partial(per_device, shape), mesh=mesh, in_specs=placed, out_specs=P("gx", "gy", "gz"), check_vma=False
    )
```

```python
import functools
import itertools

import jax
import jax.numpy as jnp
from jax import lax
from jax.experimental import pallas as pl
from jax.experimental.pallas import tpu as pltpu
from jax.sharding import PartitionSpec as P

OMEGA = 0.8
F32 = jnp.float32
BF16 = jnp.bfloat16
MESH = pl.DeviceIdType.MESH
BOX = [d for d in itertools.product((-1, 0, 1), repeat=3) if d != (0, 0, 0)]
BOX.sort(key=lambda d: -sum(map(abs, d)))
BOX2 = [d for d in itertools.product((-1, 0, 1), repeat=2) if d != (0, 0)]
REACH = 5


class Level:
    def __init__(self, index, own, size, split, total):
        self.index, self.own, self.size, self.split, self.total = index, own, size, split, total
        self.scale = 0.25**index


L0 = Level(0, (16, 16, 128), (22, 24, 256), (19, 20, 192), (256, 192, 512))
L1 = Level(1, (8, 8, 64), (16, 16, 128), (12, 12, 96), (128, 96, 256))
L2 = Level(2, (4, 4, 0), (12, 16, 128), (8, 8, 128), (64, 48, 128))
L3 = Level(3, (2, 2, 0), (22, 24, 128), (12, 24, 128), (32, 24, 64))
LEVELS = (L0, L1, L2, L3)


def tiles_0(d):
    if d[2] == 0:
        if d[1] == 0:
            return 6
        return 8 if d[0] == 0 else 2
    return 2 if d[1] == 0 else 1


def tiles_1(d):
    if d[2] == 0:
        return 4 if d[0] == 0 else 2
    return 2 if d[0] == 0 else 1


def slots(count_of):
    table, at = {}, 0
    for d in BOX:
        table[d] = (at, count_of(d))
        at += count_of(d)
    return table, at


SLOT_0, TILES_0 = slots(tiles_0)
SLOT_1, TILES_1 = slots(tiles_1)


def peers(shape):
    nx, ny, nz = shape
    out = [tuple(d) for d in BOX]
    out += [(0, 0, k) for k in range(2, nz - 1)]
    out += [(0, k, 0) for k in range(-REACH, REACH + 1) if abs(k) > 1]
    out += [(k, 0, 0) for k in range(-REACH, REACH + 1) if abs(k) > 1]
    return out


def split3(x):
    hi = x.astype(BF16)
    rest = x - hi.astype(F32)
    mid = rest.astype(BF16)
    low = (rest - mid.astype(F32)).astype(BF16)
    return hi, mid, low


def right(x, mat):
    parts = [jnp.dot(p, mat, preferred_element_type=F32) for p in split3(x)]
    return parts[0] + parts[1] + parts[2]


def left(mat, x):
    parts = [jnp.dot(mat, p, preferred_element_type=F32) for p in split3(x)]
    return parts[0] + parts[1] + parts[2]


def wrap(at, size):
    return jnp.where(at < 0, at + size, jnp.where(at >= size, at - size, at))


def kernel(shape, chi_hbm, ind_hbm, dest_hbm, cell_hbm, val_hbm, out_ref, *refs):
    it = iter(refs)
    take = lambda n: [next(it) for _ in range(n)]
    K, B, VA, VB, IW, DW = [], [], [], [], [], []
    C = []
    for _ in LEVELS:
        k, b, va, vb, iw, dw, c = take(7)
        K.append(k), B.append(b), VA.append(va), VB.append(vb), IW.append(iw), DW.append(dw), C.append(c)
    rec, mom_out, mom_in, hot, val_hot, rhs = take(6)
    pack_0, land_0, pack_1, land_1 = take(4)
    pack_2, land_2z, full_2, land_2 = take(4)
    pack_3, land_3y, col_3, land_3x = take(4)
    tall_0, tall_1, tall_2, tall_3, tall_4 = take(5)
    chi, ind, rec_in, val_in = take(4)
    send_sem, recv_sem, load_sem = take(3)

    me = [lax.axis_index(a) for a in ("gx", "gy", "gz")]

    def device(o):
        return tuple(lax.rem(me[i] + (o[i] + shape[i]), shape[i]) for i in range(3))

    barrier = pltpu.get_barrier_semaphore()
    all_peers = peers(shape)
    for o in all_peers:
        pl.semaphore_signal(barrier, inc=1, device_id=device(o), device_id_type=MESH)

    copies = [
        pltpu.make_async_copy(src, dst, load_sem.at[j])
        for j, (src, dst) in enumerate([
            (chi_hbm, chi), (ind_hbm, ind), (dest_hbm, rec_in.at[0]), (cell_hbm, rec_in.at[1]), (val_hbm, val_in),
        ])
    ]
    for j in (2, 3, 4, 0, 1):
        copies[j].start()

    sub = lax.broadcasted_iota(jnp.int32, (8, 128), 0)
    lane = lax.broadcasted_iota(jnp.int32, (8, 128), 1)
    lane16 = lax.broadcasted_iota(jnp.int32, (16, 128), 1)

    def send(src, dst, o, n):
        pltpu.make_async_remote_copy(
            src_ref=src, dst_ref=dst, send_sem=send_sem.at[n], recv_sem=recv_sem.at[n],
            device_id=device(o), device_id_type=MESH,
        ).start()

    def arrive(ref, n):
        pltpu.make_async_copy(ref, ref, recv_sem.at[n]).wait()

    def sent(ref, n):
        pltpu.make_async_copy(ref, ref, send_sem.at[n]).wait()

    def make_0(src, i):
        pack = pack_0.at[i]
        for p in range(3):
            for t in range(2):
                pack[2 * p + t] = src[13 + p, 8 * t : 8 * t + 8, 0:128]
                pack[6 + 2 * p + t] = src[p, 8 * t : 8 * t + 8, 0:128]
        for k in range(8):
            pack[12 + k] = jnp.where(sub >= 4, src[2 * k, 8:16, 0:128], pltpu.roll(src[2 * k + 1, 8:16, 0:128], 4, 0))
            pack[20 + k] = jnp.where(sub < 4, src[2 * k, 0:8, 0:128], pltpu.roll(src[2 * k + 1, 0:8, 0:128], 4, 0))
        up = jnp.zeros((16, 128), F32)
        down = jnp.zeros((16, 128), F32)
        for x in range(16):
            p = src[x, 0:16, 0:128]
            here = (lane16 >= 4 * x) & (lane16 < 4 * x + 4)
            up = jnp.where(here, pltpu.roll(p, (4 * x + 4) % 128, 1), up)
            down = jnp.where(here, pltpu.roll(p, 4 * x, 1) if x else p, down)
        for t in range(2):
            pack[28 + t] = up[8 * t : 8 * t + 8]
            pack[30 + t] = down[8 * t : 8 * t + 8]

    def ship_0(i, n):
        pack, land = pack_0.at[i], land_0.at[i]
        for d in BOX:
            at, count = SLOT_0[d]
            if d[2] == 0:
                if d[1] == 0:
                    first = 0 if d[0] == 1 else 6
                else:
                    first = (12 if d[1] == 1 else 20) + (6 if d[0] == 1 else 0)
            else:
                first = (28 if d[2] == 1 else 30) + (1 if d[1] == 1 else 0)
            send(pack.at[pl.ds(first, count)], land.at[pl.ds(at, count)], d, n)

    def finish_0(dst, i, n):
        land = land_0.at[i]
        arrive(land, n)
        for xp in range(22):
            sx, px = (0, xp) if xp < 16 else (1, xp - 16) if xp < 19 else (-1, xp - 6)
            at = lambda y, z: SLOT_0[(-sx, -y, -z)][0]
            base = 6 if sx == -1 else 0
            if sx:
                row = px - 13 if sx == -1 else px
                dst[xp, 0:8, 0:128] = land[at(0, 0) + 2 * row]
                dst[xp, 8:16, 0:128] = land[at(0, 0) + 2 * row + 1]
            k = px // 2 - base
            above, below = land[at(1, 0) + k], land[at(-1, 0) + k]
            if px % 2:
                above, below = pltpu.roll(above, 4, 0), pltpu.roll(below, 4, 0)
            dst[xp, 16:24, 0:128] = jnp.where(sub < 4, above, below)
            for t in range(3):
                if t < 2:
                    a, b = land[at(0, 1) + t], land[at(0, -1) + t]
                else:
                    a = jnp.where(sub < 4, land[at(1, 1)], land[at(-1, 1)])
                    b = jnp.where(sub < 4, land[at(1, -1)], land[at(-1, -1)])
                a = pltpu.roll(a, (128 - 4 * px) % 128, 1) if px else a
                b = pltpu.roll(b, 124 - 4 * px, 1)
                dst[xp, 8 * t : 8 * t + 8, 128:256] = jnp.where(lane < 64, a, b)

    def start_1(src, i, n):
        pack, land = pack_1.at[i], land_1.at[i]
        for k in range(4):
            pack[k] = jnp.where(lane < 64, src[2 * k, 0:8, :], pltpu.roll(src[2 * k + 1, 0:8, :], 64, 1))
        for t in range(2):
            up = jnp.zeros((8, 128), F32)
            down = jnp.zeros((8, 128), F32)
            for j in range(4):
                p = src[4 * t + j, 0:8, :]
                here = (lane >= 32 * j) & (lane < 32 * j + 32)
                up = jnp.where(here, pltpu.roll(p, (32 * j + 96) % 128, 1) if j != 1 else p, up)
                down = jnp.where(here, pltpu.roll(p, 32 * j, 1) if j else p, down)
            pack[4 + t] = up
            pack[6 + t] = down
        for d in BOX:
            at, count = SLOT_1[d]
            if d[2] == 0:
                first = 2 if d[0] == 1 else 0
            else:
                first = (4 if d[2] == 1 else 6) + (1 if d[0] == 1 else 0)
            send(pack.at[pl.ds(first, count)], land.at[pl.ds(at, count)], d, n)

    def finish_1(dst, i, n):
        land = land_1.at[i]
        arrive(land, n)
        for xp in range(16):
            sx, px = (0, xp) if xp < 8 else (1, xp - 8) if xp < 12 else (-1, xp - 8)
            half = 1 if sx == -1 else 0

            def piece(y, z):
                at = SLOT_1[(-sx, -y, -z)][0]
                return land[at + px // 2 - 2 * half] if z == 0 else land[at + px // 4 - half]

            for t in range(2):
                if t == 0:
                    a, b = piece(0, 1), piece(0, -1)
                    if sx == 0:
                        m = dst[xp, 0:8, :]
                    else:
                        m = piece(0, 0)
                else:
                    m, a, b = (jnp.where(sub < 4, piece(1, z), piece(-1, z)) for z in (0, 1, -1))
                if px % 2 and not (t == 0 and sx == 0):
                    m = pltpu.roll(m, 64, 1)
                sa, sb = (64 - 32 * (px % 4)) % 128, 96 - 32 * (px % 4)
                a = pltpu.roll(a, sa, 1) if sa else a
                b = pltpu.roll(b, sb, 1) if sb else b
                dst[xp, 8 * t : 8 * t + 8, :] = jnp.where(lane < 64, m, jnp.where(lane < 96, a, b))

    def start_2z(i, n):
        for k in (2, 1, 3):
            send(pack_2.at[i], land_2z.at[i, k - 1], (0, 0, -k), n)

    def finish_2z(i, n):
        arrive(land_2z.at[i], n)
        whole = pack_2[i]
        for k in range(1, shape[2]):
            whole = whole + land_2z[i, k - 1]
        return whole

    def start_2(whole, i, n):
        full_2[i] = whole
        for j, d in enumerate(BOX2):
            send(full_2.at[i], land_2.at[i, j], (d[0], d[1], 0), n)

    def place_2(dst, block, sx, sy):
        x0 = 0 if sx == 0 else 4 if sx == 1 else 8
        y0 = 0 if sy == 0 else 4 if sy == 1 else 12
        for p in range(4):
            dst[x0 + p, y0 : y0 + 4, :] = block[4 * p : 4 * p + 4, :]

    def finish_2(dst, i, n, own=True):
        arrive(land_2.at[i], n)
        for j, d in enumerate(BOX2):
            place_2(dst, land_2[i, j], -d[0], -d[1])
        if own:
            place_2(dst, full_2[i], 0, 0)

    steps = sorted([k for k in range(-REACH, REACH + 1) if k], key=lambda k: -abs(k))

    def start_3y(i, n):
        for j, k in enumerate(steps):
            send(pack_3.at[i], land_3y.at[i, j], (0, -k, 0), n)

    def finish_3y(i, n):
        arrive(land_3y.at[i], n)
        col_3[i, 2 * REACH + 2 : 24 - 2 * REACH, :] = jnp.zeros((22 - 4 * REACH, 128), F32)
        col_3[i, 0:2, :] = pack_3[i]
        for j, k in enumerate(steps):
            row = (2 * k) % 24
            col_3[i, row : row + 2, :] = land_3y[i, j]

    def start_3x(i, n):
        for j, k in enumerate(steps):
            send(col_3.at[i], land_3x.at[i, j], (-k, 0, 0), n)

    def finish_3x(dst, i, n):
        arrive(land_3x.at[i], n)
        for k in range(-REACH, REACH + 1):
            pair = col_3[i] if k == 0 else land_3x[i, steps.index(k)]
            dst[(2 * k) % 22] = pair
            dst[(2 * k + 1) % 22] = pltpu.roll(pair, 64, 1)

    def around(ref, x, size):
        nx = size[0]
        v = ref[x]
        return v, (
            ref[(x + 1) % nx], ref[(x - 1) % nx],
            pltpu.roll(v, size[1] - 1, 0), pltpu.roll(v, 1, 0),
            pltpu.roll(v, size[2] - 1, 1), pltpu.roll(v, 1, 1),
        )

    def planes(lv, halo):
        return [r % lv.size[0] for r in range(-halo, lv.own[0] + halo)]

    def edge_masks(lv):
        X, Y, Z = lv.size
        rows = lax.broadcasted_iota(jnp.int32, (Y, Z), 0)
        lanes = lax.broadcasted_iota(jnp.int32, (Y, Z), 1)
        y = wrap(me[1] * lv.own[1] + jnp.where(rows < lv.split[1], rows, rows - Y), lv.total[1])
        z = wrap(me[2] * lv.own[2] + jnp.where(lanes < lv.split[2], lanes, lanes - Z), lv.total[2])
        sides = [
            jnp.where(y == lv.total[1] - 1, 0.0, 1.0), jnp.where(y == 0, 0.0, 1.0),
            jnp.where(z == lv.total[2] - 1, 0.0, 1.0), jnp.where(z == 0, 0.0, 1.0),
        ]

        def at(x):
            rel = x if x < lv.split[0] else x - X
            g = wrap(me[0] * lv.own[0] + rel, lv.total[0])
            return [jnp.where(g == lv.total[0] - 1, 0.0, 1.0), jnp.where(g == 0, 0.0, 1.0)] + sides

        return at

    def face_sums(lv, x, masks):
        k, near = around(K[lv.index], x, lv.size)
        c = [0.5 * (k + m * o) for m, o in zip(masks, near)]
        total = c[0] + c[1] + c[2] + c[3] + c[4] + c[5]
        return c, jnp.where(total > 0.5, total, 1.0)

    def coefficients(lv, halo):
        i = lv.index
        at = edge_masks(lv)
        for x in planes(lv, halo):
            masks = at(x)
            c, total = face_sums(lv, x, masks)
            inv = OMEGA / total
            for j in range(6):
                C[i][j, x] = c[j] * masks[j] * inv
            if x < lv.own[0]:
                IW[i][x] = inv * (1.0 / lv.scale)
                DW[i][x] = total * (lv.scale / OMEGA)

    def gathered(lv, src, x):
        i = lv.index
        v, near = around(src, x, lv.size)
        acc = B[i][x]
        for j in range(6):
            acc = acc + C[i][j, x] * near[j]
        return v, acc

    def sweep(lv, src, dst, halo):
        for x in planes(lv, halo):
            v, acc = gathered(lv, src, x)
            dst[x] = (1.0 - OMEGA) * v + acc

    def residual(lv, src, x):
        v, acc = gathered(lv, src, x)
        return (acc - OMEGA * v) * DW[lv.index][x]

    def eye(shape2, fn):
        r = lax.broadcasted_iota(jnp.int32, shape2, 0)
        c = lax.broadcasted_iota(jnp.int32, shape2, 1)
        return fn(r, c)

    def as_mat(cond, value=1.0):
        return jnp.where(cond, value, 0.0).astype(BF16)

    half = lambda a: lax.shift_right_arithmetic(a, 1)
    down_rows_0 = eye((8, 16), lambda r, c: as_mat(half(c) == r))
    down_rows = eye((8, 8), lambda r, c: as_mat((half(c) == r) & (r < 4)))
    down_lanes_0 = eye((128, 128), lambda r, c: as_mat(half(r) == c, 0.125))
    down_lanes_1 = eye((128, 128), lambda r, c: as_mat((half(r) + me[2] * 32 == c) & (r < 64), 0.125))
    down_lanes_2 = [
        eye((128, 128), lambda r, c: as_mat(half(r) + 64 * p == c, 0.125)) for p in range(2)
    ]

    def restrict_0(plane):
        for p in range(8):
            tall_0[16 * p : 16 * p + 16, :] = plane(2 * p) + plane(2 * p + 1)
        tall_0[...] = right(tall_0[...], down_lanes_0)
        return [left(down_rows_0, tall_0[16 * p : 16 * p + 16, :]) for p in range(8)]

    def restrict_1(plane, i):
        for p in range(4):
            tall_1[8 * p : 8 * p + 8, :] = plane(2 * p) + plane(2 * p + 1)
        tall_1[...] = right(tall_1[...], down_lanes_1)
        for p in range(4):
            pack_2[i, 4 * p : 4 * p + 4, :] = left(down_rows, tall_1[8 * p : 8 * p + 8, :])[0:4]

    def restrict_2(plane, i):
        both = right(plane(0) + plane(1), down_lanes_2[0]) + right(plane(2) + plane(3), down_lanes_2[1])
        pack_3[i] = left(down_rows, both)[0:2]

    def prolong(fine, coarse, halo, e_ref, v_ref, tall, lanes_mat, rows_of):
        XF, YF, ZF = fine.size
        XC, YC, ZC = coarse.size
        rows_mat = eye((YF, YC), lambda r, c: as_mat(rows_of(r) == c))
        todo = {}
        for rel in range(-halo, fine.own[0] + halo):
            todo.setdefault((rel // 2) % XC, []).append(rel % XF)
        for q, p in enumerate(todo):
            tall[YC * q : YC * q + YC, :] = e_ref[p]
        spread = right(tall[...], lanes_mat)
        for q, p in enumerate(todo):
            out = left(rows_mat, spread[YC * q : YC * q + YC])
            for x in todo[p]:
                v_ref[x] = v_ref[x] + out

    for copy in copies[2:]:
        copy.wait()
    rec[0, 0:8, :] = rec_in[0].astype(F32)
    rec[0, 8:16, :] = rec_in[1].astype(F32)
    rec[0, 16:24, :] = val_in[...]
    copies[0].wait()
    for x in range(16):
        K[0][x, 0:16, 0:128] = 1.0 + chi[x]
    make_0(K[0], 0)
    copies[1].wait()
    up = jnp.zeros((16, 128), F32)
    down = jnp.zeros((16, 128), F32)
    for x in range(16):
        mz = chi[x] * ind[2, x]
        up = jnp.where(lane16 == x, pltpu.roll(mz, (x + 1) % 128, 1), up)
        down = jnp.where(lane16 == x, pltpu.roll(mz, x, 1) if x else mz, down)
        my = chi[x] * ind[1, x]
        mom_out[2, x : x + 1, :] = my[15:16]
        mom_out[3, x : x + 1, :] = my[0:1]
    mom_out[0] = chi[15] * ind[0, 15]
    mom_out[1] = chi[0] * ind[0, 0]
    mom_out[4] = up
    mom_out[5] = down

    pl.semaphore_wait(barrier, len(all_peers))

    for k in (2, 1, 3):
        send(rec.at[0], rec.at[k], (0, 0, -k), 0)
    FACES = [(1, 0, 0), (-1, 0, 0), (0, 1, 0), (0, -1, 0), (0, 0, 1), (0, 0, -1)]
    for j, d in enumerate(FACES):
        send(mom_out.at[j], mom_in.at[j], d, 1)
    ship_0(0, 2)

    for ref in (K[2], B[2]):
        for x in range(12):
            ref[x, 8:16, :] = jnp.zeros((8, 128), F32)
    for p, block in enumerate(restrict_0(lambda x: K[0][x, 0:16, 0:128])):
        K[1][p, 0:8, :] = block
    start_1(K[1], 0, 3)
    restrict_1(lambda x: K[1][x, 0:8, :], 0)
    start_2z(0, 4)

    rows256 = lax.broadcasted_iota(jnp.int32, (256, 128), 0).astype(F32)
    rows128 = lax.broadcasted_iota(jnp.int32, (128, 128), 0).astype(F32)
    mine = me[2].astype(F32)

    def deposit(s):
        to, cell = rec[s, 0:8, :], rec[s, 8:16, :]
        row = jnp.floor(cell * (1.0 / 128.0))
        col = cell - 128.0 * row
        row = jnp.where(to == mine, row, -1.0)
        parts = [p.astype(F32) for p in split3(rec[s, 16:24, :])]
        for j in range(8):
            hot[:, 128 * j : 128 * j + 128] = jnp.where(rows256 == row[j : j + 1], 1.0, 0.0).astype(BF16)
            same = rows128 == col[j : j + 1]
            for q in range(3):
                val_hot[128 * q : 128 * q + 128, 128 * j : 128 * j + 128] = jnp.where(same, parts[q][j : j + 1], 0.0).astype(BF16)
        got = lax.dot_general(hot[...], val_hot[...], (((1,), (1,)), ((), ())), preferred_element_type=F32)
        return got[:, 0:128] + got[:, 128:256] + got[:, 256:384]

    rhs[...] = deposit(0)

    arrive(rec.at[pl.ds(1, 3)], 0)

    def more(s, carry):
        rhs[...] = rhs[...] + deposit(s)
        return carry

    lax.fori_loop(1, shape[2], more, 0)

    finish_0(K[0], 0, 2)

    arrive(mom_in, 1)
    inside = [
        jnp.where(me[i] == edge, 0.0, 1.0) for i in range(3) for edge in (shape[i] - 1, 0)
    ]
    masks_0 = edge_masks(L0)
    row16 = lax.broadcasted_iota(jnp.int32, (16, 128), 0)
    for x in range(16):
        xp = chi[x + 1] * ind[0, x + 1] if x < 15 else mom_in[1] * inside[0]
        xm = chi[x - 1] * ind[0, x - 1] if x > 0 else mom_in[0] * inside[1]
        my = chi[x] * ind[1, x]
        yp = jnp.where(row16 == 15, mom_in[3, x : x + 1, :] * inside[2], pltpu.roll(my, 15, 0))
        ym = jnp.where(row16 == 0, mom_in[2, x : x + 1, :] * inside[3], pltpu.roll(my, 1, 0))
        mz = chi[x] * ind[2, x]
        far = pltpu.roll(mom_in[5] * inside[4], 127 - x, 1)
        near = mom_in[4] * inside[5]
        near = pltpu.roll(near, 128 - x, 1) if x else near
        zp = jnp.where(lane16 == 127, far, pltpu.roll(mz, 127, 1))
        zm = jnp.where(lane16 == 0, near, pltpu.roll(mz, 1, 1))
        total = -0.5 * (xp - xm + (yp - ym) + (zp - zm)) + rhs[16 * x : 16 * x + 16, :]
        sums = face_sums(L0, x, masks_0(x))[1][0:16, 0:128]
        B[0][x, 0:16, 0:128] = total * (OMEGA / sums)
    make_0(B[0], 1)
    ship_0(1, 5)
    coefficients(L0, 2)

    finish_1(K[1], 0, 3)
    coefficients(L1, 3)
    start_2(finish_2z(0, 4), 0, 6)
    for p in range(4):
        K[2][p, 0:4, :] = full_2[0, 4 * p : 4 * p + 4, :]
    restrict_2(lambda x: K[2][x, 0:8, :], 0)
    start_3y(0, 7)

    finish_0(B[0], 1, 5)
    sweep(L0, B[0], VA[0], 2)

    blocks = restrict_0(lambda x: residual(L0, VA[0], x)[0:16, 0:128])
    for p, block in enumerate(blocks):
        B[1][p, 0:8, :] = block * IW[1][p, 0:8, :]
    start_1(B[1], 1, 8)
    finish_2(K[2], 0, 6)
    coefficients(L2, 3)
    finish_3y(0, 7)
    start_3x(0, 9)

    finish_1(B[1], 1, 8)
    sweep(L1, B[1], VA[1], 3)
    restrict_1(lambda x: residual(L1, VA[1], x)[0:8, :], 1)
    start_2z(1, 10)
    finish_3x(K[3], 0, 9)
    coefficients(L3, 8)

    whole = finish_2z(1, 10)
    for p in range(4):
        B[2][p, 0:4, :] = whole[4 * p : 4 * p + 4, :] * IW[2][p, 0:4, :]
        full_2[1, 4 * p : 4 * p + 4, :] = B[2][p, 0:4, :]
    start_2(full_2[1], 1, 11)
    finish_2(B[2], 1, 11, own=False)
    sweep(L2, B[2], VA[2], 3)
    restrict_2(lambda x: residual(L2, VA[2], x)[0:8, :], 1)
    own_rows = pack_3[1]
    low = IW[3][0, 0:2, :]
    high = pltpu.roll(IW[3][1], 64, 1)[0:2, :]
    pack_3[1] = own_rows * jnp.where(lax.broadcasted_iota(jnp.int32, (2, 128), 1) < 64, low, high)
    start_3y(1, 12)
    for p in range(4):
        full_2[2, 4 * p : 4 * p + 4, :] = VA[2][p, 0:4, :]
    start_2(full_2[2], 2, 13)

    finish_3y(1, 12)
    start_3x(1, 14)
    finish_2(VA[2], 2, 13, own=False)
    finish_3x(B[3], 1, 14)
    now, other = B[3], VA[3]
    for halo in range(8, 1, -1):
        sweep(L3, now, other, halo)
        now, other = other, VB[3] if other is VA[3] else VA[3]

    up_2 = eye((128, 128), lambda r, c: as_mat(r == half(c)))
    prolong(L2, L3, 4, now, VA[2], tall_2, up_2, lambda r: wrap(half(jnp.where(r < 8, r, r - 16)), 24))
    sweep(L2, VA[2], VB[2], 3)
    sweep(L2, VB[2], VA[2], 2)
    up_1 = eye((128, 128), lambda r, c: as_mat(r == wrap(half(jnp.where(c < 96, c, c - 128)) + 32 * me[2], 128)))
    prolong(L1, L2, 3, VA[2], VA[1], tall_3, up_1, lambda r: wrap(half(jnp.where(r < 12, r, r - 16)), 16))
    sweep(L1, VA[1], VB[1], 2)
    sweep(L1, VB[1], VA[1], 1)
    up_0 = eye((128, 256), lambda r, c: as_mat(r == wrap(half(jnp.where(c < 192, c, c - 256)), 128)))
    prolong(L0, L1, 2, VA[1], VA[0], tall_4, up_0, lambda r: wrap(half(jnp.where(r < 20, r, r - 24)), 16))
    sweep(L0, VA[0], VB[0], 1)

    for x in range(16):
        v, acc = gathered(L0, VB[0], x)
        out_ref[x] = ((1.0 - OMEGA) * v + acc)[0:16, 0:128]

    sent(rec.at[pl.ds(1, 3)], 0)
    sent(mom_in, 1)
    for i, n in ((0, 2), (1, 5)):
        sent(land_0.at[i], n)
    for i, n in ((0, 3), (1, 8)):
        sent(land_1.at[i], n)
    for i, n in ((0, 4), (1, 10)):
        sent(land_2z.at[i], n)
    for i, n in ((0, 6), (1, 11), (2, 13)):
        sent(land_2.at[i], n)
    for i, n in ((0, 7), (1, 12)):
        sent(land_3y.at[i], n)
    for i, n in ((0, 9), (1, 14)):
        sent(land_3x.at[i], n)


def scratch(shape):
    out = []
    for lv in LEVELS:
        out += [pltpu.VMEM(lv.size, F32)] * 6 + [pltpu.VMEM((6,) + lv.size, F32)]
    nz = shape[2]
    out += [
        pltpu.VMEM((nz, 24, 128), F32), pltpu.VMEM((6, 16, 128), F32), pltpu.VMEM((6, 16, 128), F32),
        pltpu.VMEM((256, 1024), BF16), pltpu.VMEM((384, 1024), BF16), pltpu.VMEM((256, 128), F32),
        pltpu.VMEM((2, 32, 8, 128), F32), pltpu.VMEM((2, TILES_0, 8, 128), F32),
        pltpu.VMEM((2, 8, 8, 128), F32), pltpu.VMEM((2, TILES_1, 8, 128), F32),
        pltpu.VMEM((2, 16, 128), F32), pltpu.VMEM((2, nz - 1, 16, 128), F32),
        pltpu.VMEM((3, 16, 128), F32), pltpu.VMEM((3, 8, 16, 128), F32),
        pltpu.VMEM((2, 2, 128), F32), pltpu.VMEM((2, 2 * REACH, 2, 128), F32),
        pltpu.VMEM((2, 24, 128), F32), pltpu.VMEM((2, 2 * REACH, 24, 128), F32),
        pltpu.VMEM((128, 128), F32), pltpu.VMEM((32, 128), F32),
        pltpu.VMEM((144, 128), F32), pltpu.VMEM((128, 128), F32),
        pltpu.VMEM((160, 128), F32),
        pltpu.VMEM((16, 16, 128), F32), pltpu.VMEM((3, 16, 16, 128), F32),
        pltpu.VMEM((2, 8, 128), jnp.int32), pltpu.VMEM((8, 128), F32),
        pltpu.SemaphoreType.DMA((15,)), pltpu.SemaphoreType.DMA((15,)), pltpu.SemaphoreType.DMA((5,)),
    ]
    return out


def per_device(shape, chi, inducing, record_dest, record_cell, record_value):
    vmem = pl.BlockSpec(memory_space=pltpu.VMEM)
    return pl.pallas_call(
        functools.partial(kernel, shape),
        out_shape=jax.ShapeDtypeStruct((16, 16, 128), F32),
        in_specs=[pl.BlockSpec(memory_space=pltpu.HBM)] * 5,
        out_specs=vmem,
        scratch_shapes=scratch(shape),
        compiler_params=pltpu.CompilerParams(
            collective_id=0, has_side_effects=True, vmem_limit_bytes=40 * 1024 * 1024
        ),
        name="cycle",
    )(chi, inducing, record_dest.reshape(8, 128), record_cell.reshape(8, 128), record_value.reshape(8, 128))


def solution(mesh):
    shape = tuple(mesh.shape[a] for a in ("gx", "gy", "gz"))
    placed = (
        P("gx", "gy", "gz"),
        P(None, "gx", "gy", "gz"),
        P("gx", "gy", "gz", None, None),
        P("gx", "gy", "gz", None),
        P("gx", "gy", "gz", None),
    )
    return jax.shard_map(
        functools.partial(per_device, shape), mesh=mesh, in_specs=placed, out_specs=P("gx", "gy", "gz"), check_vma=False
    )
```

```python
import functools
import itertools

import jax
import jax.numpy as jnp
from jax import lax
from jax.experimental import pallas as pl
from jax.experimental.pallas import tpu as pltpu
from jax.sharding import PartitionSpec as P

OMEGA = 0.8
F32 = jnp.float32
BF16 = jnp.bfloat16
MESH = pl.DeviceIdType.MESH
BOX = [d for d in itertools.product((-1, 0, 1), repeat=3) if d != (0, 0, 0)]
BOX.sort(key=lambda d: -sum(map(abs, d)))
BOX2 = [d for d in itertools.product((-1, 0, 1), repeat=2) if d != (0, 0)]
REACH = 5
FAR = 15


class Level:
    def __init__(self, index, own, size, split, total):
        self.index, self.own, self.size, self.split, self.total = index, own, size, split, total
        self.scale = 0.25**index


L0 = Level(0, (16, 16, 128), (22, 24, 256), (19, 20, 192), (256, 192, 512))
L1 = Level(1, (8, 8, 64), (16, 16, 128), (12, 12, 96), (128, 96, 256))
L2 = Level(2, (4, 4, 0), (12, 16, 128), (8, 8, 128), (64, 48, 128))
L3 = Level(3, (2, 2, 0), (22, 24, 128), (12, 24, 128), (32, 24, 64))
LEVELS = (L0, L1, L2, L3)


def tiles_0(d):
    if d[2] == 0:
        if d[1] == 0:
            return 6
        return 8 if d[0] == 0 else 2
    return 2 if d[1] == 0 else 1


def tiles_1(d):
    if d[2] == 0:
        return 4 if d[0] == 0 else 2
    return 2 if d[0] == 0 else 1


def slots(count_of):
    table, at = {}, 0
    for d in BOX:
        table[d] = (at, count_of(d))
        at += count_of(d)
    return table, at


SLOT_0, TILES_0 = slots(tiles_0)
SLOT_1, TILES_1 = slots(tiles_1)


def peers(shape):
    nx, ny, nz = shape
    out = [tuple(d) for d in BOX]
    out += [(0, 0, k) for k in range(2, nz - 1)]
    out += [(0, k, 0) for k in range(-REACH, REACH + 1) if abs(k) > 1]
    out += [(k, 0, 0) for k in range(-REACH, REACH + 1) if abs(k) > 1]
    return out


def split3(x):
    hi = x.astype(BF16)
    rest = x - hi.astype(F32)
    mid = rest.astype(BF16)
    low = (rest - mid.astype(F32)).astype(BF16)
    return hi, mid, low


def right(x, mat):
    parts = [jnp.dot(p, mat, preferred_element_type=F32) for p in split3(x)]
    return parts[0] + parts[1] + parts[2]


def left(mat, x):
    parts = [jnp.dot(mat, p, preferred_element_type=F32) for p in split3(x)]
    return parts[0] + parts[1] + parts[2]


def wrap(at, size):
    return jnp.where(at < 0, at + size, jnp.where(at >= size, at - size, at))


def kernel(shape, chi_hbm, ind_hbm, dest_hbm, cell_hbm, val_hbm, out_ref, *refs):
    it = iter(refs)
    take = lambda n: [next(it) for _ in range(n)]
    K, B, VA, VB, IW, DW = [], [], [], [], [], []
    C = []
    for _ in LEVELS:
        k, b, va, vb, iw, dw, c = take(7)
        K.append(k), B.append(b), VA.append(va), VB.append(vb), IW.append(iw), DW.append(dw), C.append(c)
    rec, mom_out, mom_in, hot, val_hot, rhs = take(6)
    pack_0, land_0, pack_1, land_1 = take(4)
    pack_2, land_2z, full_2, land_2 = take(4)
    pack_3, land_3y, col_3, land_3x = take(4)
    tall_0, tall_1, tall_2, tall_3, tall_4 = take(5)
    chi, ind, rec_in, val_in = take(4)
    send_sem, recv_sem, load_sem = take(3)

    me = [lax.axis_index(a) for a in ("gx", "gy", "gz")]

    known = {}

    def along(i, o):
        if (i, o) not in known:
            known[i, o] = wrap(me[i] + o, shape[i]) if o else me[i]
        return known[i, o]

    def device(o):
        return tuple(along(i, o[i]) for i in range(3))

    barrier = pltpu.get_barrier_semaphore()
    all_peers = peers(shape)
    for o in all_peers:
        pl.semaphore_signal(barrier, inc=1, device_id=device(o), device_id_type=MESH)

    copies = [
        pltpu.make_async_copy(src, dst, load_sem.at[j])
        for j, (src, dst) in enumerate([
            (chi_hbm, chi), (ind_hbm, ind), (dest_hbm, rec_in.at[0]), (cell_hbm, rec_in.at[1]), (val_hbm, val_in),
        ])
    ]
    for j in (2, 3, 4, 0, 1):
        copies[j].start()

    sub = lax.broadcasted_iota(jnp.int32, (8, 128), 0)
    lane = lax.broadcasted_iota(jnp.int32, (8, 128), 1)
    lane16 = lax.broadcasted_iota(jnp.int32, (16, 128), 1)

    def send(src, dst, o, n):
        pltpu.make_async_remote_copy(
            src_ref=src, dst_ref=dst, send_sem=send_sem.at[n], recv_sem=recv_sem.at[n],
            device_id=device(o), device_id_type=MESH,
        ).start()

    def arrive(ref, n):
        pltpu.make_async_copy(ref, ref, recv_sem.at[n]).wait()

    def sent(ref, n):
        pltpu.make_async_copy(ref, ref, send_sem.at[n]).wait()

    def make_0(src, i):
        pack = pack_0.at[i]
        for p in range(3):
            for t in range(2):
                pack[2 * p + t] = src[13 + p, 8 * t : 8 * t + 8, 0:128]
                pack[6 + 2 * p + t] = src[p, 8 * t : 8 * t + 8, 0:128]
        for k in range(8):
            pack[12 + k] = jnp.where(sub >= 4, src[2 * k, 8:16, 0:128], pltpu.roll(src[2 * k + 1, 8:16, 0:128], 4, 0))
            pack[20 + k] = jnp.where(sub < 4, src[2 * k, 0:8, 0:128], pltpu.roll(src[2 * k + 1, 0:8, 0:128], 4, 0))
        up = jnp.zeros((16, 128), F32)
        down = jnp.zeros((16, 128), F32)
        for x in range(16):
            p = src[x, 0:16, 0:128]
            here = (lane16 >= 4 * x) & (lane16 < 4 * x + 4)
            up = jnp.where(here, pltpu.roll(p, (4 * x + 4) % 128, 1), up)
            down = jnp.where(here, pltpu.roll(p, 4 * x, 1) if x else p, down)
        for t in range(2):
            pack[28 + t] = up[8 * t : 8 * t + 8]
            pack[30 + t] = down[8 * t : 8 * t + 8]

    def ship_0(i, n):
        pack, land = pack_0.at[i], land_0.at[i]
        for d in BOX:
            to = n + FAR if 0 not in d else n
            at, count = SLOT_0[d]
            if d[2] == 0:
                if d[1] == 0:
                    first = 0 if d[0] == 1 else 6
                else:
                    first = (12 if d[1] == 1 else 20) + (6 if d[0] == 1 else 0)
            else:
                first = (28 if d[2] == 1 else 30) + (1 if d[1] == 1 else 0)
            send(pack.at[pl.ds(first, count)], land.at[pl.ds(at, count)], d, to)

    def finish_0(dst, i, n, corners):
        land = land_0.at[i]
        if corners:
            arrive(land.at[0:8], n + FAR)
        else:
            arrive(land.at[8:TILES_0], n)
        for xp in range(22):
            sx, px = (0, xp) if xp < 16 else (1, xp - 16) if xp < 19 else (-1, xp - 6)
            at = lambda y, z: SLOT_0[(-sx, -y, -z)][0]
            base = 6 if sx == -1 else 0
            if sx and not corners:
                row = px - 13 if sx == -1 else px
                dst[xp, 0:8, 0:128] = land[at(0, 0) + 2 * row]
                dst[xp, 8:16, 0:128] = land[at(0, 0) + 2 * row + 1]
            if not corners:
                k = px // 2 - base
                above, below = land[at(1, 0) + k], land[at(-1, 0) + k]
                if px % 2:
                    above, below = pltpu.roll(above, 4, 0), pltpu.roll(below, 4, 0)
                dst[xp, 16:24, 0:128] = jnp.where(sub < 4, above, below)
            for t in range(3):
                if corners != (sx != 0 and t == 2):
                    continue
                if t < 2:
                    a, b = land[at(0, 1) + t], land[at(0, -1) + t]
                else:
                    a = jnp.where(sub < 4, land[at(1, 1)], land[at(-1, 1)])
                    b = jnp.where(sub < 4, land[at(1, -1)], land[at(-1, -1)])
                a = pltpu.roll(a, (128 - 4 * px) % 128, 1) if px else a
                b = pltpu.roll(b, 124 - 4 * px, 1)
                dst[xp, 8 * t : 8 * t + 8, 128:256] = jnp.where(lane < 64, a, b)

    def start_1(src, i, n):
        pack, land = pack_1.at[i], land_1.at[i]
        for k in range(4):
            pack[k] = jnp.where(lane < 64, src[2 * k, 0:8, :], pltpu.roll(src[2 * k + 1, 0:8, :], 64, 1))
        for t in range(2):
            up = jnp.zeros((8, 128), F32)
            down = jnp.zeros((8, 128), F32)
            for j in range(4):
                p = src[4 * t + j, 0:8, :]
                here = (lane >= 32 * j) & (lane < 32 * j + 32)
                up = jnp.where(here, pltpu.roll(p, (32 * j + 96) % 128, 1) if j != 1 else p, up)
                down = jnp.where(here, pltpu.roll(p, 32 * j, 1) if j else p, down)
            pack[4 + t] = up
            pack[6 + t] = down
        for d in BOX:
            to = n + FAR if 0 not in d else n
            at, count = SLOT_1[d]
            if d[2] == 0:
                first = 2 if d[0] == 1 else 0
            else:
                first = (4 if d[2] == 1 else 6) + (1 if d[0] == 1 else 0)
            send(pack.at[pl.ds(first, count)], land.at[pl.ds(at, count)], d, to)

    def finish_1(dst, i, n, corners):
        land = land_1.at[i]
        if corners:
            arrive(land.at[0:8], n + FAR)
        else:
            arrive(land.at[8:TILES_1], n)
        for xp in range(16):
            sx, px = (0, xp) if xp < 8 else (1, xp - 8) if xp < 12 else (-1, xp - 8)
            half = 1 if sx == -1 else 0
            if corners and sx == 0:
                continue

            def piece(y, z):
                at = SLOT_1[(-sx, -y, -z)][0]
                return land[at + px // 2 - 2 * half] if z == 0 else land[at + px // 4 - half]

            def both(z):
                return jnp.where(sub < 4, piece(1, z), piece(-1, z))

            sa, sb = (64 - 32 * (px % 4)) % 128, 96 - 32 * (px % 4)

            def ends(a, b):
                a = pltpu.roll(a, sa, 1) if sa else a
                b = pltpu.roll(b, sb, 1) if sb else b
                return jnp.where(lane < 96, a, b)

            def middle(m):
                return pltpu.roll(m, 64, 1) if px % 2 else m

            if corners:
                dst[xp, 8:16, :] = jnp.where(lane < 64, dst[xp, 8:16, :], ends(both(1), both(-1)))
                continue
            m = middle(piece(0, 0)) if sx else dst[xp, 0:8, :]
            dst[xp, 0:8, :] = jnp.where(lane < 64, m, ends(piece(0, 1), piece(0, -1)))
            m = middle(both(0))
            dst[xp, 8:16, :] = m if sx else jnp.where(lane < 64, m, ends(both(1), both(-1)))

    def start_2z(i, n):
        for k in (2, 1, 3):
            send(pack_2.at[i], land_2z.at[i, k - 1], (0, 0, -k), n)

    def finish_2z(i, n):
        arrive(land_2z.at[i], n)
        whole = pack_2[i]
        for k in range(1, shape[2]):
            whole = whole + land_2z[i, k - 1]
        return whole

    def start_2(whole, i, n):
        full_2[i] = whole
        for j, d in enumerate(BOX2):
            send(full_2.at[i], land_2.at[i, j], (d[0], d[1], 0), n)

    def place_2(dst, block, sx, sy):
        x0 = 0 if sx == 0 else 4 if sx == 1 else 8
        y0 = 0 if sy == 0 else 4 if sy == 1 else 12
        for p in range(4):
            dst[x0 + p, y0 : y0 + 4, :] = block[4 * p : 4 * p + 4, :]

    def finish_2(dst, i, n, own=True):
        arrive(land_2.at[i], n)
        for j, d in enumerate(BOX2):
            place_2(dst, land_2[i, j], -d[0], -d[1])
        if own:
            place_2(dst, full_2[i], 0, 0)

    steps = sorted([k for k in range(-REACH, REACH + 1) if k], key=lambda k: -abs(k))

    def start_3y(i, n):
        for j, k in enumerate(steps):
            send(pack_3.at[i], land_3y.at[i, j], (0, -k, 0), n)

    def finish_3y(i, n):
        arrive(land_3y.at[i], n)
        col_3[i, 2 * REACH + 2 : 24 - 2 * REACH, :] = jnp.zeros((22 - 4 * REACH, 128), F32)
        col_3[i, 0:2, :] = pack_3[i]
        for j, k in enumerate(steps):
            row = (2 * k) % 24
            col_3[i, row : row + 2, :] = land_3y[i, j]

    def start_3x(i, n):
        for j, k in enumerate(steps):
            send(col_3.at[i], land_3x.at[i, j], (-k, 0, 0), n)

    def finish_3x(dst, i, n):
        arrive(land_3x.at[i], n)
        for k in range(-REACH, REACH + 1):
            pair = col_3[i] if k == 0 else land_3x[i, steps.index(k)]
            dst[(2 * k) % 22] = pair
            dst[(2 * k + 1) % 22] = pltpu.roll(pair, 64, 1)

    def around(ref, x, size):
        nx = size[0]
        v = ref[x]
        return v, (
            ref[(x + 1) % nx], ref[(x - 1) % nx],
            pltpu.roll(v, size[1] - 1, 0), pltpu.roll(v, 1, 0),
            pltpu.roll(v, size[2] - 1, 1), pltpu.roll(v, 1, 1),
        )

    def planes(lv, halo):
        return [r % lv.size[0] for r in range(-halo, lv.own[0] + halo)]

    def edge_masks(lv):
        X, Y, Z = lv.size
        rows = lax.broadcasted_iota(jnp.int32, (Y, Z), 0)
        lanes = lax.broadcasted_iota(jnp.int32, (Y, Z), 1)
        y = wrap(me[1] * lv.own[1] + jnp.where(rows < lv.split[1], rows, rows - Y), lv.total[1])
        z = wrap(me[2] * lv.own[2] + jnp.where(lanes < lv.split[2], lanes, lanes - Z), lv.total[2])
        sides = [
            jnp.where(y == lv.total[1] - 1, 0.0, 1.0), jnp.where(y == 0, 0.0, 1.0),
            jnp.where(z == lv.total[2] - 1, 0.0, 1.0), jnp.where(z == 0, 0.0, 1.0),
        ]

        def at(x):
            rel = x if x < lv.split[0] else x - X
            g = wrap(me[0] * lv.own[0] + rel, lv.total[0])
            return [jnp.where(g == lv.total[0] - 1, 0.0, 1.0), jnp.where(g == 0, 0.0, 1.0)] + sides

        return at

    def face_sums(lv, x, masks):
        k, near = around(K[lv.index], x, lv.size)
        c = [0.5 * (k + m * o) for m, o in zip(masks, near)]
        total = c[0] + c[1] + c[2] + c[3] + c[4] + c[5]
        return c, jnp.where(total > 0.5, total, 1.0)

    def coefficients(lv, halo):
        i = lv.index
        at = edge_masks(lv)
        for x in planes(lv, halo):
            masks = at(x)
            c, total = face_sums(lv, x, masks)
            inv = OMEGA / total
            for j in range(6):
                C[i][j, x] = c[j] * masks[j] * inv
            if x < lv.own[0]:
                IW[i][x] = inv * (1.0 / lv.scale)
                DW[i][x] = total * (lv.scale / OMEGA)

    def gathered(lv, src, x):
        i = lv.index
        v, near = around(src, x, lv.size)
        acc = B[i][x]
        for j in range(6):
            acc = acc + C[i][j, x] * near[j]
        return v, acc

    def sweep(lv, src, dst, halo):
        for x in planes(lv, halo):
            v, acc = gathered(lv, src, x)
            dst[x] = (1.0 - OMEGA) * v + acc

    def residual(lv, src, x):
        v, acc = gathered(lv, src, x)
        return (acc - OMEGA * v) * DW[lv.index][x]

    def eye(shape2, fn):
        r = lax.broadcasted_iota(jnp.int32, shape2, 0)
        c = lax.broadcasted_iota(jnp.int32, shape2, 1)
        return fn(r, c)

    def as_mat(cond, value=1.0):
        return jnp.where(cond, value, 0.0).astype(BF16)

    half = lambda a: lax.shift_right_arithmetic(a, 1)
    down_rows_0 = eye((8, 16), lambda r, c: as_mat(half(c) == r))
    down_rows = eye((8, 8), lambda r, c: as_mat((half(c) == r) & (r < 4)))
    down_lanes_0 = eye((128, 128), lambda r, c: as_mat(half(r) == c, 0.125))
    down_lanes_1 = eye((128, 128), lambda r, c: as_mat((half(r) + me[2] * 32 == c) & (r < 64), 0.125))
    down_lanes_2 = [
        eye((128, 128), lambda r, c: as_mat(half(r) + 64 * p == c, 0.125)) for p in range(2)
    ]

    def restrict_0(plane):
        for p in range(8):
            tall_0[16 * p : 16 * p + 16, :] = plane(2 * p) + plane(2 * p + 1)
        tall_0[...] = right(tall_0[...], down_lanes_0)
        return [left(down_rows_0, tall_0[16 * p : 16 * p + 16, :]) for p in range(8)]

    def restrict_1(plane, i):
        for p in range(4):
            tall_1[8 * p : 8 * p + 8, :] = plane(2 * p) + plane(2 * p + 1)
        tall_1[...] = right(tall_1[...], down_lanes_1)
        for p in range(4):
            pack_2[i, 4 * p : 4 * p + 4, :] = left(down_rows, tall_1[8 * p : 8 * p + 8, :])[0:4]

    def restrict_2(plane, i):
        both = right(plane(0) + plane(1), down_lanes_2[0]) + right(plane(2) + plane(3), down_lanes_2[1])
        pack_3[i] = left(down_rows, both)[0:2]

    def prolong(fine, coarse, halo, e_ref, v_ref, tall, lanes_mat, rows_of):
        XF, YF, ZF = fine.size
        XC, YC, ZC = coarse.size
        rows_mat = eye((YF, YC), lambda r, c: as_mat(rows_of(r) == c))
        todo = {}
        for rel in range(-halo, fine.own[0] + halo):
            todo.setdefault((rel // 2) % XC, []).append(rel % XF)
        for q, p in enumerate(todo):
            tall[YC * q : YC * q + YC, :] = e_ref[p]
        spread = right(tall[...], lanes_mat)
        for q, p in enumerate(todo):
            out = left(rows_mat, spread[YC * q : YC * q + YC])
            for x in todo[p]:
                v_ref[x] = v_ref[x] + out

    for copy in copies[2:]:
        copy.wait()
    rec[0, 0:8, :] = rec_in[0].astype(F32)
    rec[0, 8:16, :] = rec_in[1].astype(F32)
    rec[0, 16:24, :] = val_in[...]
    copies[0].wait()
    for x in range(16):
        K[0][x, 0:16, 0:128] = 1.0 + chi[x]
    make_0(K[0], 0)
    copies[1].wait()
    up = jnp.zeros((16, 128), F32)
    down = jnp.zeros((16, 128), F32)
    for x in range(16):
        mz = chi[x] * ind[2, x]
        up = jnp.where(lane16 == x, pltpu.roll(mz, (x + 1) % 128, 1), up)
        down = jnp.where(lane16 == x, pltpu.roll(mz, x, 1) if x else mz, down)
        my = chi[x] * ind[1, x]
        mom_out[2, x : x + 1, :] = my[15:16]
        mom_out[3, x : x + 1, :] = my[0:1]
    mom_out[0] = chi[15] * ind[0, 15]
    mom_out[1] = chi[0] * ind[0, 0]
    mom_out[4] = up
    mom_out[5] = down

    pl.semaphore_wait(barrier, len(all_peers))

    rec_order = sorted(range(1, shape[2]), key=lambda k: min(k, shape[2] - k))
    rec_sem = lambda k: (0, 33, 34)[k - 1]
    for k in reversed(rec_order):
        send(rec.at[0], rec.at[k], (0, 0, -k), rec_sem(k))
    FACES = [(1, 0, 0), (-1, 0, 0), (0, 1, 0), (0, -1, 0), (0, 0, 1), (0, 0, -1)]
    for j, d in enumerate(FACES):
        send(mom_out.at[j], mom_in.at[j], d, 1)
    ship_0(0, 2)

    for ref in (K[2], B[2]):
        for x in range(12):
            ref[x, 8:16, :] = jnp.zeros((8, 128), F32)
    for p, block in enumerate(restrict_0(lambda x: K[0][x, 0:16, 0:128])):
        K[1][p, 0:8, :] = block
    start_1(K[1], 0, 3)
    restrict_1(lambda x: K[1][x, 0:8, :], 0)
    start_2z(0, 4)

    rows256 = lax.broadcasted_iota(jnp.int32, (256, 128), 0).astype(F32)
    rows128 = lax.broadcasted_iota(jnp.int32, (128, 128), 0).astype(F32)
    mine = me[2].astype(F32)

    def deposit(s):
        to, cell = rec[s, 0:8, :], rec[s, 8:16, :]
        row = jnp.floor(cell * (1.0 / 128.0))
        col = cell - 128.0 * row
        row = jnp.where(to == mine, row, -1.0)
        parts = [p.astype(F32) for p in split3(rec[s, 16:24, :])]
        for j in range(8):
            hot[s % 2, :, 128 * j : 128 * j + 128] = jnp.where(rows256 == row[j : j + 1], 1.0, 0.0).astype(BF16)
            same = rows128 == col[j : j + 1]
            for q in range(3):
                val_hot[s % 2, 128 * q : 128 * q + 128, 128 * j : 128 * j + 128] = jnp.where(same, parts[q][j : j + 1], 0.0).astype(BF16)
        got = lax.dot_general(hot[s % 2], val_hot[s % 2], (((1,), (1,)), ((), ())), preferred_element_type=F32)
        return got[:, 0:128] + got[:, 128:256] + got[:, 256:384]

    rhs[...] = deposit(0)
    for k in rec_order:
        arrive(rec.at[k], rec_sem(k))
        rhs[...] = rhs[...] + deposit(k)

    finish_0(K[0], 0, 2, False)

    arrive(mom_in, 1)
    inside = [
        jnp.where(me[i] == edge, 0.0, 1.0) for i in range(3) for edge in (shape[i] - 1, 0)
    ]
    masks_0 = edge_masks(L0)
    row16 = lax.broadcasted_iota(jnp.int32, (16, 128), 0)
    for x in range(16):
        xp = chi[x + 1] * ind[0, x + 1] if x < 15 else mom_in[1] * inside[0]
        xm = chi[x - 1] * ind[0, x - 1] if x > 0 else mom_in[0] * inside[1]
        my = chi[x] * ind[1, x]
        yp = jnp.where(row16 == 15, mom_in[3, x : x + 1, :] * inside[2], pltpu.roll(my, 15, 0))
        ym = jnp.where(row16 == 0, mom_in[2, x : x + 1, :] * inside[3], pltpu.roll(my, 1, 0))
        mz = chi[x] * ind[2, x]
        far = pltpu.roll(mom_in[5] * inside[4], 127 - x, 1)
        near = mom_in[4] * inside[5]
        near = pltpu.roll(near, 128 - x, 1) if x else near
        zp = jnp.where(lane16 == 127, far, pltpu.roll(mz, 127, 1))
        zm = jnp.where(lane16 == 0, near, pltpu.roll(mz, 1, 1))
        total = -0.5 * (xp - xm + (yp - ym) + (zp - zm)) + rhs[16 * x : 16 * x + 16, :]
        sums = face_sums(L0, x, masks_0(x))[1][0:16, 0:128]
        B[0][x, 0:16, 0:128] = total * (OMEGA / sums)
    make_0(B[0], 1)
    ship_0(1, 5)
    finish_0(K[0], 0, 2, True)
    coefficients(L0, 2)

    finish_1(K[1], 0, 3, False)
    finish_1(K[1], 0, 3, True)
    coefficients(L1, 3)
    start_2(finish_2z(0, 4), 0, 6)
    for p in range(4):
        K[2][p, 0:4, :] = full_2[0, 4 * p : 4 * p + 4, :]
    restrict_2(lambda x: K[2][x, 0:8, :], 0)
    start_3y(0, 7)

    finish_0(B[0], 1, 5, False)
    sweep(L0, B[0], VA[0], 1)

    blocks = restrict_0(lambda x: residual(L0, VA[0], x)[0:16, 0:128])
    for p, block in enumerate(blocks):
        B[1][p, 0:8, :] = block * IW[1][p, 0:8, :]
    start_1(B[1], 1, 8)
    finish_0(B[0], 1, 5, True)
    sweep(L0, B[0], VA[0], 2)
    finish_2(K[2], 0, 6)
    coefficients(L2, 3)
    finish_3y(0, 7)
    start_3x(0, 9)

    finish_1(B[1], 1, 8, False)
    sweep(L1, B[1], VA[1], 1)
    restrict_1(lambda x: residual(L1, VA[1], x)[0:8, :], 1)
    start_2z(1, 10)
    finish_1(B[1], 1, 8, True)
    sweep(L1, B[1], VA[1], 3)
    finish_3x(K[3], 0, 9)
    coefficients(L3, 8)

    whole = finish_2z(1, 10)
    for p in range(4):
        B[2][p, 0:4, :] = whole[4 * p : 4 * p + 4, :] * IW[2][p, 0:4, :]
        full_2[1, 4 * p : 4 * p + 4, :] = B[2][p, 0:4, :]
    start_2(full_2[1], 1, 11)
    finish_2(B[2], 1, 11, own=False)
    sweep(L2, B[2], VA[2], 3)
    restrict_2(lambda x: residual(L2, VA[2], x)[0:8, :], 1)
    own_rows = pack_3[1]
    low = IW[3][0, 0:2, :]
    high = pltpu.roll(IW[3][1], 64, 1)[0:2, :]
    pack_3[1] = own_rows * jnp.where(lax.broadcasted_iota(jnp.int32, (2, 128), 1) < 64, low, high)
    start_3y(1, 12)
    for p in range(4):
        full_2[2, 4 * p : 4 * p + 4, :] = VA[2][p, 0:4, :]
    start_2(full_2[2], 2, 13)

    finish_3y(1, 12)
    start_3x(1, 14)
    finish_2(VA[2], 2, 13, own=False)
    finish_3x(B[3], 1, 14)
    now, other = B[3], VA[3]
    for halo in range(8, 1, -1):
        sweep(L3, now, other, halo)
        now, other = other, VB[3] if other is VA[3] else VA[3]

    up_2 = eye((128, 128), lambda r, c: as_mat(r == half(c)))
    prolong(L2, L3, 4, now, VA[2], tall_2, up_2, lambda r: wrap(half(jnp.where(r < 8, r, r - 16)), 24))
    sweep(L2, VA[2], VB[2], 3)
    sweep(L2, VB[2], VA[2], 2)
    up_1 = eye((128, 128), lambda r, c: as_mat(r == wrap(half(jnp.where(c < 96, c, c - 128)) + 32 * me[2], 128)))
    prolong(L1, L2, 3, VA[2], VA[1], tall_3, up_1, lambda r: wrap(half(jnp.where(r < 12, r, r - 16)), 16))
    sweep(L1, VA[1], VB[1], 2)
    sweep(L1, VB[1], VA[1], 1)
    up_0 = eye((128, 256), lambda r, c: as_mat(r == wrap(half(jnp.where(c < 192, c, c - 256)), 128)))
    prolong(L0, L1, 2, VA[1], VA[0], tall_4, up_0, lambda r: wrap(half(jnp.where(r < 20, r, r - 24)), 16))
    sweep(L0, VA[0], VB[0], 1)

    for x in range(16):
        v, acc = gathered(L0, VB[0], x)
        out_ref[x] = ((1.0 - OMEGA) * v + acc)[0:16, 0:128]

    for k in rec_order:
        sent(rec.at[k], rec_sem(k))
    sent(mom_in, 1)
    for i, n in ((0, 2), (1, 5)):
        sent(land_0.at[i, 8:TILES_0], n)
        sent(land_0.at[i, 0:8], n + FAR)
    for i, n in ((0, 3), (1, 8)):
        sent(land_1.at[i, 8:TILES_1], n)
        sent(land_1.at[i, 0:8], n + FAR)
    for i, n in ((0, 4), (1, 10)):
        sent(land_2z.at[i], n)
    for i, n in ((0, 6), (1, 11), (2, 13)):
        sent(land_2.at[i], n)
    for i, n in ((0, 7), (1, 12)):
        sent(land_3y.at[i], n)
    for i, n in ((0, 9), (1, 14)):
        sent(land_3x.at[i], n)


def scratch(shape):
    out = []
    for lv in LEVELS:
        out += [pltpu.VMEM(lv.size, F32)] * 6 + [pltpu.VMEM((6,) + lv.size, F32)]
    nz = shape[2]
    out += [
        pltpu.VMEM((nz, 24, 128), F32), pltpu.VMEM((6, 16, 128), F32), pltpu.VMEM((6, 16, 128), F32),
        pltpu.VMEM((2, 256, 1024), BF16), pltpu.VMEM((2, 384, 1024), BF16), pltpu.VMEM((256, 128), F32),
        pltpu.VMEM((2, 32, 8, 128), F32), pltpu.VMEM((2, TILES_0, 8, 128), F32),
        pltpu.VMEM((2, 8, 8, 128), F32), pltpu.VMEM((2, TILES_1, 8, 128), F32),
        pltpu.VMEM((2, 16, 128), F32), pltpu.VMEM((2, nz - 1, 16, 128), F32),
        pltpu.VMEM((3, 16, 128), F32), pltpu.VMEM((3, 8, 16, 128), F32),
        pltpu.VMEM((2, 2, 128), F32), pltpu.VMEM((2, 2 * REACH, 2, 128), F32),
        pltpu.VMEM((2, 24, 128), F32), pltpu.VMEM((2, 2 * REACH, 24, 128), F32),
        pltpu.VMEM((128, 128), F32), pltpu.VMEM((32, 128), F32),
        pltpu.VMEM((144, 128), F32), pltpu.VMEM((128, 128), F32),
        pltpu.VMEM((160, 128), F32),
        pltpu.VMEM((16, 16, 128), F32), pltpu.VMEM((3, 16, 16, 128), F32),
        pltpu.VMEM((2, 8, 128), jnp.int32), pltpu.VMEM((8, 128), F32),
        pltpu.SemaphoreType.DMA((35,)), pltpu.SemaphoreType.DMA((35,)), pltpu.SemaphoreType.DMA((5,)),
    ]
    return out


def per_device(shape, chi, inducing, record_dest, record_cell, record_value):
    vmem = pl.BlockSpec(memory_space=pltpu.VMEM)
    return pl.pallas_call(
        functools.partial(kernel, shape),
        out_shape=jax.ShapeDtypeStruct((16, 16, 128), F32),
        in_specs=[pl.BlockSpec(memory_space=pltpu.HBM)] * 5,
        out_specs=vmem,
        scratch_shapes=scratch(shape),
        compiler_params=pltpu.CompilerParams(
            collective_id=0, has_side_effects=True, vmem_limit_bytes=60 * 1024 * 1024
        ),
        name="cycle",
    )(chi, inducing, record_dest.reshape(8, 128), record_cell.reshape(8, 128), record_value.reshape(8, 128))


def solution(mesh):
    shape = tuple(mesh.shape[a] for a in ("gx", "gy", "gz"))
    placed = (
        P("gx", "gy", "gz"),
        P(None, "gx", "gy", "gz"),
        P("gx", "gy", "gz", None, None),
        P("gx", "gy", "gz", None),
        P("gx", "gy", "gz", None),
    )
    return jax.shard_map(
        functools.partial(per_device, shape), mesh=mesh, in_specs=placed, out_specs=P("gx", "gy", "gz"), check_vma=False
    )
```

```python
import functools
import itertools

import jax
import jax.numpy as jnp
from jax import lax
from jax.experimental import pallas as pl
from jax.experimental.pallas import tpu as pltpu
from jax.sharding import PartitionSpec as P

OMEGA = 0.8
F32 = jnp.float32
BF16 = jnp.bfloat16
MESH = pl.DeviceIdType.MESH
BOX = [d for d in itertools.product((-1, 0, 1), repeat=3) if d != (0, 0, 0)]
BOX.sort(key=lambda d: -sum(map(abs, d)))
BOX2 = [d for d in itertools.product((-1, 0, 1), repeat=2) if d != (0, 0)]
REACH = 5
FAR = 15


class Level:
    def __init__(self, index, own, size, split, total):
        self.index, self.own, self.size, self.split, self.total = index, own, size, split, total
        self.scale = 0.25**index


L0 = Level(0, (16, 16, 128), (22, 24, 256), (19, 20, 192), (256, 192, 512))
L1 = Level(1, (8, 8, 64), (16, 16, 128), (12, 12, 96), (128, 96, 256))
L2 = Level(2, (4, 4, 32), (12, 16, 128), (8, 8, 128), (64, 48, 128))
L3 = Level(3, (2, 2, 16), (22, 24, 128), (12, 24, 64), (32, 24, 64))
LEVELS = (L0, L1, L2, L3)


def tiles_0(d):
    if d[2] == 0:
        if d[1] == 0:
            return 6
        return 8 if d[0] == 0 else 2
    return 2 if d[1] == 0 else 1


def tiles_1(d):
    if d[2] == 0:
        return 4 if d[0] == 0 else 2
    return 2 if d[0] == 0 else 1


def slots(count_of):
    table, at = {}, 0
    for d in BOX:
        table[d] = (at, count_of(d))
        at += count_of(d)
    return table, at


SLOT_0, TILES_0 = slots(tiles_0)
SLOT_1, TILES_1 = slots(tiles_1)


def peers(shape):
    nx, ny, nz = shape
    out = [tuple(d) for d in BOX]
    out += [(x, y, k) for x in (-1, 0, 1) for y in (-1, 0, 1) for k in range(2, nz - 1)]
    out += [(0, k, 0) for k in range(-REACH, REACH + 1) if abs(k) > 1]
    out += [(k, 0, 0) for k in range(-REACH, REACH + 1) if abs(k) > 1]
    return out


def split3(x):
    hi = x.astype(BF16)
    rest = x - hi.astype(F32)
    mid = rest.astype(BF16)
    low = (rest - mid.astype(F32)).astype(BF16)
    return hi, mid, low


def right(x, mat):
    parts = [jnp.dot(p, mat, preferred_element_type=F32) for p in split3(x)]
    return parts[0] + parts[1] + parts[2]


def left(mat, x):
    parts = [jnp.dot(mat, p, preferred_element_type=F32) for p in split3(x)]
    return parts[0] + parts[1] + parts[2]


def wrap(at, size):
    return jnp.where(at < 0, at + size, jnp.where(at >= size, at - size, at))


def kernel(shape, chi_hbm, ind_hbm, dest_hbm, cell_hbm, val_hbm, out_ref, *refs):
    it = iter(refs)
    take = lambda n: [next(it) for _ in range(n)]
    K, B, VA, VB, IW, DW = [], [], [], [], [], []
    C = []
    for _ in LEVELS:
        k, b, va, vb, iw, dw, c = take(7)
        K.append(k), B.append(b), VA.append(va), VB.append(vb), IW.append(iw), DW.append(dw), C.append(c)
    rec, mom_out, mom_in, hot, val_hot, rhs = take(6)
    pack_0, land_0, pack_1, land_1 = take(4)
    pack_2, land_2z, full_2, land_2 = take(4)
    pack_3, land_3y, col_3, land_3x = take(4)
    tall_0, tall_1, tall_2, tall_3, tall_4 = take(5)
    chi, ind, rec_in, val_in = take(4)
    send_sem, recv_sem, load_sem = take(3)

    me = [lax.axis_index(a) for a in ("gx", "gy", "gz")]

    known = {}

    def along(i, o):
        if (i, o) not in known:
            known[i, o] = wrap(me[i] + o, shape[i]) if o else me[i]
        return known[i, o]

    def device(o):
        return tuple(along(i, o[i]) for i in range(3))

    barrier = pltpu.get_barrier_semaphore()
    all_peers = peers(shape)
    for o in all_peers:
        pl.semaphore_signal(barrier, inc=1, device_id=device(o), device_id_type=MESH)

    copies = [
        pltpu.make_async_copy(src, dst, load_sem.at[j])
        for j, (src, dst) in enumerate([
            (chi_hbm, chi), (ind_hbm, ind), (dest_hbm, rec_in.at[0]), (cell_hbm, rec_in.at[1]), (val_hbm, val_in),
        ])
    ]
    for j in (2, 3, 4, 0, 1):
        copies[j].start()

    sub = lax.broadcasted_iota(jnp.int32, (8, 128), 0)
    lane = lax.broadcasted_iota(jnp.int32, (8, 128), 1)
    lane24 = lax.broadcasted_iota(jnp.int32, (24, 128), 1)
    lane16 = lax.broadcasted_iota(jnp.int32, (16, 128), 1)

    def send(src, dst, o, n):
        pltpu.make_async_remote_copy(
            src_ref=src, dst_ref=dst, send_sem=send_sem.at[n], recv_sem=recv_sem.at[n],
            device_id=device(o), device_id_type=MESH,
        ).start()

    def arrive(ref, n):
        pltpu.make_async_copy(ref, ref, recv_sem.at[n]).wait()

    def sent(ref, n):
        pltpu.make_async_copy(ref, ref, send_sem.at[n]).wait()

    def make_0(src, i):
        pack = pack_0.at[i]
        for p in range(3):
            for t in range(2):
                pack[2 * p + t] = src[13 + p, 8 * t : 8 * t + 8, 0:128]
                pack[6 + 2 * p + t] = src[p, 8 * t : 8 * t + 8, 0:128]
        for k in range(8):
            pack[12 + k] = jnp.where(sub >= 4, src[2 * k, 8:16, 0:128], pltpu.roll(src[2 * k + 1, 8:16, 0:128], 4, 0))
            pack[20 + k] = jnp.where(sub < 4, src[2 * k, 0:8, 0:128], pltpu.roll(src[2 * k + 1, 0:8, 0:128], 4, 0))
        up = jnp.zeros((16, 128), F32)
        down = jnp.zeros((16, 128), F32)
        for x in range(16):
            p = src[x, 0:16, 0:128]
            here = (lane16 >= 4 * x) & (lane16 < 4 * x + 4)
            up = jnp.where(here, pltpu.roll(p, (4 * x + 4) % 128, 1), up)
            down = jnp.where(here, pltpu.roll(p, 4 * x, 1) if x else p, down)
        for t in range(2):
            pack[28 + t] = up[8 * t : 8 * t + 8]
            pack[30 + t] = down[8 * t : 8 * t + 8]

    def ship_0(i, n):
        pack, land = pack_0.at[i], land_0.at[i]
        for d in BOX:
            to = n + FAR if 0 not in d else n
            at, count = SLOT_0[d]
            if d[2] == 0:
                if d[1] == 0:
                    first = 0 if d[0] == 1 else 6
                else:
                    first = (12 if d[1] == 1 else 20) + (6 if d[0] == 1 else 0)
            else:
                first = (28 if d[2] == 1 else 30) + (1 if d[1] == 1 else 0)
            send(pack.at[pl.ds(first, count)], land.at[pl.ds(at, count)], d, to)

    def finish_0(dst, i, n, corners):
        land = land_0.at[i]
        if corners:
            arrive(land.at[0:8], n + FAR)
        else:
            arrive(land.at[8:TILES_0], n)
        for xp in range(22):
            sx, px = (0, xp) if xp < 16 else (1, xp - 16) if xp < 19 else (-1, xp - 6)
            at = lambda y, z: SLOT_0[(-sx, -y, -z)][0]
            base = 6 if sx == -1 else 0
            if sx and not corners:
                row = px - 13 if sx == -1 else px
                dst[xp, 0:8, 0:128] = land[at(0, 0) + 2 * row]
                dst[xp, 8:16, 0:128] = land[at(0, 0) + 2 * row + 1]
            if not corners:
                k = px // 2 - base
                above, below = land[at(1, 0) + k], land[at(-1, 0) + k]
                if px % 2:
                    above, below = pltpu.roll(above, 4, 0), pltpu.roll(below, 4, 0)
                dst[xp, 16:24, 0:128] = jnp.where(sub < 4, above, below)
            for t in range(3):
                if corners != (sx != 0 and t == 2):
                    continue
                if t < 2:
                    a, b = land[at(0, 1) + t], land[at(0, -1) + t]
                else:
                    a = jnp.where(sub < 4, land[at(1, 1)], land[at(-1, 1)])
                    b = jnp.where(sub < 4, land[at(1, -1)], land[at(-1, -1)])
                a = pltpu.roll(a, (128 - 4 * px) % 128, 1) if px else a
                b = pltpu.roll(b, 124 - 4 * px, 1)
                dst[xp, 8 * t : 8 * t + 8, 128:256] = jnp.where(lane < 64, a, b)

    def start_1(src, i, n):
        pack, land = pack_1.at[i], land_1.at[i]
        for k in range(4):
            pack[k] = jnp.where(lane < 64, src[2 * k, 0:8, :], pltpu.roll(src[2 * k + 1, 0:8, :], 64, 1))
        for t in range(2):
            up = jnp.zeros((8, 128), F32)
            down = jnp.zeros((8, 128), F32)
            for j in range(4):
                p = src[4 * t + j, 0:8, :]
                here = (lane >= 32 * j) & (lane < 32 * j + 32)
                up = jnp.where(here, pltpu.roll(p, (32 * j + 96) % 128, 1) if j != 1 else p, up)
                down = jnp.where(here, pltpu.roll(p, 32 * j, 1) if j else p, down)
            pack[4 + t] = up
            pack[6 + t] = down
        for d in BOX:
            to = n + FAR if 0 not in d else n
            at, count = SLOT_1[d]
            if d[2] == 0:
                first = 2 if d[0] == 1 else 0
            else:
                first = (4 if d[2] == 1 else 6) + (1 if d[0] == 1 else 0)
            send(pack.at[pl.ds(first, count)], land.at[pl.ds(at, count)], d, to)

    def finish_1(dst, i, n, corners):
        land = land_1.at[i]
        if corners:
            arrive(land.at[0:8], n + FAR)
        else:
            arrive(land.at[8:TILES_1], n)
        for xp in range(16):
            sx, px = (0, xp) if xp < 8 else (1, xp - 8) if xp < 12 else (-1, xp - 8)
            half = 1 if sx == -1 else 0
            if corners and sx == 0:
                continue

            def piece(y, z):
                at = SLOT_1[(-sx, -y, -z)][0]
                return land[at + px // 2 - 2 * half] if z == 0 else land[at + px // 4 - half]

            def both(z):
                return jnp.where(sub < 4, piece(1, z), piece(-1, z))

            sa, sb = (64 - 32 * (px % 4)) % 128, 96 - 32 * (px % 4)

            def ends(a, b):
                a = pltpu.roll(a, sa, 1) if sa else a
                b = pltpu.roll(b, sb, 1) if sb else b
                return jnp.where(lane < 96, a, b)

            def middle(m):
                return pltpu.roll(m, 64, 1) if px % 2 else m

            if corners:
                dst[xp, 8:16, :] = jnp.where(lane < 64, dst[xp, 8:16, :], ends(both(1), both(-1)))
                continue
            m = middle(piece(0, 0)) if sx else dst[xp, 0:8, :]
            dst[xp, 0:8, :] = jnp.where(lane < 64, m, ends(piece(0, 1), piece(0, -1)))
            m = middle(both(0))
            dst[xp, 8:16, :] = m if sx else jnp.where(lane < 64, m, ends(both(1), both(-1)))

    columns = [(x, y, z) for x in (-1, 0, 1) for y in (-1, 0, 1) for z in range(shape[2]) if (x, y, z) != (0, 0, 0)]
    columns.sort(key=lambda d: -(abs(d[0]) + abs(d[1]) + min(d[2], shape[2] - d[2])))

    def start_2z(i, n):
        for j, d in enumerate(columns):
            send(pack_2.at[i], land_2z.at[i, j], (d[0], d[1], -d[2]), n)

    lane4 = lax.broadcasted_iota(jnp.int32, (4, 128), 1)

    def pick(blocks):
        out = blocks[3]
        for g in (2, 1, 0):
            out = jnp.where(lane4 < 32 * (g + 1), blocks[g], out)
        return out

    def finish_2z(dst, i, n):
        arrive(land_2z.at[i], n)
        for sx in (-1, 0, 1):
            for sy in (-1, 0, 1):
                own = [
                    pack_2[i] if (sx, sy, z) == (0, 0, 0) else land_2z[i, columns.index((-sx, -sy, z))] for z in range(4)
                ]
                turned = []
                for k in range(4):
                    mixed = pick([own[(g + k) % 4] for g in range(4)])
                    turned.append(pltpu.roll(mixed, 32 * k, 1) if k else mixed)
                x0 = 0 if sx == 0 else 4 if sx == 1 else 8
                y0 = 0 if sy == 0 else 4 if sy == 1 else 12
                for p in range(4):
                    dst[x0 + p, y0 : y0 + 4, :] = pick([turned[(z - p) % 4] for z in range(4)])

    def start_2(n):
        for j, d in enumerate(BOX2):
            send(full_2, land_2.at[j], (d[0], d[1], 0), n)

    def finish_2(dst, n):
        arrive(land_2, n)
        for j, d in enumerate(BOX2):
            x0 = 0 if d[0] == 0 else 4 if d[0] == -1 else 8
            y0 = 0 if d[1] == 0 else 4 if d[1] == -1 else 12
            for p in range(4):
                dst[x0 + p, y0 : y0 + 4, :] = land_2[j, 4 * p : 4 * p + 4, :]

    steps = sorted([k for k in range(-REACH, REACH + 1) if k], key=lambda k: -abs(k))

    def start_3y(i, n):
        for j, k in enumerate(steps):
            send(pack_3.at[i], land_3y.at[i, j], (0, -k, 0), n)

    def finish_3y(i, n):
        arrive(land_3y.at[i], n)
        col_3[i, 2 * REACH + 2 : 24 - 2 * REACH, :] = jnp.zeros((22 - 4 * REACH, 128), F32)
        col_3[i, 0:2, :] = pack_3[i]
        for j, k in enumerate(steps):
            row = (2 * k) % 24
            col_3[i, row : row + 2, :] = land_3y[i, j]

    def start_3x(i, n):
        for j, k in enumerate(steps):
            send(col_3.at[i], land_3x.at[i, j], (-k, 0, 0), n)

    def finish_3x(dst, i, n):
        arrive(land_3x.at[i], n)
        for k in range(-REACH, REACH + 1):
            pair = col_3[i] if k == 0 else land_3x[i, steps.index(k)]
            other = pltpu.roll(pair, 64, 1)
            dst[(2 * k) % 22] = jnp.where(lane24 < 64, pair, other)
            dst[(2 * k + 1) % 22] = jnp.where(lane24 < 64, other, pair)

    def around(ref, x, size):
        nx = size[0]
        v = ref[x]
        return v, (
            ref[(x + 1) % nx], ref[(x - 1) % nx],
            pltpu.roll(v, size[1] - 1, 0), pltpu.roll(v, 1, 0),
            pltpu.roll(v, size[2] - 1, 1), pltpu.roll(v, 1, 1),
        )

    def planes(lv, halo):
        return [r % lv.size[0] for r in range(-halo, lv.own[0] + halo)]

    def edge_masks(lv):
        X, Y, Z = lv.size
        rows = lax.broadcasted_iota(jnp.int32, (Y, Z), 0)
        lanes = lax.broadcasted_iota(jnp.int32, (Y, Z), 1)
        y = wrap(me[1] * lv.own[1] + jnp.where(rows < lv.split[1], rows, rows - Y), lv.total[1])
        z = wrap(me[2] * lv.own[2] + jnp.where(lanes < lv.split[2], lanes, lanes - Z), lv.total[2])
        sides = [
            jnp.where(y == lv.total[1] - 1, 0.0, 1.0), jnp.where(y == 0, 0.0, 1.0),
            jnp.where(z == lv.total[2] - 1, 0.0, 1.0), jnp.where(z == 0, 0.0, 1.0),
        ]

        def at(x):
            rel = x if x < lv.split[0] else x - X
            g = wrap(me[0] * lv.own[0] + rel, lv.total[0])
            return [jnp.where(g == lv.total[0] - 1, 0.0, 1.0), jnp.where(g == 0, 0.0, 1.0)] + sides

        return at

    def face_sums(lv, x, masks):
        k, near = around(K[lv.index], x, lv.size)
        c = [0.5 * (k + m * o) for m, o in zip(masks, near)]
        total = c[0] + c[1] + c[2] + c[3] + c[4] + c[5]
        return c, jnp.where(total > 0.5, total, 1.0)

    def coefficients(lv, halo):
        i = lv.index
        at = edge_masks(lv)
        for x in planes(lv, halo):
            masks = at(x)
            c, total = face_sums(lv, x, masks)
            inv = OMEGA / total
            for j in range(6):
                C[i][j, x] = c[j] * masks[j] * inv
            if x < lv.own[0]:
                IW[i][x] = inv * (1.0 / lv.scale)
                DW[i][x] = total * (lv.scale / OMEGA)

    def gathered(lv, src, x):
        i = lv.index
        v, near = around(src, x, lv.size)
        acc = B[i][x]
        for j in range(6):
            acc = acc + C[i][j, x] * near[j]
        return v, acc

    def sweep(lv, src, dst, halo):
        for x in planes(lv, halo):
            v, acc = gathered(lv, src, x)
            dst[x] = (1.0 - OMEGA) * v + acc

    def residual(lv, src, x):
        v, acc = gathered(lv, src, x)
        return (acc - OMEGA * v) * DW[lv.index][x]

    def eye(shape2, fn):
        r = lax.broadcasted_iota(jnp.int32, shape2, 0)
        c = lax.broadcasted_iota(jnp.int32, shape2, 1)
        return fn(r, c)

    def as_mat(cond, value=1.0):
        return jnp.where(cond, value, 0.0).astype(BF16)

    half = lambda a: lax.shift_right_arithmetic(a, 1)
    down_rows_0 = eye((8, 16), lambda r, c: as_mat(half(c) == r))
    down_rows = eye((8, 8), lambda r, c: as_mat((half(c) == r) & (r < 4)))
    down_lanes_0 = eye((128, 128), lambda r, c: as_mat(half(r) == c, 0.125))
    down_lanes_1 = eye((128, 128), lambda r, c: as_mat((half(r) == c) & (r < 64), 0.125))
    down_lanes_2 = [
        eye((128, 128), lambda r, c: as_mat(half(r) + 64 * p == c, 0.125)) for p in range(2)
    ]

    def restrict_0(plane):
        for p in range(8):
            tall_0[16 * p : 16 * p + 16, :] = plane(2 * p) + plane(2 * p + 1)
        tall_0[...] = right(tall_0[...], down_lanes_0)
        return [left(down_rows_0, tall_0[16 * p : 16 * p + 16, :]) for p in range(8)]

    def restrict_1(plane):
        for p in range(4):
            tall_1[8 * p : 8 * p + 8, :] = plane(2 * p) + plane(2 * p + 1)
        part = right(tall_1[...], down_lanes_1)
        whole = part[0:8]
        for p in range(1, 4):
            whole = whole + pltpu.roll(part[8 * p : 8 * p + 8], 32 * p, 1)
        return left(down_rows, whole)[0:4]

    def restrict_2(plane, i):
        both = right(plane(0) + plane(1), down_lanes_2[0]) + right(plane(2) + plane(3), down_lanes_2[1])
        pack_3[i] = left(down_rows, both)[0:2]

    def prolong(fine, coarse, halo, e_ref, v_ref, tall, lanes_mat, rows_of):
        XF, YF, ZF = fine.size
        XC, YC, ZC = coarse.size
        rows_mat = eye((YF, YC), lambda r, c: as_mat(rows_of(r) == c))
        todo = {}
        for rel in range(-halo, fine.own[0] + halo):
            todo.setdefault((rel // 2) % XC, []).append(rel % XF)
        for q, p in enumerate(todo):
            tall[YC * q : YC * q + YC, :] = e_ref[p]
        spread = right(tall[...], lanes_mat)
        for q, p in enumerate(todo):
            out = left(rows_mat, spread[YC * q : YC * q + YC])
            for x in todo[p]:
                v_ref[x] = v_ref[x] + out

    for copy in copies[2:]:
        copy.wait()
    rec[0, 0:8, :] = rec_in[0].astype(F32)
    rec[0, 8:16, :] = rec_in[1].astype(F32)
    rec[0, 16:24, :] = val_in[...]
    copies[0].wait()
    for x in range(16):
        K[0][x, 0:16, 0:128] = 1.0 + chi[x]
    make_0(K[0], 0)
    copies[1].wait()
    up = jnp.zeros((16, 128), F32)
    down = jnp.zeros((16, 128), F32)
    for x in range(16):
        mz = chi[x] * ind[2, x]
        up = jnp.where(lane16 == x, pltpu.roll(mz, (x + 1) % 128, 1), up)
        down = jnp.where(lane16 == x, pltpu.roll(mz, x, 1) if x else mz, down)
        my = chi[x] * ind[1, x]
        mom_out[2, x : x + 1, :] = my[15:16]
        mom_out[3, x : x + 1, :] = my[0:1]
    mom_out[0] = chi[15] * ind[0, 15]
    mom_out[1] = chi[0] * ind[0, 0]
    mom_out[4] = up
    mom_out[5] = down

    pl.semaphore_wait(barrier, len(all_peers))

    rec_order = sorted(range(1, shape[2]), key=lambda k: min(k, shape[2] - k))
    rec_sem = lambda k: (0, 33, 34)[k - 1]
    for k in reversed(rec_order):
        send(rec.at[0], rec.at[k], (0, 0, -k), rec_sem(k))
    FACES = [(1, 0, 0), (-1, 0, 0), (0, 1, 0), (0, -1, 0), (0, 0, 1), (0, 0, -1)]
    for j, d in enumerate(FACES):
        send(mom_out.at[j], mom_in.at[j], d, 1)
    ship_0(0, 2)

    for ref in (K[2], B[2]):
        for x in range(12):
            ref[x, 8:16, :] = jnp.zeros((8, 128), F32)
    for p, block in enumerate(restrict_0(lambda x: K[0][x, 0:16, 0:128])):
        K[1][p, 0:8, :] = block
    start_1(K[1], 0, 3)
    pack_2[0] = restrict_1(lambda x: K[1][x, 0:8, :])
    start_2z(0, 4)

    rows256 = lax.broadcasted_iota(jnp.int32, (256, 128), 0).astype(F32)
    rows128 = lax.broadcasted_iota(jnp.int32, (128, 128), 0).astype(F32)
    mine = me[2].astype(F32)

    def deposit(s):
        to, cell = rec[s, 0:8, :], rec[s, 8:16, :]
        row = jnp.floor(cell * (1.0 / 128.0))
        col = cell - 128.0 * row
        row = jnp.where(to == mine, row, -1.0)
        parts = [p.astype(F32) for p in split3(rec[s, 16:24, :])]
        for j in range(8):
            hot[s % 2, :, 128 * j : 128 * j + 128] = jnp.where(rows256 == row[j : j + 1], 1.0, 0.0).astype(BF16)
            same = rows128 == col[j : j + 1]
            for q in range(3):
                val_hot[s % 2, 128 * q : 128 * q + 128, 128 * j : 128 * j + 128] = jnp.where(same, parts[q][j : j + 1], 0.0).astype(BF16)
        got = lax.dot_general(hot[s % 2], val_hot[s % 2], (((1,), (1,)), ((), ())), preferred_element_type=F32)
        return got[:, 0:128] + got[:, 128:256] + got[:, 256:384]

    rhs[...] = deposit(0)
    for k in rec_order:
        arrive(rec.at[k], rec_sem(k))
        rhs[...] = rhs[...] + deposit(k)

    finish_0(K[0], 0, 2, False)

    arrive(mom_in, 1)
    inside = [
        jnp.where(me[i] == edge, 0.0, 1.0) for i in range(3) for edge in (shape[i] - 1, 0)
    ]
    masks_0 = edge_masks(L0)
    row16 = lax.broadcasted_iota(jnp.int32, (16, 128), 0)
    for x in range(16):
        xp = chi[x + 1] * ind[0, x + 1] if x < 15 else mom_in[1] * inside[0]
        xm = chi[x - 1] * ind[0, x - 1] if x > 0 else mom_in[0] * inside[1]
        my = chi[x] * ind[1, x]
        yp = jnp.where(row16 == 15, mom_in[3, x : x + 1, :] * inside[2], pltpu.roll(my, 15, 0))
        ym = jnp.where(row16 == 0, mom_in[2, x : x + 1, :] * inside[3], pltpu.roll(my, 1, 0))
        mz = chi[x] * ind[2, x]
        far = pltpu.roll(mom_in[5] * inside[4], 127 - x, 1)
        near = mom_in[4] * inside[5]
        near = pltpu.roll(near, 128 - x, 1) if x else near
        zp = jnp.where(lane16 == 127, far, pltpu.roll(mz, 127, 1))
        zm = jnp.where(lane16 == 0, near, pltpu.roll(mz, 1, 1))
        total = -0.5 * (xp - xm + (yp - ym) + (zp - zm)) + rhs[16 * x : 16 * x + 16, :]
        sums = face_sums(L0, x, masks_0(x))[1][0:16, 0:128]
        B[0][x, 0:16, 0:128] = total * (OMEGA / sums)
    make_0(B[0], 1)
    ship_0(1, 5)
    finish_0(K[0], 0, 2, True)
    coefficients(L0, 2)

    finish_1(K[1], 0, 3, False)
    finish_1(K[1], 0, 3, True)
    coefficients(L1, 3)
    finish_2z(K[2], 0, 4)
    restrict_2(lambda x: K[2][x, 0:8, :], 0)
    start_3y(0, 7)

    finish_0(B[0], 1, 5, False)
    sweep(L0, B[0], VA[0], 1)

    blocks = restrict_0(lambda x: residual(L0, VA[0], x)[0:16, 0:128])
    for p, block in enumerate(blocks):
        B[1][p, 0:8, :] = block * IW[1][p, 0:8, :]
    start_1(B[1], 1, 8)
    finish_0(B[0], 1, 5, True)
    sweep(L0, B[0], VA[0], 2)
    coefficients(L2, 3)
    finish_3y(0, 7)
    start_3x(0, 9)

    finish_1(B[1], 1, 8, False)
    sweep(L1, B[1], VA[1], 1)
    inv_2 = pick([pltpu.roll(IW[2][p, 0:4, :], 32 * p, 1) if p else IW[2][p, 0:4, :] for p in range(4)])
    pack_2[1] = restrict_1(lambda x: residual(L1, VA[1], x)[0:8, :]) * inv_2
    start_2z(1, 10)
    finish_1(B[1], 1, 8, True)
    sweep(L1, B[1], VA[1], 3)
    finish_3x(K[3], 0, 9)
    coefficients(L3, 8)

    finish_2z(B[2], 1, 10)
    sweep(L2, B[2], VA[2], 3)
    restrict_2(lambda x: residual(L2, VA[2], x)[0:8, :], 1)
    own_rows = pack_3[1]
    low = IW[3][0, 0:2, :]
    high = IW[3][1, 0:2, :]
    pack_3[1] = own_rows * jnp.where(lax.broadcasted_iota(jnp.int32, (2, 128), 1) < 64, low, high)
    start_3y(1, 12)
    for p in range(4):
        full_2[4 * p : 4 * p + 4, :] = VA[2][p, 0:4, :]
    start_2(13)

    finish_3y(1, 12)
    start_3x(1, 14)
    finish_2(VA[2], 13)
    finish_3x(B[3], 1, 14)
    now, other = B[3], VA[3]
    for halo in range(8, 1, -1):
        sweep(L3, now, other, halo)
        now, other = other, VB[3] if other is VA[3] else VA[3]

    up_2 = eye((128, 128), lambda r, c: as_mat(r == half(c)))
    prolong(L2, L3, 4, now, VA[2], tall_2, up_2, lambda r: wrap(half(jnp.where(r < 8, r, r - 16)), 24))
    sweep(L2, VA[2], VB[2], 3)
    sweep(L2, VB[2], VA[2], 2)
    up_1 = eye((128, 128), lambda r, c: as_mat(r == wrap(half(jnp.where(c < 96, c, c - 128)), 128)))
    prolong(L1, L2, 3, VA[2], VA[1], tall_3, up_1, lambda r: wrap(half(jnp.where(r < 12, r, r - 16)), 16))
    sweep(L1, VA[1], VB[1], 2)
    sweep(L1, VB[1], VA[1], 1)
    up_0 = eye((128, 256), lambda r, c: as_mat(r == wrap(half(jnp.where(c < 192, c, c - 256)), 128)))
    prolong(L0, L1, 2, VA[1], VA[0], tall_4, up_0, lambda r: wrap(half(jnp.where(r < 20, r, r - 24)), 16))
    sweep(L0, VA[0], VB[0], 1)

    for x in range(16):
        v, acc = gathered(L0, VB[0], x)
        out_ref[x] = ((1.0 - OMEGA) * v + acc)[0:16, 0:128]

    for k in rec_order:
        sent(rec.at[k], rec_sem(k))
    sent(mom_in, 1)
    for i, n in ((0, 2), (1, 5)):
        sent(land_0.at[i, 8:TILES_0], n)
        sent(land_0.at[i, 0:8], n + FAR)
    for i, n in ((0, 3), (1, 8)):
        sent(land_1.at[i, 8:TILES_1], n)
        sent(land_1.at[i, 0:8], n + FAR)
    for i, n in ((0, 4), (1, 10)):
        sent(land_2z.at[i], n)
    sent(land_2, 13)
    for i, n in ((0, 7), (1, 12)):
        sent(land_3y.at[i], n)
    for i, n in ((0, 9), (1, 14)):
        sent(land_3x.at[i], n)


def scratch(shape):
    out = []
    for lv in LEVELS:
        out += [pltpu.VMEM(lv.size, F32)] * 6 + [pltpu.VMEM((6,) + lv.size, F32)]
    nz = shape[2]
    out += [
        pltpu.VMEM((nz, 24, 128), F32), pltpu.VMEM((6, 16, 128), F32), pltpu.VMEM((6, 16, 128), F32),
        pltpu.VMEM((2, 256, 1024), BF16), pltpu.VMEM((2, 384, 1024), BF16), pltpu.VMEM((256, 128), F32),
        pltpu.VMEM((2, 32, 8, 128), F32), pltpu.VMEM((2, TILES_0, 8, 128), F32),
        pltpu.VMEM((2, 8, 8, 128), F32), pltpu.VMEM((2, TILES_1, 8, 128), F32),
        pltpu.VMEM((2, 4, 128), F32), pltpu.VMEM((2, 9 * nz - 1, 4, 128), F32),
        pltpu.VMEM((16, 128), F32), pltpu.VMEM((8, 16, 128), F32),
        pltpu.VMEM((2, 2, 128), F32), pltpu.VMEM((2, 2 * REACH, 2, 128), F32),
        pltpu.VMEM((2, 24, 128), F32), pltpu.VMEM((2, 2 * REACH, 24, 128), F32),
        pltpu.VMEM((128, 128), F32), pltpu.VMEM((32, 128), F32),
        pltpu.VMEM((144, 128), F32), pltpu.VMEM((128, 128), F32),
        pltpu.VMEM((160, 128), F32),
        pltpu.VMEM((16, 16, 128), F32), pltpu.VMEM((3, 16, 16, 128), F32),
        pltpu.VMEM((2, 8, 128), jnp.int32), pltpu.VMEM((8, 128), F32),
        pltpu.SemaphoreType.DMA((35,)), pltpu.SemaphoreType.DMA((35,)), pltpu.SemaphoreType.DMA((5,)),
    ]
    return out


def per_device(shape, chi, inducing, record_dest, record_cell, record_value):
    vmem = pl.BlockSpec(memory_space=pltpu.VMEM)
    keep = lambda a: pltpu.with_memory_space_constraint(a, pltpu.HBM)
    return pl.pallas_call(
        functools.partial(kernel, shape),
        out_shape=jax.ShapeDtypeStruct((16, 16, 128), F32),
        in_specs=[pl.BlockSpec(memory_space=pltpu.HBM)] * 5,
        out_specs=vmem,
        scratch_shapes=scratch(shape),
        compiler_params=pltpu.CompilerParams(
            collective_id=0, has_side_effects=True, vmem_limit_bytes=40 * 1024 * 1024
        ),
        name="cycle",
    )(*map(keep, (chi, inducing, record_dest.reshape(8, 128), record_cell.reshape(8, 128), record_value.reshape(8, 128))))


def solution(mesh):
    shape = tuple(mesh.shape[a] for a in ("gx", "gy", "gz"))
    placed = (
        P("gx", "gy", "gz"),
        P(None, "gx", "gy", "gz"),
        P("gx", "gy", "gz", None, None),
        P("gx", "gy", "gz", None),
        P("gx", "gy", "gz", None),
    )
    return jax.shard_map(
        functools.partial(per_device, shape), mesh=mesh, in_specs=placed, out_specs=P("gx", "gy", "gz"), check_vma=False
    )
```

```python
import functools
import itertools

import jax
import jax.numpy as jnp
from jax import lax
from jax.experimental import pallas as pl
from jax.experimental.pallas import tpu as pltpu
from jax.sharding import PartitionSpec as P

OMEGA = 0.8
F32 = jnp.float32
BF16 = jnp.bfloat16
MESH = pl.DeviceIdType.MESH
BOX = [d for d in itertools.product((-1, 0, 1), repeat=3) if d != (0, 0, 0)]
BOX.sort(key=lambda d: -sum(map(abs, d)))
BOX2 = [d for d in itertools.product((-1, 0, 1), repeat=2) if d != (0, 0)]
REACH = 5
FAR = 15


class Level:
    def __init__(self, index, own, size, split, total):
        self.index, self.own, self.size, self.split, self.total = index, own, size, split, total
        self.scale = 0.25**index


L0 = Level(0, (16, 16, 128), (22, 24, 256), (19, 20, 192), (256, 192, 512))
L1 = Level(1, (8, 8, 64), (16, 16, 128), (12, 12, 96), (128, 96, 256))
L2 = Level(2, (4, 4, 32), (12, 16, 128), (8, 8, 128), (64, 48, 128))
L3 = Level(3, (2, 2, 16), (22, 24, 128), (12, 24, 64), (32, 24, 64))
LEVELS = (L0, L1, L2, L3)


def tiles_0(d):
    if d[2] == 0:
        if d[1] == 0:
            return 6
        return 8 if d[0] == 0 else 2
    return 2 if d[1] == 0 else 1


def tiles_1(d):
    if d[2] == 0:
        return 4 if d[0] == 0 else 2
    return 2 if d[0] == 0 else 1


def slots(count_of):
    table, at = {}, 0
    for d in BOX:
        table[d] = (at, count_of(d))
        at += count_of(d)
    return table, at


SLOT_0, TILES_0 = slots(tiles_0)
SLOT_1, TILES_1 = slots(tiles_1)


def peers(shape):
    nx, ny, nz = shape
    out = [tuple(d) for d in BOX]
    out += [(x, y, k) for x in (-1, 0, 1) for y in (-1, 0, 1) for k in range(2, nz - 1)]
    out += [(0, k, 0) for k in range(-REACH, REACH + 1) if abs(k) > 1]
    out += [(k, 0, 0) for k in range(-REACH, REACH + 1) if abs(k) > 1]
    return out


def split3(x):
    hi = x.astype(BF16)
    rest = x - hi.astype(F32)
    mid = rest.astype(BF16)
    low = (rest - mid.astype(F32)).astype(BF16)
    return hi, mid, low


def right(x, mat):
    parts = [jnp.dot(p, mat, preferred_element_type=F32) for p in split3(x)]
    return parts[0] + parts[1] + parts[2]


def left(mat, x):
    parts = [jnp.dot(mat, p, preferred_element_type=F32) for p in split3(x)]
    return parts[0] + parts[1] + parts[2]


def wrap(at, size):
    return jnp.where(at < 0, at + size, jnp.where(at >= size, at - size, at))


def kernel(shape, chi_hbm, ind_hbm, dest_hbm, cell_hbm, val_hbm, out_ref, *refs):
    it = iter(refs)
    take = lambda n: [next(it) for _ in range(n)]
    K, B, VA, VB, IW, DW = [], [], [], [], [], []
    C = []
    for _ in LEVELS:
        k, b, va, vb, iw, dw, c = take(7)
        K.append(k), B.append(b), VA.append(va), VB.append(vb), IW.append(iw), DW.append(dw), C.append(c)
    rec, mom_out, mom_in, hot, val_hot, rhs = take(6)
    pack_0, land_0, pack_1, land_1 = take(4)
    pack_2, land_2z, full_2, land_2 = take(4)
    pack_3, land_3y, col_3, land_3x = take(4)
    tall_0, tall_1, tall_2, tall_3, tall_4 = take(5)
    chi, ind, rec_in, val_in = take(4)
    send_sem, recv_sem, load_sem = take(3)

    me = [lax.axis_index(a) for a in ("gx", "gy", "gz")]

    known = {}

    def along(i, o):
        if (i, o) not in known:
            known[i, o] = wrap(me[i] + o, shape[i]) if o else me[i]
        return known[i, o]

    def device(o):
        return tuple(along(i, o[i]) for i in range(3))

    copies = [
        pltpu.make_async_copy(src, dst, load_sem.at[j])
        for j, (src, dst) in enumerate([
            (chi_hbm, chi), (ind_hbm, ind), (dest_hbm, rec_in.at[0]), (cell_hbm, rec_in.at[1]), (val_hbm, val_in),
        ])
    ]
    for j in (2, 3, 4, 0, 1):
        copies[j].start()

    barrier = pltpu.get_barrier_semaphore()
    all_peers = peers(shape)
    for o in all_peers:
        pl.semaphore_signal(barrier, inc=1, device_id=device(o), device_id_type=MESH)

    sub = lax.broadcasted_iota(jnp.int32, (8, 128), 0)
    lane = lax.broadcasted_iota(jnp.int32, (8, 128), 1)
    lane24 = lax.broadcasted_iota(jnp.int32, (24, 128), 1)
    lane16 = lax.broadcasted_iota(jnp.int32, (16, 128), 1)

    def send(src, dst, o, n):
        pltpu.make_async_remote_copy(
            src_ref=src, dst_ref=dst, send_sem=send_sem.at[n], recv_sem=recv_sem.at[n],
            device_id=device(o), device_id_type=MESH,
        ).start()

    def arrive(ref, n):
        pltpu.make_async_copy(ref, ref, recv_sem.at[n]).wait()

    def sent(ref, n):
        pltpu.make_async_copy(ref, ref, send_sem.at[n]).wait()

    def make_0(src, i):
        pack = pack_0.at[i]
        for p in range(3):
            for t in range(2):
                pack[2 * p + t] = src[13 + p, 8 * t : 8 * t + 8, 0:128]
                pack[6 + 2 * p + t] = src[p, 8 * t : 8 * t + 8, 0:128]
        for k in range(8):
            pack[12 + k] = jnp.where(sub >= 4, src[2 * k, 8:16, 0:128], pltpu.roll(src[2 * k + 1, 8:16, 0:128], 4, 0))
            pack[20 + k] = jnp.where(sub < 4, src[2 * k, 0:8, 0:128], pltpu.roll(src[2 * k + 1, 0:8, 0:128], 4, 0))
        up = jnp.zeros((16, 128), F32)
        down = jnp.zeros((16, 128), F32)
        for x in range(16):
            p = src[x, 0:16, 0:128]
            here = (lane16 >= 4 * x) & (lane16 < 4 * x + 4)
            up = jnp.where(here, pltpu.roll(p, (4 * x + 4) % 128, 1), up)
            down = jnp.where(here, pltpu.roll(p, 4 * x, 1) if x else p, down)
        for t in range(2):
            pack[28 + t] = up[8 * t : 8 * t + 8]
            pack[30 + t] = down[8 * t : 8 * t + 8]

    def ship_0(i, n):
        pack, land = pack_0.at[i], land_0.at[i]
        for d in BOX:
            to = n + FAR if 0 not in d else n
            at, count = SLOT_0[d]
            if d[2] == 0:
                if d[1] == 0:
                    first = 0 if d[0] == 1 else 6
                else:
                    first = (12 if d[1] == 1 else 20) + (6 if d[0] == 1 else 0)
            else:
                first = (28 if d[2] == 1 else 30) + (1 if d[1] == 1 else 0)
            send(pack.at[pl.ds(first, count)], land.at[pl.ds(at, count)], d, to)

    def finish_0(dst, i, n, corners):
        land = land_0.at[i]
        if corners:
            arrive(land.at[0:8], n + FAR)
        else:
            arrive(land.at[8:TILES_0], n)
        for xp in range(22):
            sx, px = (0, xp) if xp < 16 else (1, xp - 16) if xp < 19 else (-1, xp - 6)
            at = lambda y, z: SLOT_0[(-sx, -y, -z)][0]
            base = 6 if sx == -1 else 0
            if sx and not corners:
                row = px - 13 if sx == -1 else px
                dst[xp, 0:8, 0:128] = land[at(0, 0) + 2 * row]
                dst[xp, 8:16, 0:128] = land[at(0, 0) + 2 * row + 1]
            if not corners:
                k = px // 2 - base
                above, below = land[at(1, 0) + k], land[at(-1, 0) + k]
                if px % 2:
                    above, below = pltpu.roll(above, 4, 0), pltpu.roll(below, 4, 0)
                dst[xp, 16:24, 0:128] = jnp.where(sub < 4, above, below)
            for t in range(3):
                if corners != (sx != 0 and t == 2):
                    continue
                if t < 2:
                    a, b = land[at(0, 1) + t], land[at(0, -1) + t]
                else:
                    a = jnp.where(sub < 4, land[at(1, 1)], land[at(-1, 1)])
                    b = jnp.where(sub < 4, land[at(1, -1)], land[at(-1, -1)])
                a = pltpu.roll(a, (128 - 4 * px) % 128, 1) if px else a
                b = pltpu.roll(b, 124 - 4 * px, 1)
                dst[xp, 8 * t : 8 * t + 8, 128:256] = jnp.where(lane < 64, a, b)

    def start_1(src, i, n):
        pack, land = pack_1.at[i], land_1.at[i]
        for k in range(4):
            pack[k] = jnp.where(lane < 64, src[2 * k, 0:8, :], pltpu.roll(src[2 * k + 1, 0:8, :], 64, 1))
        for t in range(2):
            up = jnp.zeros((8, 128), F32)
            down = jnp.zeros((8, 128), F32)
            for j in range(4):
                p = src[4 * t + j, 0:8, :]
                here = (lane >= 32 * j) & (lane < 32 * j + 32)
                up = jnp.where(here, pltpu.roll(p, (32 * j + 96) % 128, 1) if j != 1 else p, up)
                down = jnp.where(here, pltpu.roll(p, 32 * j, 1) if j else p, down)
            pack[4 + t] = up
            pack[6 + t] = down
        for d in BOX:
            to = n + FAR if 0 not in d else n
            at, count = SLOT_1[d]
            if d[2] == 0:
                first = 2 if d[0] == 1 else 0
            else:
                first = (4 if d[2] == 1 else 6) + (1 if d[0] == 1 else 0)
            send(pack.at[pl.ds(first, count)], land.at[pl.ds(at, count)], d, to)

    def finish_1(dst, i, n, corners):
        land = land_1.at[i]
        if corners:
            arrive(land.at[0:8], n + FAR)
        else:
            arrive(land.at[8:TILES_1], n)
        for xp in range(16):
            sx, px = (0, xp) if xp < 8 else (1, xp - 8) if xp < 12 else (-1, xp - 8)
            half = 1 if sx == -1 else 0
            if corners and sx == 0:
                continue

            def piece(y, z):
                at = SLOT_1[(-sx, -y, -z)][0]
                return land[at + px // 2 - 2 * half] if z == 0 else land[at + px // 4 - half]

            def both(z):
                return jnp.where(sub < 4, piece(1, z), piece(-1, z))

            sa, sb = (64 - 32 * (px % 4)) % 128, 96 - 32 * (px % 4)

            def ends(a, b):
                a = pltpu.roll(a, sa, 1) if sa else a
                b = pltpu.roll(b, sb, 1) if sb else b
                return jnp.where(lane < 96, a, b)

            def middle(m):
                return pltpu.roll(m, 64, 1) if px % 2 else m

            if corners:
                dst[xp, 8:16, :] = jnp.where(lane < 64, dst[xp, 8:16, :], ends(both(1), both(-1)))
                continue
            m = middle(piece(0, 0)) if sx else dst[xp, 0:8, :]
            dst[xp, 0:8, :] = jnp.where(lane < 64, m, ends(piece(0, 1), piece(0, -1)))
            m = middle(both(0))
            dst[xp, 8:16, :] = m if sx else jnp.where(lane < 64, m, ends(both(1), both(-1)))

    columns = [(x, y, z) for x in (-1, 0, 1) for y in (-1, 0, 1) for z in range(shape[2]) if (x, y, z) != (0, 0, 0)]
    columns.sort(key=lambda d: -(abs(d[0]) + abs(d[1]) + min(d[2], shape[2] - d[2])))

    def start_2z(i, n):
        for j, d in enumerate(columns):
            send(pack_2.at[i], land_2z.at[i, j], (d[0], d[1], -d[2]), n)

    lane4 = lax.broadcasted_iota(jnp.int32, (4, 128), 1)

    def pick(blocks):
        out = blocks[3]
        for g in (2, 1, 0):
            out = jnp.where(lane4 < 32 * (g + 1), blocks[g], out)
        return out

    def finish_2z(dst, i, n):
        arrive(land_2z.at[i], n)
        for sx in (-1, 0, 1):
            for sy in (-1, 0, 1):
                own = [
                    pack_2[i] if (sx, sy, z) == (0, 0, 0) else land_2z[i, columns.index((-sx, -sy, z))] for z in range(4)
                ]
                turned = []
                for k in range(4):
                    mixed = pick([own[(g + k) % 4] for g in range(4)])
                    turned.append(pltpu.roll(mixed, 32 * k, 1) if k else mixed)
                x0 = 0 if sx == 0 else 4 if sx == 1 else 8
                y0 = 0 if sy == 0 else 4 if sy == 1 else 12
                for p in range(4):
                    dst[x0 + p, y0 : y0 + 4, :] = pick([turned[(z - p) % 4] for z in range(4)])

    def start_2(n):
        for j, d in enumerate(BOX2):
            send(full_2, land_2.at[j], (d[0], d[1], 0), n)

    def finish_2(dst, n):
        arrive(land_2, n)
        for j, d in enumerate(BOX2):
            x0 = 0 if d[0] == 0 else 4 if d[0] == -1 else 8
            y0 = 0 if d[1] == 0 else 4 if d[1] == -1 else 12
            for p in range(4):
                dst[x0 + p, y0 : y0 + 4, :] = land_2[j, 4 * p : 4 * p + 4, :]

    steps = sorted([k for k in range(-REACH, REACH + 1) if k], key=lambda k: -abs(k))

    def start_3y(i, n):
        for j, k in enumerate(steps):
            send(pack_3.at[i], land_3y.at[i, j], (0, -k, 0), n)

    def finish_3y(i, n):
        arrive(land_3y.at[i], n)
        col_3[i, 2 * REACH + 2 : 24 - 2 * REACH, :] = jnp.zeros((22 - 4 * REACH, 128), F32)
        col_3[i, 0:2, :] = pack_3[i]
        for j, k in enumerate(steps):
            row = (2 * k) % 24
            col_3[i, row : row + 2, :] = land_3y[i, j]

    def start_3x(i, n):
        for j, k in enumerate(steps):
            send(col_3.at[i], land_3x.at[i, j], (-k, 0, 0), n)

    def finish_3x(dst, i, n):
        arrive(land_3x.at[i], n)
        for k in range(-REACH, REACH + 1):
            pair = col_3[i] if k == 0 else land_3x[i, steps.index(k)]
            other = pltpu.roll(pair, 64, 1)
            dst[(2 * k) % 22] = jnp.where(lane24 < 64, pair, other)
            dst[(2 * k + 1) % 22] = jnp.where(lane24 < 64, other, pair)

    def around(ref, x, size):
        nx = size[0]
        v = ref[x]
        return v, (
            ref[(x + 1) % nx], ref[(x - 1) % nx],
            pltpu.roll(v, size[1] - 1, 0), pltpu.roll(v, 1, 0),
            pltpu.roll(v, size[2] - 1, 1), pltpu.roll(v, 1, 1),
        )

    def planes(lv, halo):
        return [r % lv.size[0] for r in range(-halo, lv.own[0] + halo)]

    def edge_masks(lv):
        X, Y, Z = lv.size
        rows = lax.broadcasted_iota(jnp.int32, (Y, Z), 0)
        lanes = lax.broadcasted_iota(jnp.int32, (Y, Z), 1)
        y = wrap(me[1] * lv.own[1] + jnp.where(rows < lv.split[1], rows, rows - Y), lv.total[1])
        z = wrap(me[2] * lv.own[2] + jnp.where(lanes < lv.split[2], lanes, lanes - Z), lv.total[2])
        sides = [
            jnp.where(y == lv.total[1] - 1, 0.0, 1.0), jnp.where(y == 0, 0.0, 1.0),
            jnp.where(z == lv.total[2] - 1, 0.0, 1.0), jnp.where(z == 0, 0.0, 1.0),
        ]

        def at(x):
            rel = x if x < lv.split[0] else x - X
            g = wrap(me[0] * lv.own[0] + rel, lv.total[0])
            return [jnp.where(g == lv.total[0] - 1, 0.0, 1.0), jnp.where(g == 0, 0.0, 1.0)] + sides

        return at

    def face_sums(lv, x, masks):
        k, near = around(K[lv.index], x, lv.size)
        c = [0.5 * (k + m * o) for m, o in zip(masks, near)]
        total = c[0] + c[1] + c[2] + c[3] + c[4] + c[5]
        return c, jnp.where(total > 0.5, total, 1.0)

    def coefficients(lv, halo):
        i = lv.index
        at = edge_masks(lv)
        for x in planes(lv, halo):
            masks = at(x)
            c, total = face_sums(lv, x, masks)
            inv = OMEGA / total
            for j in range(6):
                C[i][j, x] = c[j] * masks[j] * inv
            if x < lv.own[0]:
                IW[i][x] = inv * (1.0 / lv.scale)
                DW[i][x] = total * (lv.scale / OMEGA)

    def gathered(lv, src, x):
        i = lv.index
        v, near = around(src, x, lv.size)
        acc = B[i][x]
        for j in range(6):
            acc = acc + C[i][j, x] * near[j]
        return v, acc

    def sweep(lv, src, dst, halo):
        for x in planes(lv, halo):
            v, acc = gathered(lv, src, x)
            dst[x] = (1.0 - OMEGA) * v + acc

    def residual(lv, src, x):
        v, acc = gathered(lv, src, x)
        return (acc - OMEGA * v) * DW[lv.index][x]

    def eye(shape2, fn):
        r = lax.broadcasted_iota(jnp.int32, shape2, 0)
        c = lax.broadcasted_iota(jnp.int32, shape2, 1)
        return fn(r, c)

    def as_mat(cond, value=1.0):
        return jnp.where(cond, value, 0.0).astype(BF16)

    half = lambda a: lax.shift_right_arithmetic(a, 1)
    down_lanes_0 = eye((128, 128), lambda r, c: as_mat(half(r) == c, 0.125))
    down_lanes_1 = eye((128, 128), lambda r, c: as_mat((half(r) == c) & (r < 64), 0.125))
    down_lanes_2 = [
        eye((128, 128), lambda r, c: as_mat(half(r) + 64 * p == c, 0.125)) for p in range(2)
    ]

    def restrict_0(plane):
        for p in range(8):
            tall_0[16 * p : 16 * p + 16, :] = plane(2 * p) + plane(2 * p + 1)
        rows = right(tall_0[pl.ds(0, 64, 2), :] + tall_0[pl.ds(1, 64, 2), :], down_lanes_0)
        return [rows[8 * p : 8 * p + 8] for p in range(8)]

    def restrict_1(plane):
        for p in range(4):
            tall_1[8 * p : 8 * p + 8, :] = plane(2 * p) + plane(2 * p + 1)
        part = right(tall_1[pl.ds(0, 16, 2), :] + tall_1[pl.ds(1, 16, 2), :], down_lanes_1)
        whole = part[0:4]
        for p in range(1, 4):
            whole = whole + pltpu.roll(part[4 * p : 4 * p + 4], 32 * p, 1)
        return whole

    def restrict_2(plane, i):
        both = right(plane(0) + plane(1), down_lanes_2[0]) + right(plane(2) + plane(3), down_lanes_2[1])
        for r in range(2):
            pack_3[i, r : r + 1, :] = both[2 * r : 2 * r + 1] + both[2 * r + 1 : 2 * r + 2]

    def prolong(fine, coarse, halo, e_ref, v_ref, tall, lanes_mat, rows_of):
        XF, YF, ZF = fine.size
        XC, YC, ZC = coarse.size
        rows_mat = eye((YF, YC), lambda r, c: as_mat(rows_of(r) == c))
        todo = {}
        for rel in range(-halo, fine.own[0] + halo):
            todo.setdefault((rel // 2) % XC, []).append(rel % XF)
        for q, p in enumerate(todo):
            tall[YC * q : YC * q + YC, :] = e_ref[p]
        spread = right(tall[...], lanes_mat)
        for q, p in enumerate(todo):
            out = left(rows_mat, spread[YC * q : YC * q + YC])
            for x in todo[p]:
                v_ref[x] = v_ref[x] + out

    for copy in copies[2:]:
        copy.wait()
    rec[0, 0:8, :] = rec_in[0].astype(F32)
    rec[0, 8:16, :] = rec_in[1].astype(F32)
    rec[0, 16:24, :] = val_in[...]
    pl.semaphore_wait(barrier, len(all_peers))

    rec_order = sorted(range(1, shape[2]), key=lambda k: min(k, shape[2] - k))
    rec_sem = lambda k: (0, 33, 34)[k - 1]
    for k in reversed(rec_order):
        send(rec.at[0], rec.at[k], (0, 0, -k), rec_sem(k))
    copies[0].wait()
    for x in range(16):
        K[0][x, 0:16, 0:128] = 1.0 + chi[x]
    make_0(K[0], 0)
    copies[1].wait()
    up = jnp.zeros((16, 128), F32)
    down = jnp.zeros((16, 128), F32)
    for x in range(16):
        mz = chi[x] * ind[2, x]
        up = jnp.where(lane16 == x, pltpu.roll(mz, (x + 1) % 128, 1), up)
        down = jnp.where(lane16 == x, pltpu.roll(mz, x, 1) if x else mz, down)
        my = chi[x] * ind[1, x]
        mom_out[2, x : x + 1, :] = my[15:16]
        mom_out[3, x : x + 1, :] = my[0:1]
    mom_out[0] = chi[15] * ind[0, 15]
    mom_out[1] = chi[0] * ind[0, 0]
    mom_out[4] = up
    mom_out[5] = down

    FACES = [(1, 0, 0), (-1, 0, 0), (0, 1, 0), (0, -1, 0), (0, 0, 1), (0, 0, -1)]
    for j, d in enumerate(FACES):
        send(mom_out.at[j], mom_in.at[j], d, 1)
    ship_0(0, 2)

    for ref in (K[2], B[2]):
        for x in range(12):
            ref[x, 8:16, :] = jnp.zeros((8, 128), F32)
    for p, block in enumerate(restrict_0(lambda x: K[0][x, 0:16, 0:128])):
        K[1][p, 0:8, :] = block
    start_1(K[1], 0, 3)
    pack_2[0] = restrict_1(lambda x: K[1][x, 0:8, :])
    start_2z(0, 4)

    rows256 = lax.broadcasted_iota(jnp.int32, (256, 128), 0).astype(F32)
    rows128 = lax.broadcasted_iota(jnp.int32, (128, 128), 0).astype(F32)
    mine = me[2].astype(F32)

    def deposit(s):
        to, cell = rec[s, 0:8, :], rec[s, 8:16, :]
        row = jnp.floor(cell * (1.0 / 128.0))
        col = cell - 128.0 * row
        row = jnp.where(to == mine, row, -1.0)
        parts = [p.astype(F32) for p in split3(rec[s, 16:24, :])]
        for j in range(8):
            hot[s % 2, :, 128 * j : 128 * j + 128] = jnp.where(rows256 == row[j : j + 1], 1.0, 0.0).astype(BF16)
            same = rows128 == col[j : j + 1]
            for q in range(3):
                val_hot[s % 2, 128 * q : 128 * q + 128, 128 * j : 128 * j + 128] = jnp.where(same, parts[q][j : j + 1], 0.0).astype(BF16)
        got = lax.dot_general(hot[s % 2], val_hot[s % 2], (((1,), (1,)), ((), ())), preferred_element_type=F32)
        return got[:, 0:128] + got[:, 128:256] + got[:, 256:384]

    row16 = lax.broadcasted_iota(jnp.int32, (16, 128), 0)
    for x in range(16):
        my = chi[x] * ind[1, x]
        mz = chi[x] * ind[2, x]
        inner = jnp.where(row16 == 15, 0.0, pltpu.roll(my, 15, 0)) - jnp.where(row16 == 0, 0.0, pltpu.roll(my, 1, 0))
        inner = inner + jnp.where(lane16 == 127, 0.0, pltpu.roll(mz, 127, 1)) - jnp.where(lane16 == 0, 0.0, pltpu.roll(mz, 1, 1))
        if x < 15:
            inner = inner + chi[x + 1] * ind[0, x + 1]
        if x > 0:
            inner = inner - chi[x - 1] * ind[0, x - 1]
        rhs[16 * x : 16 * x + 16, :] = -0.5 * inner
    rhs[...] = rhs[...] + deposit(0)
    for k in rec_order:
        arrive(rec.at[k], rec_sem(k))
        rhs[...] = rhs[...] + deposit(k)

    finish_0(K[0], 0, 2, False)

    arrive(mom_in, 1)
    inside = [
        jnp.where(me[i] == edge, 0.0, 1.0) for i in range(3) for edge in (shape[i] - 1, 0)
    ]
    masks_0 = edge_masks(L0)
    mom_in[0] = mom_in[0] * inside[1]
    mom_in[1] = mom_in[1] * inside[0]
    far_all = mom_in[5] * inside[4]
    near_all = mom_in[4] * inside[5]
    for x in range(16):
        edge = jnp.where(row16 == 15, mom_in[3, x : x + 1, :] * inside[2], 0.0)
        edge = edge - jnp.where(row16 == 0, mom_in[2, x : x + 1, :] * inside[3], 0.0)
        near = pltpu.roll(near_all, 128 - x, 1) if x else near_all
        edge = edge + jnp.where(lane16 == 127, pltpu.roll(far_all, 127 - x, 1), 0.0) - jnp.where(lane16 == 0, near, 0.0)
        if x == 15:
            edge = edge + mom_in[1]
        if x == 0:
            edge = edge - mom_in[0]
        total = rhs[16 * x : 16 * x + 16, :] - 0.5 * edge
        sums = face_sums(L0, x, masks_0(x))[1][0:16, 0:128]
        B[0][x, 0:16, 0:128] = total * (OMEGA / sums)
    make_0(B[0], 1)
    ship_0(1, 5)
    finish_0(K[0], 0, 2, True)
    coefficients(L0, 2)

    finish_1(K[1], 0, 3, False)
    finish_1(K[1], 0, 3, True)
    coefficients(L1, 3)
    finish_2z(K[2], 0, 4)
    restrict_2(lambda x: K[2][x, 0:8, :], 0)
    start_3y(0, 7)

    finish_0(B[0], 1, 5, False)
    sweep(L0, B[0], VA[0], 1)

    blocks = restrict_0(lambda x: residual(L0, VA[0], x)[0:16, 0:128])
    for p, block in enumerate(blocks):
        B[1][p, 0:8, :] = block * IW[1][p, 0:8, :]
    start_1(B[1], 1, 8)
    finish_0(B[0], 1, 5, True)
    sweep(L0, B[0], VA[0], 2)
    coefficients(L2, 3)
    finish_3y(0, 7)
    start_3x(0, 9)

    finish_1(B[1], 1, 8, False)
    sweep(L1, B[1], VA[1], 1)
    inv_2 = pick([pltpu.roll(IW[2][p, 0:4, :], 32 * p, 1) if p else IW[2][p, 0:4, :] for p in range(4)])
    pack_2[1] = restrict_1(lambda x: residual(L1, VA[1], x)[0:8, :]) * inv_2
    start_2z(1, 10)
    finish_1(B[1], 1, 8, True)
    sweep(L1, B[1], VA[1], 3)
    finish_3x(K[3], 0, 9)
    coefficients(L3, 8)

    finish_2z(B[2], 1, 10)
    sweep(L2, B[2], VA[2], 3)
    restrict_2(lambda x: residual(L2, VA[2], x)[0:8, :], 1)
    own_rows = pack_3[1]
    low = IW[3][0, 0:2, :]
    high = IW[3][1, 0:2, :]
    pack_3[1] = own_rows * jnp.where(lax.broadcasted_iota(jnp.int32, (2, 128), 1) < 64, low, high)
    start_3y(1, 12)
    for p in range(4):
        full_2[4 * p : 4 * p + 4, :] = VA[2][p, 0:4, :]
    start_2(13)

    finish_3y(1, 12)
    start_3x(1, 14)
    finish_2(VA[2], 13)
    finish_3x(B[3], 1, 14)
    now, other = B[3], VA[3]
    for halo in range(8, 1, -1):
        sweep(L3, now, other, halo)
        now, other = other, VB[3] if other is VA[3] else VA[3]

    up_2 = eye((128, 128), lambda r, c: as_mat(r == half(c)))
    prolong(L2, L3, 4, now, VA[2], tall_2, up_2, lambda r: wrap(half(jnp.where(r < 8, r, r - 16)), 24))
    sweep(L2, VA[2], VB[2], 3)
    sweep(L2, VB[2], VA[2], 2)
    up_1 = eye((128, 128), lambda r, c: as_mat(r == wrap(half(jnp.where(c < 96, c, c - 128)), 128)))
    prolong(L1, L2, 3, VA[2], VA[1], tall_3, up_1, lambda r: wrap(half(jnp.where(r < 12, r, r - 16)), 16))
    sweep(L1, VA[1], VB[1], 2)
    sweep(L1, VB[1], VA[1], 1)
    up_0 = eye((128, 256), lambda r, c: as_mat(r == wrap(half(jnp.where(c < 192, c, c - 256)), 128)))
    prolong(L0, L1, 2, VA[1], VA[0], tall_4, up_0, lambda r: wrap(half(jnp.where(r < 20, r, r - 24)), 16))
    sweep(L0, VA[0], VB[0], 1)

    for x in range(16):
        v, acc = gathered(L0, VB[0], x)
        out_ref[x] = ((1.0 - OMEGA) * v + acc)[0:16, 0:128]

    for k in rec_order:
        sent(rec.at[k], rec_sem(k))
    sent(mom_in, 1)
    for i, n in ((0, 2), (1, 5)):
        sent(land_0.at[i, 8:TILES_0], n)
        sent(land_0.at[i, 0:8], n + FAR)
    for i, n in ((0, 3), (1, 8)):
        sent(land_1.at[i, 8:TILES_1], n)
        sent(land_1.at[i, 0:8], n + FAR)
    for i, n in ((0, 4), (1, 10)):
        sent(land_2z.at[i], n)
    sent(land_2, 13)
    for i, n in ((0, 7), (1, 12)):
        sent(land_3y.at[i], n)
    for i, n in ((0, 9), (1, 14)):
        sent(land_3x.at[i], n)


def scratch(shape):
    out = []
    for lv in LEVELS:
        out += [pltpu.VMEM(lv.size, F32)] * 6 + [pltpu.VMEM((6,) + lv.size, F32)]
    nz = shape[2]
    out += [
        pltpu.VMEM((nz, 24, 128), F32), pltpu.VMEM((6, 16, 128), F32), pltpu.VMEM((6, 16, 128), F32),
        pltpu.VMEM((2, 256, 1024), BF16), pltpu.VMEM((2, 384, 1024), BF16), pltpu.VMEM((256, 128), F32),
        pltpu.VMEM((2, 32, 8, 128), F32), pltpu.VMEM((2, TILES_0, 8, 128), F32),
        pltpu.VMEM((2, 8, 8, 128), F32), pltpu.VMEM((2, TILES_1, 8, 128), F32),
        pltpu.VMEM((2, 4, 128), F32), pltpu.VMEM((2, 9 * nz - 1, 4, 128), F32),
        pltpu.VMEM((16, 128), F32), pltpu.VMEM((8, 16, 128), F32),
        pltpu.VMEM((2, 2, 128), F32), pltpu.VMEM((2, 2 * REACH, 2, 128), F32),
        pltpu.VMEM((2, 24, 128), F32), pltpu.VMEM((2, 2 * REACH, 24, 128), F32),
        pltpu.VMEM((128, 128), F32), pltpu.VMEM((32, 128), F32),
        pltpu.VMEM((144, 128), F32), pltpu.VMEM((128, 128), F32),
        pltpu.VMEM((160, 128), F32),
        pltpu.VMEM((16, 16, 128), F32), pltpu.VMEM((3, 16, 16, 128), F32),
        pltpu.VMEM((2, 8, 128), jnp.int32), pltpu.VMEM((8, 128), F32),
        pltpu.SemaphoreType.DMA((35,)), pltpu.SemaphoreType.DMA((35,)), pltpu.SemaphoreType.DMA((5,)),
    ]
    return out


def per_device(shape, chi, inducing, record_dest, record_cell, record_value):
    vmem = pl.BlockSpec(memory_space=pltpu.VMEM)
    keep = lambda a: pltpu.with_memory_space_constraint(a, pltpu.HBM)
    return pl.pallas_call(
        functools.partial(kernel, shape),
        out_shape=jax.ShapeDtypeStruct((16, 16, 128), F32),
        in_specs=[pl.BlockSpec(memory_space=pltpu.HBM)] * 5,
        out_specs=vmem,
        scratch_shapes=scratch(shape),
        compiler_params=pltpu.CompilerParams(
            collective_id=0, has_side_effects=True, vmem_limit_bytes=40 * 1024 * 1024
        ),
        name="cycle",
    )(*map(keep, (chi, inducing, record_dest.reshape(8, 128), record_cell.reshape(8, 128), record_value.reshape(8, 128))))


def solution(mesh):
    shape = tuple(mesh.shape[a] for a in ("gx", "gy", "gz"))
    placed = (
        P("gx", "gy", "gz"),
        P(None, "gx", "gy", "gz"),
        P("gx", "gy", "gz", None, None),
        P("gx", "gy", "gz", None),
        P("gx", "gy", "gz", None),
    )
    return jax.shard_map(
        functools.partial(per_device, shape), mesh=mesh, in_specs=placed, out_specs=P("gx", "gy", "gz"), check_vma=False
    )
```

```python
import functools
import itertools

import jax
import jax.numpy as jnp
from jax import lax
from jax.experimental import pallas as pl
from jax.experimental.pallas import tpu as pltpu
from jax.sharding import PartitionSpec as P

OMEGA = 0.8
F32 = jnp.float32
BF16 = jnp.bfloat16
MESH = pl.DeviceIdType.MESH
BOX = [d for d in itertools.product((-1, 0, 1), repeat=3) if d != (0, 0, 0)]
BOX.sort(key=lambda d: -sum(map(abs, d)))
BOX2 = [d for d in itertools.product((-1, 0, 1), repeat=2) if d != (0, 0)]
REACH = 5
FAR = 15


def apart(k):
    return max(0, 2 * abs(k) - 3)


DIAMOND = [
    (a, b)
    for a in range(-REACH, REACH + 1)
    for b in range(-REACH, REACH + 1)
    if (a, b) != (0, 0) and apart(a) + apart(b) <= apart(REACH)
]
DIAMOND.sort(key=lambda d: -(abs(d[1]) + abs(d[0]) / 2))


class Level:
    def __init__(self, index, own, size, split, total):
        self.index, self.own, self.size, self.split, self.total = index, own, size, split, total
        self.scale = 0.25**index


L0 = Level(0, (16, 16, 128), (22, 24, 256), (19, 20, 192), (256, 192, 512))
L1 = Level(1, (8, 8, 64), (16, 16, 128), (12, 12, 96), (128, 96, 256))
L2 = Level(2, (4, 4, 32), (12, 16, 128), (8, 8, 128), (64, 48, 128))
L3 = Level(3, (2, 2, 16), (22, 24, 128), (12, 24, 64), (32, 24, 64))
LEVELS = (L0, L1, L2, L3)


def tiles_0(d):
    if d[2] == 0:
        if d[1] == 0:
            return 6
        return 8 if d[0] == 0 else 2
    return 2 if d[1] == 0 else 1


def tiles_1(d):
    if d[2] == 0:
        return 4 if d[0] == 0 else 2
    return 2 if d[0] == 0 else 1


def slots(count_of):
    table, at = {}, 0
    for d in BOX:
        table[d] = (at, count_of(d))
        at += count_of(d)
    return table, at


SLOT_0, TILES_0 = slots(tiles_0)
SLOT_1, TILES_1 = slots(tiles_1)


def peers(shape):
    nx, ny, nz = shape
    out = [tuple(d) for d in BOX]
    out += [(x, y, k) for x in (-1, 0, 1) for y in (-1, 0, 1) for k in range(2, nz - 1)]
    out += [(a, b, 0) for a, b in reversed(DIAMOND) if max(abs(a), abs(b)) > 1]
    return out


def split3(x):
    hi = x.astype(BF16)
    rest = x - hi.astype(F32)
    mid = rest.astype(BF16)
    low = (rest - mid.astype(F32)).astype(BF16)
    return hi, mid, low


def right(x, mat):
    parts = [jnp.dot(p, mat, preferred_element_type=F32) for p in split3(x)]
    return parts[0] + parts[1] + parts[2]


def left(mat, x):
    parts = [jnp.dot(mat, p, preferred_element_type=F32) for p in split3(x)]
    return parts[0] + parts[1] + parts[2]


def wrap(at, size):
    return jnp.where(at < 0, at + size, jnp.where(at >= size, at - size, at))


def kernel(shape, chi_hbm, ind_hbm, dest_hbm, cell_hbm, val_hbm, out_ref, *refs):
    it = iter(refs)
    take = lambda n: [next(it) for _ in range(n)]
    K, B, VA, VB, IW, DW = [], [], [], [], [], []
    C = []
    for _ in LEVELS:
        k, b, va, vb, iw, dw, c = take(7)
        K.append(k), B.append(b), VA.append(va), VB.append(vb), IW.append(iw), DW.append(dw), C.append(c)
    rec, mom_out, mom_in, hot, val_hot, rhs = take(6)
    pack_0, land_0, pack_1, land_1 = take(4)
    pack_2, land_2z, full_2, land_2 = take(4)
    pack_3, land_3, col_3 = take(3)
    tall_0, tall_1, tall_2, tall_3, tall_4 = take(5)
    chi, ind, rec_in, val_in = take(4)
    send_sem, recv_sem, load_sem = take(3)

    me = [lax.axis_index(a) for a in ("gx", "gy", "gz")]

    known = {}

    def along(i, o):
        if (i, o) not in known:
            known[i, o] = wrap(me[i] + o, shape[i]) if o else me[i]
        return known[i, o]

    def device(o):
        return tuple(along(i, o[i]) for i in range(3))

    copies = [
        pltpu.make_async_copy(src, dst, load_sem.at[j])
        for j, (src, dst) in enumerate([
            (chi_hbm, chi), (ind_hbm, ind), (dest_hbm, rec_in.at[0]), (cell_hbm, rec_in.at[1]), (val_hbm, val_in),
        ])
    ]
    for j in (2, 3, 4, 0, 1):
        copies[j].start()

    barrier = pltpu.get_barrier_semaphore()
    all_peers = peers(shape)
    for o in all_peers:
        pl.semaphore_signal(barrier, inc=1, device_id=device(o), device_id_type=MESH)

    sub = lax.broadcasted_iota(jnp.int32, (8, 128), 0)
    lane = lax.broadcasted_iota(jnp.int32, (8, 128), 1)
    lane24 = lax.broadcasted_iota(jnp.int32, (24, 128), 1)
    lane16 = lax.broadcasted_iota(jnp.int32, (16, 128), 1)

    def send(src, dst, o, n):
        pltpu.make_async_remote_copy(
            src_ref=src, dst_ref=dst, send_sem=send_sem.at[n], recv_sem=recv_sem.at[n],
            device_id=device(o), device_id_type=MESH,
        ).start()

    def arrive(ref, n):
        pltpu.make_async_copy(ref, ref, recv_sem.at[n]).wait()

    def sent(ref, n):
        pltpu.make_async_copy(ref, ref, send_sem.at[n]).wait()

    def make_0(src, i):
        pack = pack_0.at[i]
        for p in range(3):
            for t in range(2):
                pack[2 * p + t] = src[13 + p, 8 * t : 8 * t + 8, 0:128]
                pack[6 + 2 * p + t] = src[p, 8 * t : 8 * t + 8, 0:128]
        for k in range(8):
            pack[12 + k] = jnp.where(sub >= 4, src[2 * k, 8:16, 0:128], pltpu.roll(src[2 * k + 1, 8:16, 0:128], 4, 0))
            pack[20 + k] = jnp.where(sub < 4, src[2 * k, 0:8, 0:128], pltpu.roll(src[2 * k + 1, 0:8, 0:128], 4, 0))
        up = jnp.zeros((16, 128), F32)
        down = jnp.zeros((16, 128), F32)
        for x in range(16):
            p = src[x, 0:16, 0:128]
            here = (lane16 >= 4 * x) & (lane16 < 4 * x + 4)
            up = jnp.where(here, pltpu.roll(p, (4 * x + 4) % 128, 1), up)
            down = jnp.where(here, pltpu.roll(p, 4 * x, 1) if x else p, down)
        for t in range(2):
            pack[28 + t] = up[8 * t : 8 * t + 8]
            pack[30 + t] = down[8 * t : 8 * t + 8]

    def ship_0(i, n):
        pack, land = pack_0.at[i], land_0.at[i]
        for d in BOX:
            to = n + FAR if 0 not in d else n
            at, count = SLOT_0[d]
            if d[2] == 0:
                if d[1] == 0:
                    first = 0 if d[0] == 1 else 6
                else:
                    first = (12 if d[1] == 1 else 20) + (6 if d[0] == 1 else 0)
            else:
                first = (28 if d[2] == 1 else 30) + (1 if d[1] == 1 else 0)
            send(pack.at[pl.ds(first, count)], land.at[pl.ds(at, count)], d, to)

    def finish_0(dst, i, n, corners):
        land = land_0.at[i]
        if corners:
            arrive(land.at[0:8], n + FAR)
        else:
            arrive(land.at[8:TILES_0], n)
        for xp in range(22):
            sx, px = (0, xp) if xp < 16 else (1, xp - 16) if xp < 19 else (-1, xp - 6)
            at = lambda y, z: SLOT_0[(-sx, -y, -z)][0]
            base = 6 if sx == -1 else 0
            if sx and not corners:
                row = px - 13 if sx == -1 else px
                dst[xp, 0:8, 0:128] = land[at(0, 0) + 2 * row]
                dst[xp, 8:16, 0:128] = land[at(0, 0) + 2 * row + 1]
            if not corners:
                k = px // 2 - base
                above, below = land[at(1, 0) + k], land[at(-1, 0) + k]
                if px % 2:
                    above, below = pltpu.roll(above, 4, 0), pltpu.roll(below, 4, 0)
                dst[xp, 16:24, 0:128] = jnp.where(sub < 4, above, below)
            for t in range(3):
                if corners != (sx != 0 and t == 2):
                    continue
                if t < 2:
                    a, b = land[at(0, 1) + t], land[at(0, -1) + t]
                else:
                    a = jnp.where(sub < 4, land[at(1, 1)], land[at(-1, 1)])
                    b = jnp.where(sub < 4, land[at(1, -1)], land[at(-1, -1)])
                a = pltpu.roll(a, (128 - 4 * px) % 128, 1) if px else a
                b = pltpu.roll(b, 124 - 4 * px, 1)
                dst[xp, 8 * t : 8 * t + 8, 128:256] = jnp.where(lane < 64, a, b)

    def start_1(src, i, n):
        pack, land = pack_1.at[i], land_1.at[i]
        for k in range(4):
            pack[k] = jnp.where(lane < 64, src[2 * k, 0:8, :], pltpu.roll(src[2 * k + 1, 0:8, :], 64, 1))
        for t in range(2):
            up = jnp.zeros((8, 128), F32)
            down = jnp.zeros((8, 128), F32)
            for j in range(4):
                p = src[4 * t + j, 0:8, :]
                here = (lane >= 32 * j) & (lane < 32 * j + 32)
                up = jnp.where(here, pltpu.roll(p, (32 * j + 96) % 128, 1) if j != 1 else p, up)
                down = jnp.where(here, pltpu.roll(p, 32 * j, 1) if j else p, down)
            pack[4 + t] = up
            pack[6 + t] = down
        for d in BOX:
            to = n + FAR if 0 not in d else n
            at, count = SLOT_1[d]
            if d[2] == 0:
                first = 2 if d[0] == 1 else 0
            else:
                first = (4 if d[2] == 1 else 6) + (1 if d[0] == 1 else 0)
            send(pack.at[pl.ds(first, count)], land.at[pl.ds(at, count)], d, to)

    def finish_1(dst, i, n, corners):
        land = land_1.at[i]
        if corners:
            arrive(land.at[0:8], n + FAR)
        else:
            arrive(land.at[8:TILES_1], n)
        for xp in range(16):
            sx, px = (0, xp) if xp < 8 else (1, xp - 8) if xp < 12 else (-1, xp - 8)
            half = 1 if sx == -1 else 0
            if corners and sx == 0:
                continue

            def piece(y, z):
                at = SLOT_1[(-sx, -y, -z)][0]
                return land[at + px // 2 - 2 * half] if z == 0 else land[at + px // 4 - half]

            def both(z):
                return jnp.where(sub < 4, piece(1, z), piece(-1, z))

            sa, sb = (64 - 32 * (px % 4)) % 128, 96 - 32 * (px % 4)

            def ends(a, b):
                a = pltpu.roll(a, sa, 1) if sa else a
                b = pltpu.roll(b, sb, 1) if sb else b
                return jnp.where(lane < 96, a, b)

            def middle(m):
                return pltpu.roll(m, 64, 1) if px % 2 else m

            if corners:
                dst[xp, 8:16, :] = jnp.where(lane < 64, dst[xp, 8:16, :], ends(both(1), both(-1)))
                continue
            m = middle(piece(0, 0)) if sx else dst[xp, 0:8, :]
            dst[xp, 0:8, :] = jnp.where(lane < 64, m, ends(piece(0, 1), piece(0, -1)))
            m = middle(both(0))
            dst[xp, 8:16, :] = m if sx else jnp.where(lane < 64, m, ends(both(1), both(-1)))

    columns = [(x, y, z) for x in (-1, 0, 1) for y in (-1, 0, 1) for z in range(shape[2]) if (x, y, z) != (0, 0, 0)]
    columns.sort(key=lambda d: -(abs(d[0]) + abs(d[1]) + min(d[2], shape[2] - d[2])))

    def start_2z(i, n):
        for j, d in enumerate(columns):
            send(pack_2.at[i], land_2z.at[i, j], (d[0], d[1], -d[2]), n)

    lane4 = lax.broadcasted_iota(jnp.int32, (4, 128), 1)

    def pick(blocks):
        out = blocks[3]
        for g in (2, 1, 0):
            out = jnp.where(lane4 < 32 * (g + 1), blocks[g], out)
        return out

    def finish_2z(dst, i, n):
        arrive(land_2z.at[i], n)
        for sx in (-1, 0, 1):
            for sy in (-1, 0, 1):
                own = [
                    pack_2[i] if (sx, sy, z) == (0, 0, 0) else land_2z[i, columns.index((-sx, -sy, z))] for z in range(4)
                ]
                turned = []
                for k in range(4):
                    mixed = pick([own[(g + k) % 4] for g in range(4)])
                    turned.append(pltpu.roll(mixed, 32 * k, 1) if k else mixed)
                x0 = 0 if sx == 0 else 4 if sx == 1 else 8
                y0 = 0 if sy == 0 else 4 if sy == 1 else 12
                for p in range(4):
                    dst[x0 + p, y0 : y0 + 4, :] = pick([turned[(z - p) % 4] for z in range(4)])

    def start_2(n):
        for j, d in enumerate(BOX2):
            send(full_2, land_2.at[j], (d[0], d[1], 0), n)

    def finish_2(dst, n):
        arrive(land_2, n)
        for j, d in enumerate(BOX2):
            x0 = 0 if d[0] == 0 else 4 if d[0] == -1 else 8
            y0 = 0 if d[1] == 0 else 4 if d[1] == -1 else 12
            for p in range(4):
                dst[x0 + p, y0 : y0 + 4, :] = land_2[j, 4 * p : 4 * p + 4, :]

    def start_3(i, n):
        for j, d in enumerate(DIAMOND):
            send(pack_3.at[i], land_3.at[i, j], (d[0], d[1], 0), n)

    def finish_3(dst, i, n):
        arrive(land_3.at[i], n)
        for a in range(-REACH, REACH + 1):
            for b in range(-REACH, REACH + 1):
                row = (2 * b) % 24
                if (a, b) == (0, 0):
                    col_3[i, REACH, 0:2, :] = pack_3[i]
                elif (-a, -b) in DIAMOND:
                    col_3[i, a + REACH, row : row + 2, :] = land_3[i, DIAMOND.index((-a, -b))]
        for k in range(-REACH, REACH + 1):
            pair = col_3[i, k + REACH]
            other = pltpu.roll(pair, 64, 1)
            dst[(2 * k) % 22] = jnp.where(lane24 < 64, pair, other)
            dst[(2 * k + 1) % 22] = jnp.where(lane24 < 64, other, pair)

    def around(ref, x, size):
        nx = size[0]
        v = ref[x]
        return v, (
            ref[(x + 1) % nx], ref[(x - 1) % nx],
            pltpu.roll(v, size[1] - 1, 0), pltpu.roll(v, 1, 0),
            pltpu.roll(v, size[2] - 1, 1), pltpu.roll(v, 1, 1),
        )

    def planes(lv, halo):
        return [r % lv.size[0] for r in range(-halo, lv.own[0] + halo)]

    def edge_masks(lv):
        X, Y, Z = lv.size
        rows = lax.broadcasted_iota(jnp.int32, (Y, Z), 0)
        lanes = lax.broadcasted_iota(jnp.int32, (Y, Z), 1)
        y = wrap(me[1] * lv.own[1] + jnp.where(rows < lv.split[1], rows, rows - Y), lv.total[1])
        z = wrap(me[2] * lv.own[2] + jnp.where(lanes < lv.split[2], lanes, lanes - Z), lv.total[2])
        sides = [
            jnp.where(y == lv.total[1] - 1, 0.0, 1.0), jnp.where(y == 0, 0.0, 1.0),
            jnp.where(z == lv.total[2] - 1, 0.0, 1.0), jnp.where(z == 0, 0.0, 1.0),
        ]

        def at(x):
            rel = x if x < lv.split[0] else x - X
            g = wrap(me[0] * lv.own[0] + rel, lv.total[0])
            return [jnp.where(g == lv.total[0] - 1, 0.0, 1.0), jnp.where(g == 0, 0.0, 1.0)] + sides

        return at

    def face_sums(lv, x, masks):
        k, near = around(K[lv.index], x, lv.size)
        c = [0.5 * (k + m * o) for m, o in zip(masks, near)]
        total = c[0] + c[1] + c[2] + c[3] + c[4] + c[5]
        return c, jnp.where(total > 0.5, total, 1.0)

    def coefficients(lv, halo):
        i = lv.index
        at = edge_masks(lv)
        for x in planes(lv, halo):
            masks = at(x)
            c, total = face_sums(lv, x, masks)
            inv = OMEGA / total
            for j in range(6):
                C[i][j, x] = c[j] * masks[j] * inv
            if x < lv.own[0]:
                IW[i][x] = inv * (1.0 / lv.scale)
                DW[i][x] = total * (lv.scale / OMEGA)

    def gathered(lv, src, x):
        i = lv.index
        v, near = around(src, x, lv.size)
        acc = B[i][x]
        for j in range(6):
            acc = acc + C[i][j, x] * near[j]
        return v, acc

    def sweep(lv, src, dst, halo):
        for x in planes(lv, halo):
            v, acc = gathered(lv, src, x)
            dst[x] = (1.0 - OMEGA) * v + acc

    def residual(lv, src, x):
        v, acc = gathered(lv, src, x)
        return (acc - OMEGA * v) * DW[lv.index][x]

    def eye(shape2, fn):
        r = lax.broadcasted_iota(jnp.int32, shape2, 0)
        c = lax.broadcasted_iota(jnp.int32, shape2, 1)
        return fn(r, c)

    def as_mat(cond, value=1.0):
        return jnp.where(cond, value, 0.0).astype(BF16)

    half = lambda a: lax.shift_right_arithmetic(a, 1)
    down_lanes_0 = eye((128, 128), lambda r, c: as_mat(half(r) == c, 0.125))
    down_lanes_1 = eye((128, 128), lambda r, c: as_mat((half(r) == c) & (r < 64), 0.125))
    down_lanes_2 = [
        eye((128, 128), lambda r, c: as_mat(half(r) + 64 * p == c, 0.125)) for p in range(2)
    ]

    def restrict_0(plane):
        for p in range(8):
            tall_0[16 * p : 16 * p + 16, :] = plane(2 * p) + plane(2 * p + 1)
        rows = right(tall_0[pl.ds(0, 64, 2), :] + tall_0[pl.ds(1, 64, 2), :], down_lanes_0)
        return [rows[8 * p : 8 * p + 8] for p in range(8)]

    def restrict_1(plane):
        for p in range(4):
            tall_1[8 * p : 8 * p + 8, :] = plane(2 * p) + plane(2 * p + 1)
        part = right(tall_1[pl.ds(0, 16, 2), :] + tall_1[pl.ds(1, 16, 2), :], down_lanes_1)
        whole = part[0:4]
        for p in range(1, 4):
            whole = whole + pltpu.roll(part[4 * p : 4 * p + 4], 32 * p, 1)
        return whole

    def restrict_2(plane, i):
        both = right(plane(0) + plane(1), down_lanes_2[0]) + right(plane(2) + plane(3), down_lanes_2[1])
        for r in range(2):
            pack_3[i, r : r + 1, :] = both[2 * r : 2 * r + 1] + both[2 * r + 1 : 2 * r + 2]

    def prolong(fine, coarse, halo, e_ref, v_ref, tall, lanes_mat, rows_of):
        XF, YF, ZF = fine.size
        XC, YC, ZC = coarse.size
        rows_mat = eye((YF, YC), lambda r, c: as_mat(rows_of(r) == c))
        todo = {}
        for rel in range(-halo, fine.own[0] + halo):
            todo.setdefault((rel // 2) % XC, []).append(rel % XF)
        for q, p in enumerate(todo):
            tall[YC * q : YC * q + YC, :] = e_ref[p]
        spread = right(tall[...], lanes_mat)
        for q, p in enumerate(todo):
            out = left(rows_mat, spread[YC * q : YC * q + YC])
            for x in todo[p]:
                v_ref[x] = v_ref[x] + out

    for copy in copies[2:]:
        copy.wait()
    rec[0, 0:8, :] = rec_in[0].astype(F32)
    rec[0, 8:16, :] = rec_in[1].astype(F32)
    rec[0, 16:24, :] = val_in[...]
    pl.semaphore_wait(barrier, len(all_peers))

    rec_order = sorted(range(1, shape[2]), key=lambda k: min(k, shape[2] - k))
    rec_sem = lambda k: (0, 33, 34)[k - 1]
    for k in reversed(rec_order):
        send(rec.at[0], rec.at[k], (0, 0, -k), rec_sem(k))
    copies[0].wait()
    for x in range(16):
        K[0][x, 0:16, 0:128] = 1.0 + chi[x]
    make_0(K[0], 0)
    copies[1].wait()
    up = jnp.zeros((16, 128), F32)
    down = jnp.zeros((16, 128), F32)
    for x in range(16):
        mz = chi[x] * ind[2, x]
        up = jnp.where(lane16 == x, pltpu.roll(mz, (x + 1) % 128, 1), up)
        down = jnp.where(lane16 == x, pltpu.roll(mz, x, 1) if x else mz, down)
        my = chi[x] * ind[1, x]
        mom_out[2, x : x + 1, :] = my[15:16]
        mom_out[3, x : x + 1, :] = my[0:1]
    mom_out[0] = chi[15] * ind[0, 15]
    mom_out[1] = chi[0] * ind[0, 0]
    mom_out[4] = up
    mom_out[5] = down

    FACES = [(1, 0, 0), (-1, 0, 0), (0, 1, 0), (0, -1, 0), (0, 0, 1), (0, 0, -1)]
    for j, d in enumerate(FACES):
        send(mom_out.at[j], mom_in.at[j], d, 1)
    ship_0(0, 2)

    for k in range(2 * REACH + 1):
        for i in range(2):
            col_3[i, k] = jnp.zeros((24, 128), F32)
    for ref in (K[2], B[2]):
        for x in range(12):
            ref[x, 8:16, :] = jnp.zeros((8, 128), F32)
    for p, block in enumerate(restrict_0(lambda x: K[0][x, 0:16, 0:128])):
        K[1][p, 0:8, :] = block
    start_1(K[1], 0, 3)
    pack_2[0] = restrict_1(lambda x: K[1][x, 0:8, :])
    start_2z(0, 4)

    rows256 = lax.broadcasted_iota(jnp.int32, (256, 128), 0).astype(F32)
    rows128 = lax.broadcasted_iota(jnp.int32, (128, 128), 0).astype(F32)
    mine = me[2].astype(F32)

    def deposit(s):
        to, cell = rec[s, 0:8, :], rec[s, 8:16, :]
        row = jnp.floor(cell * (1.0 / 128.0))
        col = cell - 128.0 * row
        row = jnp.where(to == mine, row, -1.0)
        parts = [p.astype(F32) for p in split3(rec[s, 16:24, :])]
        for j in range(8):
            hot[s % 2, :, 128 * j : 128 * j + 128] = jnp.where(rows256 == row[j : j + 1], 1.0, 0.0).astype(BF16)
            same = rows128 == col[j : j + 1]
            for q in range(3):
                val_hot[s % 2, 128 * q : 128 * q + 128, 128 * j : 128 * j + 128] = jnp.where(same, parts[q][j : j + 1], 0.0).astype(BF16)
        got = lax.dot_general(hot[s % 2], val_hot[s % 2], (((1,), (1,)), ((), ())), preferred_element_type=F32)
        return got[:, 0:128] + got[:, 128:256] + got[:, 256:384]

    row16 = lax.broadcasted_iota(jnp.int32, (16, 128), 0)
    for x in range(16):
        my = chi[x] * ind[1, x]
        mz = chi[x] * ind[2, x]
        inner = jnp.where(row16 == 15, 0.0, pltpu.roll(my, 15, 0)) - jnp.where(row16 == 0, 0.0, pltpu.roll(my, 1, 0))
        inner = inner + jnp.where(lane16 == 127, 0.0, pltpu.roll(mz, 127, 1)) - jnp.where(lane16 == 0, 0.0, pltpu.roll(mz, 1, 1))
        if x < 15:
            inner = inner + chi[x + 1] * ind[0, x + 1]
        if x > 0:
            inner = inner - chi[x - 1] * ind[0, x - 1]
        rhs[16 * x : 16 * x + 16, :] = -0.5 * inner
    rhs[...] = rhs[...] + deposit(0)
    for k in rec_order:
        arrive(rec.at[k], rec_sem(k))
        rhs[...] = rhs[...] + deposit(k)

    finish_0(K[0], 0, 2, False)

    arrive(mom_in, 1)
    inside = [
        jnp.where(me[i] == edge, 0.0, 1.0) for i in range(3) for edge in (shape[i] - 1, 0)
    ]
    masks_0 = edge_masks(L0)
    mom_in[0] = mom_in[0] * inside[1]
    mom_in[1] = mom_in[1] * inside[0]
    far_all = mom_in[5] * inside[4]
    near_all = mom_in[4] * inside[5]
    for x in range(16):
        edge = jnp.where(row16 == 15, mom_in[3, x : x + 1, :] * inside[2], 0.0)
        edge = edge - jnp.where(row16 == 0, mom_in[2, x : x + 1, :] * inside[3], 0.0)
        near = pltpu.roll(near_all, 128 - x, 1) if x else near_all
        edge = edge + jnp.where(lane16 == 127, pltpu.roll(far_all, 127 - x, 1), 0.0) - jnp.where(lane16 == 0, near, 0.0)
        if x == 15:
            edge = edge + mom_in[1]
        if x == 0:
            edge = edge - mom_in[0]
        total = rhs[16 * x : 16 * x + 16, :] - 0.5 * edge
        sums = face_sums(L0, x, masks_0(x))[1][0:16, 0:128]
        B[0][x, 0:16, 0:128] = total * (OMEGA / sums)
    make_0(B[0], 1)
    ship_0(1, 5)
    finish_0(K[0], 0, 2, True)
    coefficients(L0, 2)

    finish_1(K[1], 0, 3, False)
    finish_1(K[1], 0, 3, True)
    coefficients(L1, 3)
    finish_2z(K[2], 0, 4)
    restrict_2(lambda x: K[2][x, 0:8, :], 0)

    finish_0(B[0], 1, 5, False)
    sweep(L0, B[0], VA[0], 1)

    blocks = restrict_0(lambda x: residual(L0, VA[0], x)[0:16, 0:128])
    for p, block in enumerate(blocks):
        B[1][p, 0:8, :] = block * IW[1][p, 0:8, :]
    start_1(B[1], 1, 8)
    start_3(0, 7)
    finish_0(B[0], 1, 5, True)
    sweep(L0, B[0], VA[0], 2)
    coefficients(L2, 3)

    finish_1(B[1], 1, 8, False)
    sweep(L1, B[1], VA[1], 1)
    inv_2 = pick([pltpu.roll(IW[2][p, 0:4, :], 32 * p, 1) if p else IW[2][p, 0:4, :] for p in range(4)])
    pack_2[1] = restrict_1(lambda x: residual(L1, VA[1], x)[0:8, :]) * inv_2
    start_2z(1, 10)
    finish_1(B[1], 1, 8, True)
    sweep(L1, B[1], VA[1], 3)
    finish_3(K[3], 0, 7)
    coefficients(L3, 8)

    finish_2z(B[2], 1, 10)
    sweep(L2, B[2], VA[2], 3)
    restrict_2(lambda x: residual(L2, VA[2], x)[0:8, :], 1)
    own_rows = pack_3[1]
    low = IW[3][0, 0:2, :]
    high = IW[3][1, 0:2, :]
    pack_3[1] = own_rows * jnp.where(lax.broadcasted_iota(jnp.int32, (2, 128), 1) < 64, low, high)
    start_3(1, 12)
    for p in range(4):
        full_2[4 * p : 4 * p + 4, :] = VA[2][p, 0:4, :]
    start_2(13)

    finish_2(VA[2], 13)
    finish_3(B[3], 1, 12)
    now, other = B[3], VA[3]
    for halo in range(8, 1, -1):
        sweep(L3, now, other, halo)
        now, other = other, VB[3] if other is VA[3] else VA[3]

    up_2 = eye((128, 128), lambda r, c: as_mat(r == half(c)))
    prolong(L2, L3, 4, now, VA[2], tall_2, up_2, lambda r: wrap(half(jnp.where(r < 8, r, r - 16)), 24))
    sweep(L2, VA[2], VB[2], 3)
    sweep(L2, VB[2], VA[2], 2)
    up_1 = eye((128, 128), lambda r, c: as_mat(r == wrap(half(jnp.where(c < 96, c, c - 128)), 128)))
    prolong(L1, L2, 3, VA[2], VA[1], tall_3, up_1, lambda r: wrap(half(jnp.where(r < 12, r, r - 16)), 16))
    sweep(L1, VA[1], VB[1], 2)
    sweep(L1, VB[1], VA[1], 1)
    up_0 = eye((128, 256), lambda r, c: as_mat(r == wrap(half(jnp.where(c < 192, c, c - 256)), 128)))
    prolong(L0, L1, 2, VA[1], VA[0], tall_4, up_0, lambda r: wrap(half(jnp.where(r < 20, r, r - 24)), 16))
    sweep(L0, VA[0], VB[0], 1)

    for x in range(16):
        v, acc = gathered(L0, VB[0], x)
        out_ref[x] = ((1.0 - OMEGA) * v + acc)[0:16, 0:128]

    for k in rec_order:
        sent(rec.at[k], rec_sem(k))
    sent(mom_in, 1)
    for i, n in ((0, 2), (1, 5)):
        sent(land_0.at[i, 8:TILES_0], n)
        sent(land_0.at[i, 0:8], n + FAR)
    for i, n in ((0, 3), (1, 8)):
        sent(land_1.at[i, 8:TILES_1], n)
        sent(land_1.at[i, 0:8], n + FAR)
    for i, n in ((0, 4), (1, 10)):
        sent(land_2z.at[i], n)
    sent(land_2, 13)
    for i, n in ((0, 7), (1, 12)):
        sent(land_3.at[i], n)


def scratch(shape):
    out = []
    for lv in LEVELS:
        out += [pltpu.VMEM(lv.size, F32)] * 6 + [pltpu.VMEM((6,) + lv.size, F32)]
    nz = shape[2]
    out += [
        pltpu.VMEM((nz, 24, 128), F32), pltpu.VMEM((6, 16, 128), F32), pltpu.VMEM((6, 16, 128), F32),
        pltpu.VMEM((2, 256, 1024), BF16), pltpu.VMEM((2, 384, 1024), BF16), pltpu.VMEM((256, 128), F32),
        pltpu.VMEM((2, 32, 8, 128), F32), pltpu.VMEM((2, TILES_0, 8, 128), F32),
        pltpu.VMEM((2, 8, 8, 128), F32), pltpu.VMEM((2, TILES_1, 8, 128), F32),
        pltpu.VMEM((2, 4, 128), F32), pltpu.VMEM((2, 9 * nz - 1, 4, 128), F32),
        pltpu.VMEM((16, 128), F32), pltpu.VMEM((8, 16, 128), F32),
        pltpu.VMEM((2, 2, 128), F32), pltpu.VMEM((2, len(DIAMOND), 2, 128), F32),
        pltpu.VMEM((2, 2 * REACH + 1, 24, 128), F32),
        pltpu.VMEM((128, 128), F32), pltpu.VMEM((32, 128), F32),
        pltpu.VMEM((144, 128), F32), pltpu.VMEM((128, 128), F32),
        pltpu.VMEM((160, 128), F32),
        pltpu.VMEM((16, 16, 128), F32), pltpu.VMEM((3, 16, 16, 128), F32),
        pltpu.VMEM((2, 8, 128), jnp.int32), pltpu.VMEM((8, 128), F32),
        pltpu.SemaphoreType.DMA((35,)), pltpu.SemaphoreType.DMA((35,)), pltpu.SemaphoreType.DMA((5,)),
    ]
    return out


def per_device(shape, chi, inducing, record_dest, record_cell, record_value):
    vmem = pl.BlockSpec(memory_space=pltpu.VMEM)
    keep = lambda a: pltpu.with_memory_space_constraint(a, pltpu.HBM)
    return pl.pallas_call(
        functools.partial(kernel, shape),
        out_shape=jax.ShapeDtypeStruct((16, 16, 128), F32),
        in_specs=[pl.BlockSpec(memory_space=pltpu.HBM)] * 5,
        out_specs=vmem,
        scratch_shapes=scratch(shape),
        compiler_params=pltpu.CompilerParams(
            collective_id=0, has_side_effects=True, vmem_limit_bytes=40 * 1024 * 1024
        ),
        name="cycle",
    )(*map(keep, (chi, inducing, record_dest.reshape(8, 128), record_cell.reshape(8, 128), record_value.reshape(8, 128))))


def solution(mesh):
    shape = tuple(mesh.shape[a] for a in ("gx", "gy", "gz"))
    placed = (
        P("gx", "gy", "gz"),
        P(None, "gx", "gy", "gz"),
        P("gx", "gy", "gz", None, None),
        P("gx", "gy", "gz", None),
        P("gx", "gy", "gz", None),
    )
    return jax.shard_map(
        functools.partial(per_device, shape), mesh=mesh, in_specs=placed, out_specs=P("gx", "gy", "gz"), check_vma=False
    )
```
